32 devices in a mesh: dp: 8 (over z, x), tensor: 4 (over y, core).
Axes of the slice: x: 2, y: 2, z: 4, core: 2. Of those that a mesh axis runs over, the one named last changes fastest.
Arguments:
- prompt: bfloat16 [16, 512, 1024], P('dp'), may hold values from -6 to 6
- cont: bfloat16 [16, 256, 1024], P('dp'), may hold values from -6 to 6
- memory: bfloat16 [16, 512, 1024], P('dp'), may hold values from -6 to 6
- old_memory: bfloat16 [16, 768, 1024], P('dp'), may hold values from -6 to 6
- branch_at: int32 [16, 2], P('dp'), may hold values from 128 to 512, as said below
- gain_attn: float32 [1024], replicated, may hold values from 0.1 to 1.9
- w_query: bfloat16 [1024, 1024], P(None, 'tensor'), may hold values from -0.1875 to 0.1875
- w_key: bfloat16 [1024, 1024], P(None, 'tensor'), may hold values from -0.1875 to 0.1875
- w_value: bfloat16 [1024, 1024], P(None, 'tensor'), may hold values from -0.1875 to 0.1875
- w_out: bfloat16 [1024, 1024], P('tensor'), may hold values from -4 to 4
- gain_ffn: float32 [1024], replicated, may hold values from 0.1 to 1.9
- w_up: bfloat16 [1024, 4096], P(None, 'tensor'), may hold values from -0.1875 to 0.1875
- w_down: bfloat16 [4096, 1024], P('tensor'), may hold values from -0.125 to 0.125
- w_conv: bfloat16 [3, 1024, 1024], P(None, None, 'tensor'), may hold values from -0.109375 to 0.109375
- cot_prompt: bfloat16 [16, 512, 1024], P('dp'), may hold values from -6 to 6
- cot_cont: bfloat16 [16, 256, 1024], P('dp'), may hold values from -6 to 6
Outputs:
- out_prompt: bfloat16 [16, 512, 1024], P('dp')
- out_cont: bfloat16 [16, 256, 1024], P('dp')
- grad_prompt: bfloat16 [16, 512, 1024], P('dp')
- grad_cont: bfloat16 [16, 256, 1024], P('dp')
- grad_query: float32 [1024, 1024], P('dp', 'tensor')
- grad_key: float32 [1024, 1024], P('dp', 'tensor')
- grad_value: float32 [1024, 1024], P('dp', 'tensor')
- grad_out: float32 [1024, 1024], P('tensor', 'dp')
- grad_up: float32 [1024, 4096], P('dp', 'tensor')
- grad_down: float32 [4096, 1024], P('tensor', 'dp')
- grad_conv: float32 [3, 1024, 1024], P(None, 'dp', 'tensor')
- grad_gain_attn: float32 [1024], P('dp')
- grad_gain_ffn: float32 [1024], P('dp')
The draws below stay inside these ranges and needn't reach their ends.
Inputs may be any that keep to these rules, and one draw needn't show every extreme that they name: `branch_at`: every group has a continuation that follows the whole prompt of 512 tokens.
All inputs are finite; a program needn't handle non-finite values.
Results may differ from the reference program's by a relative error of at most 0.024.
Values may be sent and summed in bfloat16 or wider, within the bound.
No kernel may reach another device: no remote copies, remote signals or barrier semaphores. Data moves between devices by JAX's collectives and lax.ppermute only.
A program may use at most 128 MiB of HBM per device.

```python
import jax
import jax.numpy as jnp
from jax import lax

D = 1024
HEADS = 8
HEAD_DIM = 128
FF = 4096
MEM = 512
RATE = 3
CM = 256
PROMPT = 512
CONT = 2
CLEN = 128
GROUPS = 16
N_TENSOR = 4


def draw_branch_at(key, part):
    first_key, second_key = jax.random.split(jax.random.fold_in(key, 17))
    drawn = jax.random.randint(first_key, (GROUPS, CONT), PROMPT // 4, PROMPT + 1)
    chosen = jax.random.randint(second_key, (GROUPS, 1), 0, CONT)
    column = lax.broadcasted_iota(jnp.int32, (GROUPS, CONT), 1)
    return jnp.where(column == chosen, PROMPT, drawn).astype(jnp.int32)


def shard_levels(rng, dims, cuts, least, top_value):
    level = 1.0
    for dim, blocks in cuts:
        heights = jax.random.uniform(jax.random.fold_in(jax.random.fold_in(rng, 6), dim), (blocks,), jnp.float32, least / len(cuts), top_value / len(cuts))
        level = level * jnp.repeat(jnp.exp(heights), dims[dim] // blocks).reshape((-1,) + (1,) * (len(dims) - 1 - dim))
    return level


def bell_draw(own_key, extent, deviation, reach, cuts=(), held_as=jnp.bfloat16):
    result = deviation * jax.random.normal(own_key, extent, jnp.float32)
    if cuts:
        result = result * shard_levels(own_key, extent, cuts, -0.22, 0.18)
    return jnp.clip(result, -reach, reach).astype(held_as)


def setup_inputs(seed: int = 0) -> dict:
    streams_of = jax.random.split(jax.random.key(seed), 17)
    return {
        "prompt": bell_draw(streams_of[0], (GROUPS, PROMPT, D), 1.0, 6.0, ((0, 8),)),
        "cont": bell_draw(streams_of[1], (GROUPS, CONT * CLEN, D), 1.0, 6.0, ((0, 8),)),
        "memory": bell_draw(streams_of[2], (GROUPS, MEM, D), 1.0, 6.0, ((0, 8),)),
        "old_memory": bell_draw(streams_of[3], (GROUPS, RATE * CM, D), 1.0, 6.0, ((0, 8),)),
        "branch_at": draw_branch_at(jax.random.fold_in(streams_of[16], 71), 0),
        "gain_attn": jnp.clip(1.0 + 0.18 * jax.random.normal(streams_of[5], (D,), jnp.float32), 0.1, 1.9),
        "w_query": bell_draw(streams_of[6], (D, HEADS * HEAD_DIM), D ** -0.5, 0.1875, ((1, 4),)),
        "w_key": bell_draw(streams_of[7], (D, HEADS * HEAD_DIM), D ** -0.5, 0.1875, ((1, 4),)),
        "w_value": bell_draw(streams_of[8], (D, HEADS * HEAD_DIM), D ** -0.5, 0.1875, ((1, 4),)),
        "w_out": bell_draw(streams_of[9], (HEADS * HEAD_DIM, D), 2 ** -0.5, 4.0, ((0, 4),)),
        "gain_ffn": jnp.clip(1.0 + 0.18 * jax.random.normal(streams_of[10], (D,), jnp.float32), 0.1, 1.9),
        "w_up": bell_draw(streams_of[11], (D, FF), D ** -0.5, 0.1875, ((1, 4),)),
        "w_down": bell_draw(streams_of[12], (FF, D), (FF // 2) ** -0.5, 0.125, ((0, 4),)),
        "w_conv": bell_draw(streams_of[13], (RATE, D, D), (RATE * D) ** -0.5, 0.109375, ((2, 4),)),
        "cot_prompt": bell_draw(streams_of[14], (GROUPS, PROMPT, D), 1.0, 6.0, ((0, 8),)),
        "cot_cont": bell_draw(streams_of[15], (GROUPS, CONT * CLEN, D), 1.0, 6.0, ((0, 8),)),
    }


HIGH = lax.Precision.HIGHEST
EPSILON = 1e-05
NEGATIVE = -1e+30

@jax.custom_vjp
def low(v):
    return lax.optimization_barrier(v.astype(jnp.bfloat16)).astype(jnp.float32)

@jax.custom_vjp
def low_back(v):
    return v

def low_keep(v):
    return (low(v), None)

def low_pass(kept, grad):
    return (grad,)

def back_keep(v):
    return (v, None)

def back_low(kept, grad):
    return (low(grad),)
low.defvjp(low_keep, low_pass)
low_back.defvjp(back_keep, back_low)

def layer_norm(values, gain_vec):
    center = values - lax.optimization_barrier(jnp.mean(values, axis=-1, keepdims=True))
    scaled = center * lax.rsqrt(lax.optimization_barrier(jnp.mean(center * center, axis=-1, keepdims=True)) + EPSILON)
    return scaled * gain_vec

def allowed_keys(branch, prompt_len, cont_len, lead_rows):
    cont_count = branch.shape[0]
    all_rows = prompt_len + cont_count * cont_len
    query_pos = lax.broadcasted_iota(jnp.int32, (all_rows, 1), 0)
    key_pos = lax.broadcasted_iota(jnp.int32, (1, lead_rows + all_rows), 1) - lead_rows
    query_cont = jnp.where(query_pos >= prompt_len, (query_pos - prompt_len) // cont_len, -1)
    key_cont = jnp.where(key_pos >= prompt_len, (key_pos - prompt_len) // cont_len, -2)
    cont_index = lax.broadcasted_iota(jnp.int32, (1, cont_count), 1)
    seen_upto = lax.optimization_barrier(jnp.sum(jnp.where(query_cont == cont_index, branch[None, :], 0), axis=1, keepdims=True))
    seen_upto = jnp.where(query_pos >= prompt_len, seen_upto, query_pos + 1)
    in_prompt = (key_pos >= 0) & (key_pos < prompt_len) & (key_pos < seen_upto)
    in_cont = (query_cont == key_cont) & (key_pos <= query_pos)
    return (key_pos < 0) | in_prompt | in_cont

def split_heads(matrix):
    return matrix.reshape(matrix.shape[0], HEADS, HEAD_DIM)

def group_layer(weights, inputs):
    gain_attn, w_query, w_key, w_value, w_out, gain_ffn, w_up, w_down, w_conv = weights
    prompt_rows, cont_rows, memory_rows, old_rows, branch = inputs
    model_width = prompt_rows.shape[1]
    tokens_in = jnp.concatenate([prompt_rows, cont_rows], axis=0)
    row_count = tokens_in.shape[0]
    slot_count = old_rows.shape[0] // RATE
    squeezed = jnp.einsum('jtd,tde->je', old_rows.reshape(slot_count, RATE, model_width), w_conv, precision=HIGH)
    squeezed = low_back(low(squeezed))
    source = jnp.concatenate([squeezed, memory_rows, tokens_in], axis=0)
    lead_rows = slot_count + memory_rows.shape[0]
    normed = low(layer_norm(source, gain_attn))
    queries = split_heads(low_back(low(jnp.dot(normed[lead_rows:], w_query, precision=HIGH))))
    keys_all = split_heads(low_back(low(jnp.dot(normed, w_key, precision=HIGH))))
    values_all = split_heads(low_back(low(jnp.dot(normed, w_value, precision=HIGH))))
    scores = jnp.einsum('nhe,khe->hnk', queries, keys_all, precision=HIGH) * HEAD_DIM ** (-0.5)
    scores = low_back(scores)
    key_mask = allowed_keys(branch, prompt_rows.shape[0], CLEN, lead_rows)
    scores = jnp.where(key_mask[None], scores, NEGATIVE)
    probs = low(jax.nn.softmax(scores, axis=-1))
    mixed = jnp.einsum('hnk,khe->nhe', probs, values_all, precision=HIGH).reshape(row_count, HEADS * HEAD_DIM)
    mixed = low_back(low(mixed))
    partial_attn = jnp.einsum('ngc,gcd->gnd', mixed.reshape(row_count, N_TENSOR, -1), w_out.reshape(N_TENSOR, -1, model_width), precision=HIGH)
    attended = lax.optimization_barrier(jnp.sum(low(partial_attn), axis=0))
    hidden = tokens_in + low_back(attended)
    normed_ffn = low(layer_norm(hidden, gain_ffn))
    preact = low_back(jnp.dot(normed_ffn, w_up, precision=HIGH))
    active = low(jax.nn.gelu(preact, approximate=False))
    partial_ffn = jnp.einsum('ngf,gfd->gnd', active.reshape(row_count, N_TENSOR, -1), w_down.reshape(N_TENSOR, -1, model_width), precision=HIGH)
    return hidden + lax.optimization_barrier(jnp.sum(low(partial_ffn), axis=0))

def to_float(array_in):
    return array_in.astype(jnp.float32)

def reference(prompt, cont, memory, old_memory, branch_at, gain_attn, w_query, w_key, w_value, w_out, gain_ffn, w_up, w_down, w_conv, cot_prompt, cot_cont):
    weights = tuple((to_float(member) for member in (gain_attn, w_query, w_key, w_value, w_out, gain_ffn, w_up, w_down, w_conv)))
    memory_f = to_float(memory)
    old_f = to_float(old_memory)
    prompt_len = prompt.shape[1]

    def forward(prompt_x, cont_x, weight_set):
        step_fn = jax.checkpoint(lambda pieces: group_layer(weight_set, pieces))

        def scan_step(carry_val, pieces):
            return (carry_val, step_fn(pieces))
        unused, outputs = lax.scan(scan_step, jnp.float32(0.0), (prompt_x, cont_x, memory_f, old_f, branch_at))
        return (outputs[:, :prompt_len], outputs[:, prompt_len:])
    outputs, pullback = jax.vjp(forward, to_float(prompt), to_float(cont), weights)
    grad_p, grad_c, grad_w = pullback((to_float(cot_prompt), to_float(cot_cont)))
    return (outputs[0].astype(jnp.bfloat16), outputs[1].astype(jnp.bfloat16), grad_p.astype(jnp.bfloat16), grad_c.astype(jnp.bfloat16), grad_w[1], grad_w[2], grad_w[3], grad_w[4], grad_w[6], grad_w[7], grad_w[8], grad_w[0], grad_w[5])
```

```python
import functools
import math

import jax
import jax.numpy as jnp
from jax import lax
from jax.experimental import pallas as pl
from jax.experimental.pallas import tpu as pltpu
from jax.sharding import PartitionSpec as P

F32 = jnp.float32
BF16 = jnp.bfloat16
HEAD_DIM = 128
RATE = 3
EPSILON = 1e-05
NEGATIVE = -1e30
SCALE = HEAD_DIM**-0.5
LOG2E = math.log2(math.e)
SCALE2 = SCALE * LOG2E
VMEM_LIMIT = 56 * 1024 * 1024

TAIL_P = 0.3
TAIL = (
    0.11962927179738114,
    0.12075437242074172,
    0.09991089342247686,
    0.12857016178217745,
    -0.0536996295580258,
    0.20637064487815027,
    -0.15721286180378366,
    0.035677073905512405,
)


def dot(a, b):
    return lax.dot_general(a, b, (((1,), (0,)), ((), ())), preferred_element_type=F32)


def dot_nt(a, b):
    return lax.dot_general(a, b, (((1,), (1,)), ((), ())), preferred_element_type=F32)


def dot_tn(a, b):
    return lax.dot_general(a, b, (((0,), (0,)), ((), ())), preferred_element_type=F32)


def params(n):
    return pltpu.CompilerParams(
        dimension_semantics=("arbitrary",) * n, vmem_limit_bytes=VMEM_LIMIT
    )


def cost(flops, nbytes, trans=0):
    return pl.CostEstimate(flops=int(flops), bytes_accessed=int(nbytes), transcendentals=int(trans))


def normalize(values):
    center = values - jnp.mean(values, axis=-1, keepdims=True)
    inv_std = lax.rsqrt(jnp.mean(center * center, axis=-1, keepdims=True) + EPSILON)
    return center * inv_std, inv_std


def norm_pull(grad_outer, gain, scaled, inv_std):
    grad_scaled = grad_outer * gain
    mean_a = jnp.mean(grad_scaled, axis=-1, keepdims=True)
    mean_b = jnp.mean(grad_scaled * scaled, axis=-1, keepdims=True)
    return inv_std * (grad_scaled - mean_a - scaled * mean_b)


def gelu_both(x):
    a = jnp.abs(x)
    t = 1.0 / (1.0 + TAIL_P * a)
    poly = TAIL[7]
    for k in range(6, -1, -1):
        poly = poly * t + TAIL[k]
    bell = jnp.exp2((x * x) * (-0.5 * LOG2E))
    tail = bell * (t * poly)
    cdf = jnp.where(x >= 0.0, 1.0 - tail, tail)
    return x * cdf, cdf + x * (bell * (1.0 / math.sqrt(2.0 * math.pi)))


def conv_kernel(old_ref, w_ref, taps_ref, out_ref, wide):
    slots = out_ref.shape[1]
    lanes = wide.shape[2]
    for n in range(wide.shape[0]):
        wide[n] = old_ref[0, :, n * lanes:(n + 1) * lanes].astype(F32)
    total = None
    for t in range(RATE):
        rows = jnp.concatenate(
            [wide[n, pl.ds(t, slots, stride=RATE), :].astype(BF16) for n in range(wide.shape[0])], axis=1
        )
        taps_ref[t, 0] = rows
        part = dot(rows, w_ref[t])
        total = part if total is None else total + part
    out_ref[0] = total.astype(BF16)


def conv_call(old, w_conv):
    groups, rows, width = old.shape
    slots = rows // RATE
    cols = w_conv.shape[2]
    return pl.pallas_call(
        conv_kernel,
        name="conv",
        grid=(groups,),
        in_specs=[
            pl.BlockSpec((1, rows, width), lambda g: (g, 0, 0)),
            pl.BlockSpec((RATE, width, cols), lambda g: (0, 0, 0)),
        ],
        out_specs=[
            pl.BlockSpec((RATE, 1, slots, width), lambda g: (0, g, 0, 0)),
            pl.BlockSpec((1, slots, cols), lambda g: (g, 0, 0)),
        ],
        out_shape=[
            jax.ShapeDtypeStruct((RATE, groups, slots, width), BF16),
            jax.ShapeDtypeStruct((groups, slots, cols), BF16),
        ],
        scratch_shapes=[pltpu.VMEM((width // 128, rows, 128), F32)],
        compiler_params=params(1),
        cost_estimate=cost(2 * groups * rows * width * cols, 4 * groups * rows * width),
    )(old, w_conv)


def qkv_kernel(mem_ref, p_ref, c_ref, gain_ref, wq_ref, wk_ref, wv_ref,
               nm_ref, km_ref, vm_ref, nt_ref, qt_ref, kt_ref, vt_ref):
    j = pl.program_id(1)
    gain = gain_ref[...]

    @pl.when(j == 0)
    def _():
        scaled, _ = normalize(mem_ref[0].astype(F32))
        normed = (scaled * gain).astype(BF16)
        nm_ref[0] = normed
        km_ref[0] = dot(normed, wk_ref[...]).astype(BF16)
        vm_ref[0] = dot(normed, wv_ref[...]).astype(BF16)

    @pl.when(j > 0)
    def _():
        rows = jnp.concatenate([p_ref[0], c_ref[0]], axis=0).astype(F32)
        scaled, _ = normalize(rows)
        normed = (scaled * gain).astype(BF16)
        nt_ref[0] = normed
        qt_ref[0] = dot(normed, wq_ref[...]).astype(BF16)
        kt_ref[0] = dot(normed, wk_ref[...]).astype(BF16)
        vt_ref[0] = dot(normed, wv_ref[...]).astype(BF16)


def qkv_call(memory, prompt, cont, gain, w_query, w_key, w_value):
    groups, mem, width = memory.shape
    half_p, half_c = prompt.shape[1] // 2, cont.shape[1] // 2
    half = half_p + half_c
    cols = w_query.shape[1]
    whole = lambda g, j: (0, 0)
    lead = lambda g, j: (g, 0, 0)
    later = lambda g, j: (g, jnp.maximum(j - 1, 0), 0)
    sds = jax.ShapeDtypeStruct
    return pl.pallas_call(
        qkv_kernel,
        name="qkv",
        grid=(groups, 3),
        in_specs=[
            pl.BlockSpec((1, mem, width), lead),
            pl.BlockSpec((1, half_p, width), later),
            pl.BlockSpec((1, half_c, width), later),
            pl.BlockSpec((1, width), whole),
            pl.BlockSpec((width, cols), whole),
            pl.BlockSpec((width, cols), whole),
            pl.BlockSpec((width, cols), whole),
        ],
        out_specs=[
            pl.BlockSpec((1, mem, width), lead),
            pl.BlockSpec((1, mem, cols), lead),
            pl.BlockSpec((1, mem, cols), lead),
            pl.BlockSpec((1, half, width), later),
            pl.BlockSpec((1, half, cols), later),
            pl.BlockSpec((1, half, cols), later),
            pl.BlockSpec((1, half, cols), later),
        ],
        out_shape=[
            sds((groups, mem, width), BF16),
            sds((groups, mem, cols), BF16),
            sds((groups, mem, cols), BF16),
            sds((groups, 2 * half, width), BF16),
            sds((groups, 2 * half, cols), BF16),
            sds((groups, 2 * half, cols), BF16),
            sds((groups, 2 * half, cols), BF16),
        ],
        compiler_params=params(2),
        cost_estimate=cost(
            2 * groups * width * cols * (2 * mem + 6 * half), 8 * groups * (mem + 2 * half) * width
        ),
    )(memory, prompt, cont, gain, w_query, w_key, w_value)


def squeezed_kernel(place_ref, own_ref, far_ref, near_ref, diag_ref, gain_ref, wk_ref, wv_ref,
                    sq_ref, n_ref, k_ref, v_ref):
    cols = own_ref.shape[2]
    me = place_ref[0]
    for flip, block in ((0, own_ref), (2, far_ref), (1, near_ref), (3, diag_ref)):
        at = pl.multiple_of((me ^ flip) * cols, cols)
        sq_ref[0, :, pl.ds(at, cols)] = block[0]
    scaled, _ = normalize(sq_ref[0].astype(F32))
    normed = (scaled * gain_ref[...]).astype(BF16)
    n_ref[0] = normed
    k_ref[0] = dot(normed, wk_ref[...]).astype(BF16)
    v_ref[0] = dot(normed, wv_ref[...]).astype(BF16)


def squeezed_call(place, blocks, gain, w_key, w_value):
    groups, slots, cols = blocks[0].shape
    width = w_key.shape[0]
    sds = jax.ShapeDtypeStruct
    per_group = lambda g, s: (g, 0, 0)
    whole = lambda g, s: (0, 0)
    return pl.pallas_call(
        squeezed_kernel,
        name="squeezed",
        grid_spec=pltpu.PrefetchScalarGridSpec(
            num_scalar_prefetch=1,
            grid=(groups,),
            in_specs=[pl.BlockSpec((1, slots, cols), per_group)] * 4
            + [
                pl.BlockSpec((1, width), whole),
                pl.BlockSpec((width, cols), whole),
                pl.BlockSpec((width, cols), whole),
            ],
            out_specs=[
                pl.BlockSpec((1, slots, width), per_group),
                pl.BlockSpec((1, slots, width), per_group),
                pl.BlockSpec((1, slots, cols), per_group),
                pl.BlockSpec((1, slots, cols), per_group),
            ],
        ),
        out_shape=[
            sds((groups, slots, width), BF16),
            sds((groups, slots, width), BF16),
            sds((groups, slots, cols), BF16),
            sds((groups, slots, cols), BF16),
        ],
        compiler_params=params(1),
        cost_estimate=cost(4 * groups * slots * width * cols, 6 * groups * slots * width),
    )(place, *blocks, gain, w_key, w_value)


def tiles(half_p, half_c, branch_ref, group):
    half = half_p + half_c

    def causal(shape):
        return lax.broadcasted_iota(jnp.int32, shape, 0) <= lax.broadcasted_iota(jnp.int32, shape, 1)

    def seen(offset):
        def mask(shape):
            key = lax.broadcasted_iota(jnp.int32, shape, 0) + offset
            query = lax.broadcasted_iota(jnp.int32, shape, 1)
            return key < jnp.where(query < half_c, branch_ref[group, 0], branch_ref[group, 1])

        return mask

    first, second = (0, half_p), (half, half + half_p)
    cont0, cont1 = (half_p, half), (half + half_p, 2 * half)
    lead = [("s", None, None), ("m", None, None)]
    return [
        ([first], lead + [("t", first, causal)], None),
        ([second], lead + [("t", first, None), ("t", second, causal)], None),
        ([cont0, cont1], lead + [("t", first, seen(0)), ("t", second, seen(half_p))], causal),
    ]


def rows_of(ref, ranges):
    parts = [ref[a:b, :] for a, b in ranges]
    return parts[0] if len(parts) == 1 else jnp.concatenate(parts, axis=0)


def attn_kernel(group, half_p, half_c, branch_ref, q_ref, ks_ref, km_ref, kt_ref, vs_ref, vm_ref,
                vt_ref, mixed_ref, lse_ref):
    key_refs = {"s": ks_ref.at[0], "m": km_ref.at[0], "t": kt_ref.at[0]}
    value_refs = {"s": vs_ref.at[0], "m": vm_ref.at[0], "t": vt_ref.at[0]}
    query_ref = q_ref.at[0]
    vals = {
        ("s", None): value_refs["s"][...].T,
        ("m", None): value_refs["m"][...].T,
    }

    def value_t(source, span):
        if (source, span) not in vals:
            vals[(source, span)] = value_refs[source][span[0]:span[1], :].T
        return vals[(source, span)]

    for spans, pieces, own in tiles(half_p, half_c, branch_ref, group):
        q = rows_of(query_ref, spans)
        scores = []
        for source, span, mask in pieces:
            k = key_refs[source][...] if span is None else key_refs[source][span[0]:span[1], :]
            s = dot_nt(k, q)
            if mask is not None:
                s = jnp.where(mask(s.shape), s, NEGATIVE)
            scores.append(s)
        top = functools.reduce(jnp.maximum, [jnp.max(s, axis=0, keepdims=True) for s in scores])
        owns = []
        if own is not None:
            for span in spans:
                s = dot_nt(key_refs["t"][span[0]:span[1], :], query_ref[span[0]:span[1], :])
                owns.append(jnp.where(own(s.shape), s, NEGATIVE))
            top = jnp.maximum(
                top, jnp.concatenate([jnp.max(s, axis=0, keepdims=True) for s in owns], axis=1)
            )
        total = None
        out = None
        for (source, span, mask), s in zip(pieces, scores):
            p = jnp.exp2((s - top) * SCALE2)
            part = jnp.sum(p, axis=0, keepdims=True)
            term = dot(value_t(source, span), p.astype(BF16))
            total = part if total is None else total + part
            out = term if out is None else out + term
        if own is not None:
            width = half_c
            sums, terms = [], []
            for n, (span, s) in enumerate(zip(spans, owns)):
                p = jnp.exp2((s - top[:, n * width:(n + 1) * width]) * SCALE2)
                sums.append(jnp.sum(p, axis=0, keepdims=True))
                terms.append(dot(value_t("t", span), p.astype(BF16)))
            total = total + jnp.concatenate(sums, axis=1)
            out = out + jnp.concatenate(terms, axis=1)
        lse = top * SCALE2 + jnp.log(total) * LOG2E
        out = (out * (1.0 / total)).T.astype(BF16)
        at = 0
        for a, b in spans:
            mixed_ref[a:b, :] = out[at:at + b - a, :]
            lse_ref[0, :, a:b] = lse[:, at:at + b - a]
            at += b - a


def attn_call(group, branch, q, k, v, half_p, half_c):
    rows, cols = q.shape[1:]
    heads = cols // HEAD_DIM
    spec = lambda a: pl.BlockSpec((1, a.shape[1], HEAD_DIM), lambda h, s: (group, 0, h))
    keys = sum(a.shape[1] for a in k)
    return pl.pallas_call(
        functools.partial(attn_kernel, group, half_p, half_c),
        name=f"attn{group}",
        grid_spec=pltpu.PrefetchScalarGridSpec(
            num_scalar_prefetch=1,
            grid=(heads,),
            in_specs=[spec(a) for a in (q, *k, *v)],
            out_specs=[
                pl.BlockSpec((rows, HEAD_DIM), lambda h, s: (0, h)),
                pl.BlockSpec((1, 1, rows), lambda h, s: (h, 0, 0)),
            ],
        ),
        out_shape=[
            jax.ShapeDtypeStruct((rows, cols), BF16),
            jax.ShapeDtypeStruct((heads, 1, rows), F32),
        ],
        compiler_params=params(1),
        cost_estimate=cost(8 * heads * rows * keys * HEAD_DIM, 4 * keys * cols, heads * rows * keys),
    )(branch, q, *k, *v)


def attn_back_kernel(group, half_p, half_c, core_ref, branch_ref, q_ref, ks_ref, km_ref, kt_ref, vs_ref,
                     vm_ref, vt_ref, lse_ref, ga_own_ref, ga_oth_ref, wo_ref, wq_ref, wk_ref, wv_ref,
                     p_ref, c_ref, sq_ref, gain_ref,
                     dq_ref, dks_ref, dkm_ref, dkt_ref, dvs_ref, dvm_ref, dvt_ref,
                     send_ref, keep_ref, sqsend_ref, sqkeep_ref,
                     do_ref, kacc, vacc, wide):
    h = pl.program_id(0)
    half = half_p + half_c
    slots, mem = ks_ref.shape[1], km_ref.shape[1]
    me = core_ref[0]
    core = me & 1
    wo = wo_ref[...]
    do_ref[pl.ds(pl.multiple_of(core * half, half), half), :] = dot_nt(ga_own_ref[...], wo).astype(BF16)
    do_ref[pl.ds(pl.multiple_of((1 - core) * half, half), half), :] = dot_nt(ga_oth_ref[...], wo).astype(BF16)
    key_refs = {"s": ks_ref.at[0], "m": km_ref.at[0], "t": kt_ref.at[0]}
    value_refs = {"s": vs_ref.at[0], "m": vm_ref.at[0], "t": vt_ref.at[0]}
    starts = {"s": 0, "m": slots, "t": slots + mem}
    sizes = {"s": slots, "m": mem}
    query_ref = q_ref.at[0]
    column = pl.ds(pl.multiple_of(h * HEAD_DIM, HEAD_DIM), HEAD_DIM)
    done = set()

    def bounds(source, span):
        a, b = (0, sizes[source]) if span is None else span
        return starts[source] + a, starts[source] + b

    def gather(acc, source, span, value):
        a, b = bounds(source, span)
        if (id(acc), a) in done:
            acc[a:b, :] += value
        else:
            done.add((id(acc), a))
            acc[a:b, :] = value

    for spans, pieces, own in tiles(half_p, half_c, branch_ref, group):
        q = rows_of(query_ref, spans)
        do = rows_of(do_ref, spans)
        lse = [lse_ref[0, :, a:b] for a, b in spans]
        lse = lse[0] if len(lse) == 1 else jnp.concatenate(lse, axis=1)
        todo = [(source, span, mask, q, do, lse, None) for source, span, mask in pieces]
        if own is not None:
            for n, span in enumerate(spans):
                cut = slice(n * half_c, (n + 1) * half_c)
                todo.append(("t", span, own, q[cut, :], do[cut, :], lse[:, cut], n))
        kept = []
        row_dot = None
        own_dots = []
        for source, span, mask, qq, dd, ll, n in todo:
            k = key_refs[source][...] if span is None else key_refs[source][span[0]:span[1], :]
            v = value_refs[source][...] if span is None else value_refs[source][span[0]:span[1], :]
            s = dot_nt(k, qq)
            if mask is not None:
                s = jnp.where(mask(s.shape), s, NEGATIVE)
            p = jnp.exp2(s * SCALE2 - ll)
            dp = dot_nt(v, dd)
            part = jnp.sum(p * dp, axis=0, keepdims=True)
            if n is None:
                row_dot = part if row_dot is None else row_dot + part
            else:
                own_dots.append(part)
            kept.append((k, p, dp))
        if own_dots:
            row_dot = row_dot + jnp.concatenate(own_dots, axis=1)
        dq = None
        own_dq = []
        for (source, span, mask, qq, dd, ll, n), (k, p, dp) in zip(todo, kept):
            rd = row_dot if n is None else row_dot[:, n * half_c:(n + 1) * half_c]
            ds = (p * (dp - rd)).astype(BF16)
            gather(kacc, source, span, dot(ds, qq))
            gather(vacc, source, span, dot(p.astype(BF16), dd))
            term = dot_tn(k, ds)
            if n is None:
                dq = term if dq is None else dq + term
            else:
                own_dq.append(term)
        if own_dq:
            dq = dq + jnp.concatenate(own_dq, axis=1)
        dq = (dq * SCALE).T.astype(BF16)
        at = 0
        for a, b in spans:
            dq_ref[a:b, column] = dq[at:at + b - a, :]
            at += b - a
    for source, kref, vref, n in (("s", dks_ref, dvs_ref, slots), ("m", dkm_ref, dvm_ref, mem),
                                  ("t", dkt_ref, dvt_ref, 2 * half)):
        a = starts[source]
        kref[:, column] = (kacc[a:a + n, :] * SCALE).astype(BF16)
        vref[:, column] = vacc[a:a + n, :].astype(BF16)

    @pl.when(h == pl.num_programs(0) - 1)
    def _():
        gain = gain_ref[...]
        grad = dot_nt(dks_ref[...], wk_ref[...]) + dot_nt(dvs_ref[...], wv_ref[...])
        scaled, inv_std = normalize(sq_ref[0].astype(F32))
        wide[...] = norm_pull(grad, gain, scaled, inv_std)
        cols = sqkeep_ref.shape[2]
        for ref, n, flip in ((sqkeep_ref, 0, 0), (sqkeep_ref, 1, 2), (sqsend_ref, 0, 1), (sqsend_ref, 1, 3)):
            at = pl.multiple_of((me ^ flip) * cols, cols)
            ref[n] = wide[:, pl.ds(at, cols)].astype(BF16)
        for ref, part in ((send_ref, 1 - core), (keep_ref, core)):
            rows = pl.ds(pl.multiple_of(part * half, half), half)
            grad = (
                dot_nt(dkt_ref[rows, :], wk_ref[...])
                + dot_nt(dvt_ref[rows, :], wv_ref[...])
                + dot_nt(dq_ref[rows, :], wq_ref[...])
            )
            x = jnp.concatenate(
                [
                    p_ref[0, pl.ds(pl.multiple_of(part * half_p, half_p), half_p), :],
                    c_ref[0, pl.ds(pl.multiple_of(part * half_c, half_c), half_c), :],
                ],
                axis=0,
            ).astype(F32)
            scaled, inv_std = normalize(x)
            ref[...] = norm_pull(grad, gain, scaled, inv_std).astype(BF16)


def attn_back_call(group, place, branch, q, k, v, lse, ga_own, ga_oth, w_out, w_query, w_key, w_value,
                   prompt, cont, squeezed, gain):
    rows, cols = q.shape[1:]
    heads = cols // HEAD_DIM
    half_p, half_c = prompt.shape[1] // 2, cont.shape[1] // 2
    half = half_p + half_c
    width = prompt.shape[2]
    keys = [a.shape[1] for a in k]
    n_keys = sum(keys)
    slots = keys[0]
    spec = lambda a: pl.BlockSpec((1, a.shape[1], HEAD_DIM), lambda h, *s: (group, 0, h))
    full = lambda *shape: pl.BlockSpec(shape, lambda h, *s: (0,) * len(shape))
    mine = lambda a: pl.BlockSpec((1,) + a.shape[1:], lambda h, *s: (group, 0, 0))
    sds = jax.ShapeDtypeStruct
    return pl.pallas_call(
        functools.partial(attn_back_kernel, group, half_p, half_c),
        name=f"attnback{group}",
        grid_spec=pltpu.PrefetchScalarGridSpec(
            num_scalar_prefetch=2,
            grid=(heads,),
            in_specs=[spec(a) for a in (q, *k, *v)]
            + [
                pl.BlockSpec((1, 1, rows), lambda h, *s: (h, 0, 0)),
                full(half, width),
                full(half, width),
                pl.BlockSpec((HEAD_DIM, width), lambda h, *s: (h, 0)),
                full(width, cols),
                full(width, cols),
                full(width, cols),
                mine(prompt),
                mine(cont),
                mine(squeezed),
                full(1, width),
            ],
            out_specs=[full(rows, cols)]
            + [full(n, cols) for n in keys] * 2
            + [full(half, width)] * 2
            + [full(2, slots, cols)] * 2,
            scratch_shapes=[
                pltpu.VMEM((rows, HEAD_DIM), BF16),
                pltpu.VMEM((n_keys, HEAD_DIM), F32),
                pltpu.VMEM((n_keys, HEAD_DIM), F32),
                pltpu.VMEM((slots, width), F32),
            ],
        ),
        out_shape=[sds((rows, cols), BF16)]
        + [sds((n, cols), BF16) for n in keys] * 2
        + [sds((half, width), BF16)] * 2
        + [sds((2, slots, cols), BF16)] * 2,
        compiler_params=params(1),
        cost_estimate=cost(
            20 * heads * rows * n_keys * HEAD_DIM + 8 * rows * width * cols,
            8 * n_keys * cols + 12 * rows * width,
            heads * rows * n_keys,
        ),
    )(place, branch, q, *k, *v, lse, ga_own, ga_oth, w_out, w_query, w_key, w_value, prompt, cont,
      squeezed, gain)


def ffn_kernel(core_ref, p_ref, c_ref, cp_ref, cc_ref, m0_ref, m2_ref, m1_ref, m3_ref,
               w0_ref, w2_ref, w1_ref, w3_ref, gain_ref, up_ref, down_ref,
               hid_ref, nf_ref, act_ref, pre_ref, gsend_ref, gkeep_ref, fsend_ref, fkeep_ref):
    j = pl.program_id(0)
    gain = gain_ref[...]
    tokens = jnp.concatenate([p_ref[0], c_ref[0]], axis=0).astype(F32)
    cot = jnp.concatenate([cp_ref[0], cc_ref[0]], axis=0)
    attended = (dot(m0_ref[...], w0_ref[...]) + dot(m2_ref[...], w2_ref[...])) + (
        dot(m1_ref[...], w1_ref[...]) + dot(m3_ref[...], w3_ref[...])
    )
    hidden = tokens + attended
    hid_ref[...] = hidden
    scaled, inv_std = normalize(hidden)
    normed = (scaled * gain).astype(BF16)
    nf_ref[...] = normed
    units = up_ref.shape[1]
    chunk = 256
    for a in range(0, units, chunk):
        cut = slice(a, a + chunk)
        pre = dot(normed, up_ref[:, cut])
        grad = dot_nt(cot, down_ref[cut, :])
        active, slope = gelu_both(pre)
        act_ref[:, cut] = active.astype(BF16)
        pre_ref[:, cut] = (grad * slope).astype(BF16)
    grad = dot_nt(pre_ref[...], up_ref[...])
    grad = norm_pull(grad, gain, scaled, inv_std).astype(BF16)
    term = dot(act_ref[...], down_ref[...]).astype(BF16)

    @pl.when(j == 0)
    def _():
        gsend_ref[...] = grad
        fsend_ref[...] = term

    @pl.when(j == 1)
    def _():
        gkeep_ref[...] = grad
        fkeep_ref[...] = term


def ffn_call(group, place, prompt, cont, cot_p, cot_c, mixed, w_out, gain, w_up, w_down):
    half_p, half_c = prompt.shape[1] // 2, cont.shape[1] // 2
    half = half_p + half_c
    width = prompt.shape[2]
    cols = mixed[0].shape[1]
    units = w_up.shape[1]

    def part(j, s):
        core = s[0] & 1
        return jnp.where(j == 0, 1 - core, core)

    tok = lambda n: pl.BlockSpec((1, n, width), lambda j, s: (group, part(j, s), 0))
    full = lambda *shape: pl.BlockSpec(shape, lambda j, s: (0, 0), pipeline_mode=pl.Buffered(1))
    moving = lambda n: pl.BlockSpec((half, n), lambda j, s: (part(j, s), 0))
    fixed = pl.BlockSpec((half, width), lambda j, s: (0, 0))
    sds = jax.ShapeDtypeStruct
    return pl.pallas_call(
        ffn_kernel,
        name=f"ffn{group}",
        grid_spec=pltpu.PrefetchScalarGridSpec(
            num_scalar_prefetch=1,
            grid=(2,),
            in_specs=[tok(half_p), tok(half_c), tok(half_p), tok(half_c)]
            + [moving(cols)] * 4
            + [full(cols, width)] * 4
            + [full(1, width), full(width, units), full(units, width)],
            out_specs=[fixed, moving(width), moving(units), moving(units)] + [fixed] * 4,
        ),
        out_shape=[
            sds((half, width), F32),
            sds((2 * half, width), BF16),
            sds((2 * half, units), BF16),
            sds((2 * half, units), BF16),
        ]
        + [sds((half, width), BF16)] * 4,
        compiler_params=params(1),
        cost_estimate=cost(
            4 * half * width * (4 * units + 4 * cols), 2 * half * (14 * width), 4 * half * units
        ),
    )(place, prompt, cont, cot_p, cot_c, *mixed, *w_out, gain, w_up, w_down)


def swap(x, flip, axis="tensor"):
    return lax.ppermute(x, axis, [(i, i ^ flip) for i in range(lax.axis_size(axis))])


def add_low(a, b):
    return (a.astype(F32) + b.astype(F32)).astype(BF16)


def spread_sum(rows, order):
    count = lax.axis_size("dp")
    bits = count.bit_length() - 1
    if 1 << bits != count:
        return lax.psum_scatter(rows, "dp", scatter_dimension=0, tiled=True).astype(F32)
    me = lax.axis_index("dp")
    cols = rows.shape[1]
    now = rows.reshape((2,) * bits + (rows.shape[0] // count, cols))
    left = list(range(bits - 1, -1, -1))
    order = [b for b in order if b < bits] + [b for b in range(bits) if b not in order]
    for n, bit in enumerate(order):
        dim = left.index(bit)
        left.pop(dim)
        mine = (me >> bit) & 1
        send = lax.dynamic_index_in_dim(now, 1 - mine, dim, keepdims=False)
        keep = lax.dynamic_index_in_dim(now, mine, dim, keepdims=False)
        got = swap(send, 1 << bit, "dp")
        now = keep.astype(F32) + got.astype(F32)
        if n < bits - 1:
            now = now.astype(BF16)
    return now


def per_device(prompt, cont, memory, old_memory, branch_at, gain_attn, w_query, w_key, w_value, w_out,
               gain_ffn, w_up, w_down, w_conv, cot_prompt, cot_cont):
    groups, prompt_len, width = prompt.shape
    half_p, half_c = prompt_len // 2, cont.shape[1] // 2
    half = half_p + half_c
    me = lax.axis_index("tensor")
    core = me & 1
    place = jnp.reshape(me, (1,)).astype(jnp.int32)
    gain_a = gain_attn.reshape(1, width)
    gain_f = gain_ffn.reshape(1, width)

    taps, sq_own = conv_call(old_memory, w_conv)
    sq_far = swap(sq_own, 2)
    sq_near = swap(sq_own, 1)
    sq_diag = swap(sq_far, 1)
    w_far = swap(w_out, 2)
    w_near = swap(w_out, 1)
    w_diag = swap(w_far, 1)
    w_all = (w_out, w_far, w_near, w_diag)

    n_mem, k_mem, v_mem, n_tok, q_tok, k_tok, v_tok = qkv_call(
        memory, prompt, cont, gain_a, w_query, w_key, w_value
    )
    squeezed, n_sq, k_sq, v_sq = squeezed_call(
        place, (sq_own, sq_far, sq_near, sq_diag), gain_a, w_key, w_value
    )
    keys = (k_sq, k_mem, k_tok)
    values = (v_sq, v_mem, v_tok)

    mixed, lse = [], []
    for g in range(groups):
        m, l = attn_call(g, branch_at, q_tok, keys, values, half_p, half_c)
        mixed.append(m)
        lse.append(l)
    ffn = []
    for g in range(groups):
        far = swap(mixed[g], 2)
        near = swap(mixed[g], 1)
        diag = swap(far, 1)
        ffn.append(
            ffn_call(
                g, place, prompt, cont, cot_prompt, cot_cont, (mixed[g], far, near, diag), w_all,
                gain_f, w_up, w_down,
            )
        )
    mine_p = lax.dynamic_slice_in_dim(cot_prompt, core * half_p, half_p, 1)
    mine_c = lax.dynamic_slice_in_dim(cot_cont, core * half_c, half_c, 1)
    cot_own = jnp.concatenate([mine_p, mine_c], axis=1)
    outs, grads, back = [], [], []
    for g in range(groups):
        hid, nf, act, pre, gsend, gkeep, fsend, fkeep = ffn[g]
        chip = add_low(gkeep, swap(gsend, 1))
        other = swap(chip, 2)
        grad_hidden = cot_own[g].astype(F32) + (chip.astype(F32) + other.astype(F32))
        ga_own = grad_hidden.astype(BF16)
        ga_oth = swap(ga_own, 1)
        back.append(
            attn_back_call(
                g, place, branch_at, q_tok, keys, values, lse[g], ga_own, ga_oth, w_out, w_query, w_key,
                w_value, prompt, cont, squeezed, gain_a,
            )
        )
        grads.append((grad_hidden, ga_own, ga_oth))
        chip = add_low(fkeep, swap(fsend, 1))
        other = swap(chip, 2)
        outs.append((hid + (chip.astype(F32) + other.astype(F32))).astype(BF16))

    token_grads = []
    for g in range(groups):
        send, keep = back[g][7], back[g][8]
        chip = add_low(keep, swap(send, 1))
        other = swap(chip, 2)
        token_grads.append((grads[g][0] + (chip.astype(F32) + other.astype(F32))).astype(BF16))

    def assemble(own):
        own = jnp.stack(own)
        oth = swap(own, 1)
        low = jnp.where(core == 0, own, oth)
        high = jnp.where(core == 0, oth, own)
        return (
            jnp.concatenate([low[:, :half_p], high[:, :half_p]], axis=1),
            jnp.concatenate([low[:, half_p:], high[:, half_p:]], axis=1),
        )

    out_prompt, out_cont = assemble(outs)
    grad_prompt, grad_cont = assemble(token_grads)

    grad_up = sum(dot_tn(ffn[g][1], ffn[g][3]) for g in range(groups))
    cot_tok = [
        jnp.concatenate(
            [cot_prompt[g, :half_p], cot_cont[g, :half_c], cot_prompt[g, half_p:], cot_cont[g, half_c:]], axis=0
        )
        for g in range(groups)
    ]
    grad_down_t = sum(dot_tn(cot_tok[g], ffn[g][2]) for g in range(groups))
    part_f = jnp.sum(grad_up * w_up.astype(F32), axis=1) / gain_ffn

    ga_tok = []
    for g in range(groups):
        _, own, oth = grads[g]
        ga_tok.append(
            jnp.concatenate([jnp.where(core == 0, own, oth), jnp.where(core == 0, oth, own)], axis=0)
        )
    grad_out_t = sum(dot_tn(ga_tok[g], mixed[g]) for g in range(groups))
    grad_q = sum(dot_tn(n_tok[g], back[g][0]) for g in range(groups))
    grad_k = sum(
        dot_tn(n_sq[g], back[g][1]) + dot_tn(n_mem[g], back[g][2]) + dot_tn(n_tok[g], back[g][3])
        for g in range(groups)
    )
    grad_v = sum(
        dot_tn(n_sq[g], back[g][4]) + dot_tn(n_mem[g], back[g][5]) + dot_tn(n_tok[g], back[g][6])
        for g in range(groups)
    )
    part_a = (
        jnp.sum(
            grad_q * w_query.astype(F32) + grad_k * w_key.astype(F32) + grad_v * w_value.astype(F32), axis=1
        )
        / gain_attn
    )
    sq_send = jnp.stack([back[g][9] for g in range(groups)])
    sq_keep = jnp.stack([back[g][10] for g in range(groups)])
    chip = add_low(sq_keep, swap(sq_send, 1))
    got = swap(chip[:, 1], 2)
    grad_sq = add_low(chip[:, 0], got)
    slots = grad_sq.shape[1]
    grad_conv = [dot_tn(taps[t].reshape(groups * slots, width), grad_sq.reshape(groups * slots, -1)) for t in range(RATE)]

    units = w_up.shape[1]
    cols = w_query.shape[1]
    first = jnp.concatenate([grad_up.astype(BF16), grad_down_t.astype(BF16)], axis=1)
    first = lax.psum_scatter(first, "dp", scatter_dimension=0, tiled=True).astype(F32)
    second = spread_sum(
        jnp.concatenate([a.astype(BF16) for a in (grad_out_t, grad_q, grad_k, grad_v)], axis=1), (0, 1, 2)
    )
    third = spread_sum(jnp.concatenate([a.astype(BF16) for a in grad_conv], axis=1), (1, 0, 2))
    gains = lax.psum(jnp.stack([part_a, part_f]), ("dp", "tensor"))
    rows = width // lax.axis_size("dp")
    gains = lax.dynamic_slice_in_dim(gains, lax.axis_index("dp") * rows, rows, 1)
    conv = jnp.stack([third[:, t * cols:(t + 1) * cols] for t in range(RATE)])
    return (
        out_prompt,
        out_cont,
        grad_prompt,
        grad_cont,
        second[:, cols:2 * cols],
        second[:, 2 * cols:3 * cols],
        second[:, 3 * cols:4 * cols],
        second[:, :cols].T,
        first[:, :units],
        first[:, units:].T,
        conv,
        gains[0],
        gains[1],
    )


def solution(mesh):
    tokens = P("dp", None, None)
    split = P(None, "tensor")
    in_specs = (
        tokens, tokens, tokens, tokens, P("dp", None), P(), split, split, split, P("tensor", None), P(),
        split, P("tensor", None), P(None, None, "tensor"), tokens, tokens,
    )
    both = P("dp", "tensor")
    out_specs = (
        tokens, tokens, tokens, tokens, both, both, both, P("tensor", "dp"), both, P("tensor", "dp"),
        P(None, "dp", "tensor"), P("dp"), P("dp"),
    )
    return jax.shard_map(per_device, mesh=mesh, in_specs=in_specs, out_specs=out_specs, check_vma=False)
```

```python
import functools
import math

import jax
import jax.numpy as jnp
from jax import lax
from jax.experimental import pallas as pl
from jax.experimental.pallas import tpu as pltpu
from jax.sharding import PartitionSpec as P

F32 = jnp.float32
BF16 = jnp.bfloat16
HEAD_DIM = 128
RATE = 3
EPSILON = 1e-05
NEGATIVE = -1e30
SCALE = HEAD_DIM**-0.5
LOG2E = math.log2(math.e)
SCALE2 = SCALE * LOG2E
COST = 0.05
VMEM_LIMIT = 56 * 1024 * 1024
ANY = pl.BlockSpec(memory_space=pl.ANY)

TAIL_P = 0.3
TAIL = (
    0.11962927179738114,
    0.12075437242074172,
    0.09991089342247686,
    0.12857016178217745,
    -0.0536996295580258,
    0.20637064487815027,
    -0.15721286180378366,
    0.035677073905512405,
)


def dot(a, b):
    return lax.dot_general(a, b, (((1,), (0,)), ((), ())), preferred_element_type=F32)


def dot_nt(a, b):
    return lax.dot_general(a, b, (((1,), (1,)), ((), ())), preferred_element_type=F32)


def dot_tn(a, b):
    return lax.dot_general(a, b, (((0,), (0,)), ((), ())), preferred_element_type=F32)


def params(n):
    return pltpu.CompilerParams(
        dimension_semantics=("arbitrary",) * n, vmem_limit_bytes=VMEM_LIMIT
    )


def cost(flops, nbytes, trans=0):
    return pl.CostEstimate(
        flops=int(flops * COST), bytes_accessed=int(nbytes * COST), transcendentals=int(trans * COST)
    )


def normalize(values):
    center = values - jnp.mean(values, axis=-1, keepdims=True)
    inv_std = lax.rsqrt(jnp.mean(center * center, axis=-1, keepdims=True) + EPSILON)
    return center * inv_std, inv_std


def norm_pull(grad_outer, gain, scaled, inv_std):
    grad_scaled = grad_outer * gain
    mean_a = jnp.mean(grad_scaled, axis=-1, keepdims=True)
    mean_b = jnp.mean(grad_scaled * scaled, axis=-1, keepdims=True)
    return inv_std * (grad_scaled - mean_a - scaled * mean_b)


def gelu_both(x):
    a = jnp.abs(x)
    t = 1.0 / (1.0 + TAIL_P * a)
    poly = TAIL[7]
    for k in range(6, -1, -1):
        poly = poly * t + TAIL[k]
    bell = jnp.exp2((x * x) * (-0.5 * LOG2E))
    tail = bell * (t * poly)
    cdf = jnp.where(x >= 0.0, 1.0 - tail, tail)
    return x * cdf, cdf + x * (bell * (1.0 / math.sqrt(2.0 * math.pi)))


def tap_rows(old_ref, wide, group):
    lanes = wide.shape[2]
    slots = wide.shape[1] // RATE
    for n in range(wide.shape[0]):
        wide[n] = old_ref[group, :, n * lanes:(n + 1) * lanes].astype(F32)
    return [
        jnp.concatenate(
            [wide[n, pl.ds(t, slots, stride=RATE), :].astype(BF16) for n in range(wide.shape[0])], axis=1
        )
        for t in range(RATE)
    ]


def conv_kernel(old_ref, w_ref, out_ref, wide):
    total = None
    for t, rows in enumerate(tap_rows(old_ref, wide, 0)):
        part = dot(rows, w_ref[t])
        total = part if total is None else total + part
    out_ref[0] = total.astype(BF16)


def conv_call(old, w_conv):
    groups, rows, width = old.shape
    slots = rows // RATE
    cols = w_conv.shape[2]
    return pl.pallas_call(
        conv_kernel,
        name="conv",
        grid=(groups,),
        in_specs=[
            pl.BlockSpec((1, rows, width), lambda g: (g, 0, 0)),
            pl.BlockSpec((RATE, width, cols), lambda g: (0, 0, 0)),
        ],
        out_specs=pl.BlockSpec((1, slots, cols), lambda g: (g, 0, 0)),
        out_shape=jax.ShapeDtypeStruct((groups, slots, cols), BF16),
        scratch_shapes=[pltpu.VMEM((width // 128, rows, 128), F32)],
        compiler_params=params(1),
        cost_estimate=cost(2 * groups * rows * width * cols, 2 * groups * rows * width),
    )(old, w_conv)


def taps_kernel(old_ref, wait_ref, out_ref, wide):
    for t, rows in enumerate(tap_rows(old_ref, wide, 0)):
        out_ref[t, 0] = rows


def taps_call(old, wait):
    groups, rows, width = old.shape
    slots = rows // RATE
    return pl.pallas_call(
        taps_kernel,
        name="taps",
        grid=(groups,),
        in_specs=[pl.BlockSpec((1, rows, width), lambda g: (g, 0, 0)), ANY],
        out_specs=pl.BlockSpec((RATE, 1, slots, width), lambda g: (0, g, 0, 0)),
        out_shape=jax.ShapeDtypeStruct((RATE, groups, slots, width), BF16),
        scratch_shapes=[pltpu.VMEM((width // 128, rows, 128), F32)],
        compiler_params=params(1),
        cost_estimate=cost(0, 4 * groups * rows * width),
    )(old, wait)


def qkv_kernel(mem_ref, p_ref, c_ref, gain_ref, wq_ref, wk_ref, wv_ref, wait_ref,
               nm_ref, km_ref, vm_ref, nt_ref, qt_ref, kt_ref, vt_ref):
    j = pl.program_id(1)
    gain = gain_ref[...]

    @pl.when(j == 0)
    def _():
        scaled, _ = normalize(mem_ref[0].astype(F32))
        normed = (scaled * gain).astype(BF16)
        nm_ref[0] = normed
        km_ref[0] = dot(normed, wk_ref[...]).astype(BF16)
        vm_ref[0] = dot(normed, wv_ref[...]).astype(BF16)

    @pl.when(j > 0)
    def _():
        rows = jnp.concatenate([p_ref[0], c_ref[0]], axis=0).astype(F32)
        scaled, _ = normalize(rows)
        normed = (scaled * gain).astype(BF16)
        nt_ref[0] = normed
        qt_ref[0] = dot(normed, wq_ref[...]).astype(BF16)
        kt_ref[0] = dot(normed, wk_ref[...]).astype(BF16)
        vt_ref[0] = dot(normed, wv_ref[...]).astype(BF16)


def qkv_call(memory, prompt, cont, gain, w_query, w_key, w_value, wait):
    groups, mem, width = memory.shape
    half_p, half_c = prompt.shape[1] // 2, cont.shape[1] // 2
    half = half_p + half_c
    cols = w_query.shape[1]
    whole = lambda g, j: (0, 0)
    lead = lambda g, j: (g, 0, 0)
    later = lambda g, j: (g, jnp.maximum(j - 1, 0), 0)
    sds = jax.ShapeDtypeStruct
    return pl.pallas_call(
        qkv_kernel,
        name="qkv",
        grid=(groups, 3),
        in_specs=[
            pl.BlockSpec((1, mem, width), lead),
            pl.BlockSpec((1, half_p, width), later),
            pl.BlockSpec((1, half_c, width), later),
            pl.BlockSpec((1, width), whole),
            pl.BlockSpec((width, cols), whole),
            pl.BlockSpec((width, cols), whole),
            pl.BlockSpec((width, cols), whole),
            ANY,
        ],
        out_specs=[
            pl.BlockSpec((1, mem, width), lead),
            pl.BlockSpec((1, mem, cols), lead),
            pl.BlockSpec((1, mem, cols), lead),
            pl.BlockSpec((1, half, width), later),
            pl.BlockSpec((1, half, cols), later),
            pl.BlockSpec((1, half, cols), later),
            pl.BlockSpec((1, half, cols), later),
        ],
        out_shape=[
            sds((groups, mem, width), BF16),
            sds((groups, mem, cols), BF16),
            sds((groups, mem, cols), BF16),
            sds((groups, 2 * half, width), BF16),
            sds((groups, 2 * half, cols), BF16),
            sds((groups, 2 * half, cols), BF16),
            sds((groups, 2 * half, cols), BF16),
        ],
        compiler_params=params(2),
        cost_estimate=cost(
            2 * groups * width * cols * (2 * mem + 6 * half), 8 * groups * (mem + 2 * half) * width
        ),
    )(memory, prompt, cont, gain, w_query, w_key, w_value, wait)


def tiles(half_p, half_c, branch_ref, group):
    half = half_p + half_c

    def causal(shape):
        return lax.broadcasted_iota(jnp.int32, shape, 0) <= lax.broadcasted_iota(jnp.int32, shape, 1)

    def seen(offset):
        def mask(shape):
            key = lax.broadcasted_iota(jnp.int32, shape, 0) + offset
            query = lax.broadcasted_iota(jnp.int32, shape, 1)
            return key < jnp.where(query < half_c, branch_ref[group, 0], branch_ref[group, 1])

        return mask

    first, second = (0, half_p), (half, half + half_p)
    cont0, cont1 = (half_p, half), (half + half_p, 2 * half)
    lead = [("s", None, None), ("m", None, None)]
    return [
        ([first], lead + [("t", first, causal)], None),
        ([second], lead + [("t", first, None), ("t", second, causal)], None),
        ([cont0, cont1], lead + [("t", first, seen(0)), ("t", second, seen(half_p))], causal),
    ]


def rows_of(ref, ranges):
    parts = [ref[a:b, :] for a, b in ranges]
    return parts[0] if len(parts) == 1 else jnp.concatenate(parts, axis=0)


def attn_kernel(group, half_p, half_c, place_ref, branch_ref, own_ref, far_ref, near_ref, diag_ref, gain_ref,
                wk_ref, wv_ref, q_ref, km_ref, kt_ref, vm_ref, vt_ref, wait_ref,
                sq_ref, n_ref, ks_ref, vs_ref, mixed_ref, lse_ref):
    h = pl.program_id(0)
    cols = own_ref.shape[2]
    column = pl.ds(pl.multiple_of(h * HEAD_DIM, HEAD_DIM), HEAD_DIM)

    @pl.when(h == 0)
    def _():
        me = place_ref[0]
        for flip, block in ((0, own_ref), (2, far_ref), (1, near_ref), (3, diag_ref)):
            at = pl.multiple_of((me ^ flip) * cols, cols)
            sq_ref[:, pl.ds(at, cols)] = block[0]
        scaled, _ = normalize(sq_ref[...].astype(F32))
        normed = (scaled * gain_ref[...]).astype(BF16)
        n_ref[...] = normed
        ks_ref[...] = dot(normed, wk_ref[...]).astype(BF16)
        vs_ref[...] = dot(normed, wv_ref[...]).astype(BF16)

    key_refs = {"m": km_ref.at[0], "t": kt_ref.at[0]}
    value_refs = {"m": vm_ref.at[0], "t": vt_ref.at[0]}
    query_ref = q_ref.at[0]
    vals = {("s", None): vs_ref[:, column].T, ("m", None): value_refs["m"][...].T}

    def key(source, span):
        if source == "s":
            return ks_ref[:, column]
        return key_refs[source][...] if span is None else key_refs[source][span[0]:span[1], :]

    def value_t(source, span):
        if (source, span) not in vals:
            vals[(source, span)] = value_refs[source][span[0]:span[1], :].T
        return vals[(source, span)]

    for spans, pieces, own in tiles(half_p, half_c, branch_ref, group):
        q = rows_of(query_ref, spans)
        scores = []
        for source, span, mask in pieces:
            s = dot_nt(key(source, span), q)
            if mask is not None:
                s = jnp.where(mask(s.shape), s, NEGATIVE)
            scores.append(s)
        top = functools.reduce(jnp.maximum, [jnp.max(s, axis=0, keepdims=True) for s in scores])
        owns = []
        if own is not None:
            for span in spans:
                s = dot_nt(key_refs["t"][span[0]:span[1], :], query_ref[span[0]:span[1], :])
                owns.append(jnp.where(own(s.shape), s, NEGATIVE))
            top = jnp.maximum(
                top, jnp.concatenate([jnp.max(s, axis=0, keepdims=True) for s in owns], axis=1)
            )
        total = None
        out = None
        for (source, span, mask), s in zip(pieces, scores):
            p = jnp.exp2((s - top) * SCALE2)
            part = jnp.sum(p, axis=0, keepdims=True)
            term = dot(value_t(source, span), p.astype(BF16))
            total = part if total is None else total + part
            out = term if out is None else out + term
        if own is not None:
            width = half_c
            sums, terms = [], []
            for n, (span, s) in enumerate(zip(spans, owns)):
                p = jnp.exp2((s - top[:, n * width:(n + 1) * width]) * SCALE2)
                sums.append(jnp.sum(p, axis=0, keepdims=True))
                terms.append(dot(value_t("t", span), p.astype(BF16)))
            total = total + jnp.concatenate(sums, axis=1)
            out = out + jnp.concatenate(terms, axis=1)
        lse = top * SCALE2 + jnp.log(total) * LOG2E
        out = (out * (1.0 / total)).T.astype(BF16)
        at = 0
        for a, b in spans:
            mixed_ref[a:b, :] = out[at:at + b - a, :]
            lse_ref[0, :, a:b] = lse[:, at:at + b - a]
            at += b - a


def attn_call(group, place, branch, blocks, gain, w_key, w_value, q, k, v, half_p, half_c, wait):
    rows, cols = q.shape[1:]
    heads = cols // HEAD_DIM
    slots = blocks[0].shape[1]
    width = w_key.shape[0]
    spec = lambda a: pl.BlockSpec((1, a.shape[1], HEAD_DIM), lambda h, *s: (group, 0, h))
    full = lambda *shape: pl.BlockSpec(shape, lambda h, *s: (0, 0))
    sds = jax.ShapeDtypeStruct
    keys = sum(a.shape[1] for a in k)
    return pl.pallas_call(
        functools.partial(attn_kernel, group, half_p, half_c),
        name=f"attn{group}",
        grid_spec=pltpu.PrefetchScalarGridSpec(
            num_scalar_prefetch=2,
            grid=(heads,),
            in_specs=[pl.BlockSpec((1, slots, cols), lambda h, *s: (group, 0, 0))] * 4
            + [full(1, width), full(width, cols), full(width, cols)]
            + [spec(a) for a in (q, *k, *v)]
            + [ANY],
            out_specs=[
                full(slots, width),
                full(slots, width),
                full(slots, cols),
                full(slots, cols),
                pl.BlockSpec((rows, HEAD_DIM), lambda h, *s: (0, h)),
                pl.BlockSpec((1, 1, rows), lambda h, *s: (h, 0, 0)),
            ],
        ),
        out_shape=[
            sds((slots, width), BF16),
            sds((slots, width), BF16),
            sds((slots, cols), BF16),
            sds((slots, cols), BF16),
            sds((rows, cols), BF16),
            sds((heads, 1, rows), F32),
        ],
        compiler_params=params(1),
        cost_estimate=cost(8 * heads * rows * keys * HEAD_DIM, 4 * keys * cols, heads * rows * keys),
    )(place, branch, *blocks, gain, w_key, w_value, q, *k, *v, wait)


def attn_back_kernel(group, half_p, half_c, core_ref, branch_ref, q_ref, ks_ref, km_ref, kt_ref, vs_ref,
                     vm_ref, vt_ref, lse_ref, ga_own_ref, ga_oth_ref, wo_ref, wq_ref, wk_ref, wv_ref,
                     p_ref, c_ref, sq_ref, gain_ref, wait_ref,
                     ds_ref, dm_ref, dt_ref, send_ref, keep_ref, sqsend_ref, sqkeep_ref,
                     do_ref, kacc, vacc, wide):
    h = pl.program_id(0)
    half = half_p + half_c
    cols = wq_ref.shape[1]
    slots, mem = ks_ref.shape[0], km_ref.shape[1]
    me = core_ref[0]
    core = me & 1
    wo = wo_ref[...]
    do_ref[pl.ds(pl.multiple_of(core * half, half), half), :] = dot_nt(ga_own_ref[...], wo).astype(BF16)
    do_ref[pl.ds(pl.multiple_of((1 - core) * half, half), half), :] = dot_nt(ga_oth_ref[...], wo).astype(BF16)
    key_refs = {"s": ks_ref, "m": km_ref.at[0], "t": kt_ref.at[0]}
    value_refs = {"s": vs_ref, "m": vm_ref.at[0], "t": vt_ref.at[0]}
    starts = {"s": 0, "m": slots, "t": slots + mem}
    sizes = {"s": slots, "m": mem}
    query_ref = q_ref.at[0]
    column = lambda n: pl.ds(pl.multiple_of(n * cols + h * HEAD_DIM, HEAD_DIM), HEAD_DIM)
    done = set()

    def bounds(source, span):
        a, b = (0, sizes[source]) if span is None else span
        return starts[source] + a, starts[source] + b

    def gather(acc, source, span, value):
        a, b = bounds(source, span)
        if (id(acc), a) in done:
            acc[a:b, :] += value
        else:
            done.add((id(acc), a))
            acc[a:b, :] = value

    for spans, pieces, own in tiles(half_p, half_c, branch_ref, group):
        q = rows_of(query_ref, spans)
        do = rows_of(do_ref, spans)
        lse = [lse_ref[0, :, a:b] for a, b in spans]
        lse = lse[0] if len(lse) == 1 else jnp.concatenate(lse, axis=1)
        todo = [(source, span, mask, q, do, lse, None) for source, span, mask in pieces]
        if own is not None:
            for n, span in enumerate(spans):
                cut = slice(n * half_c, (n + 1) * half_c)
                todo.append(("t", span, own, q[cut, :], do[cut, :], lse[:, cut], n))
        kept = []
        row_dot = None
        own_dots = []
        for source, span, mask, qq, dd, ll, n in todo:
            k = key_refs[source][...] if span is None else key_refs[source][span[0]:span[1], :]
            v = value_refs[source][...] if span is None else value_refs[source][span[0]:span[1], :]
            s = dot_nt(k, qq)
            if mask is not None:
                s = jnp.where(mask(s.shape), s, NEGATIVE)
            p = jnp.exp2(s * SCALE2 - ll)
            dp = dot_nt(v, dd)
            part = jnp.sum(p * dp, axis=0, keepdims=True)
            if n is None:
                row_dot = part if row_dot is None else row_dot + part
            else:
                own_dots.append(part)
            kept.append((k, p, dp))
        if own_dots:
            row_dot = row_dot + jnp.concatenate(own_dots, axis=1)
        dq = None
        own_dq = []
        for (source, span, mask, qq, dd, ll, n), (k, p, dp) in zip(todo, kept):
            rd = row_dot if n is None else row_dot[:, n * half_c:(n + 1) * half_c]
            ds = (p * (dp - rd)).astype(BF16)
            gather(kacc, source, span, dot(ds, qq))
            gather(vacc, source, span, dot(p.astype(BF16), dd))
            term = dot_tn(k, ds)
            if n is None:
                dq = term if dq is None else dq + term
            else:
                own_dq.append(term)
        if own_dq:
            dq = dq + jnp.concatenate(own_dq, axis=1)
        dq = (dq * SCALE).T.astype(BF16)
        at = 0
        for a, b in spans:
            dt_ref[a:b, column(0)] = dq[at:at + b - a, :]
            at += b - a
    for source, ref, n, at in (("s", ds_ref, slots, 0), ("m", dm_ref, mem, 0), ("t", dt_ref, 2 * half, 1)):
        a = starts[source]
        ref[:, column(at)] = (kacc[a:a + n, :] * SCALE).astype(BF16)
        ref[:, column(at + 1)] = vacc[a:a + n, :].astype(BF16)

    @pl.when(h == pl.num_programs(0) - 1)
    def _():
        gain = gain_ref[...]
        grad = dot_nt(ds_ref[:, :cols], wk_ref[...]) + dot_nt(ds_ref[:, cols:], wv_ref[...])
        scaled, inv_std = normalize(sq_ref[...].astype(F32))
        wide[...] = norm_pull(grad, gain, scaled, inv_std)
        for ref, n, flip in ((sqkeep_ref, 0, 0), (sqkeep_ref, 1, 2), (sqsend_ref, 0, 1), (sqsend_ref, 1, 3)):
            at = pl.multiple_of((me ^ flip) * cols, cols)
            ref[n] = wide[:, pl.ds(at, cols)].astype(BF16)
        for ref, part in ((send_ref, 1 - core), (keep_ref, core)):
            rows = pl.ds(pl.multiple_of(part * half, half), half)
            grad = (
                dot_nt(dt_ref[rows, :cols], wq_ref[...])
                + dot_nt(dt_ref[rows, cols:2 * cols], wk_ref[...])
                + dot_nt(dt_ref[rows, 2 * cols:], wv_ref[...])
            )
            x = jnp.concatenate(
                [
                    p_ref[0, pl.ds(pl.multiple_of(part * half_p, half_p), half_p), :],
                    c_ref[0, pl.ds(pl.multiple_of(part * half_c, half_c), half_c), :],
                ],
                axis=0,
            ).astype(F32)
            scaled, inv_std = normalize(x)
            ref[...] = norm_pull(grad, gain, scaled, inv_std).astype(BF16)


def attn_back_call(group, place, branch, q, k, v, lse, ga_own, ga_oth, w_out, w_query, w_key, w_value,
                   prompt, cont, squeezed, gain, wait):
    rows, cols = q.shape[1:]
    heads = cols // HEAD_DIM
    half_p, half_c = prompt.shape[1] // 2, cont.shape[1] // 2
    half = half_p + half_c
    width = prompt.shape[2]
    slots, mem = k[0].shape[0], k[1].shape[1]
    n_keys = slots + mem + rows
    flat = pl.BlockSpec((slots, HEAD_DIM), lambda h, *s: (0, h))
    spec = lambda a: pl.BlockSpec((1, a.shape[1], HEAD_DIM), lambda h, *s: (group, 0, h))
    full = lambda *shape: pl.BlockSpec(shape, lambda h, *s: (0,) * len(shape))
    mine = lambda a: pl.BlockSpec((1,) + a.shape[1:], lambda h, *s: (group, 0, 0))
    sds = jax.ShapeDtypeStruct
    return pl.pallas_call(
        functools.partial(attn_back_kernel, group, half_p, half_c),
        name=f"attnback{group}",
        grid_spec=pltpu.PrefetchScalarGridSpec(
            num_scalar_prefetch=2,
            grid=(heads,),
            in_specs=[spec(q), flat, *map(spec, k[1:]), flat, *map(spec, v[1:])]
            + [
                pl.BlockSpec((1, 1, rows), lambda h, *s: (h, 0, 0)),
                full(half, width),
                full(half, width),
                pl.BlockSpec((HEAD_DIM, width), lambda h, *s: (h, 0)),
                full(width, cols),
                full(width, cols),
                full(width, cols),
                mine(prompt),
                mine(cont),
                full(slots, width),
                full(1, width),
                ANY,
            ],
            out_specs=[full(slots, 2 * cols), full(mem, 2 * cols), full(rows, 3 * cols)]
            + [full(half, width)] * 2
            + [full(2, slots, cols)] * 2,
            scratch_shapes=[
                pltpu.VMEM((rows, HEAD_DIM), BF16),
                pltpu.VMEM((n_keys, HEAD_DIM), F32),
                pltpu.VMEM((n_keys, HEAD_DIM), F32),
                pltpu.VMEM((slots, width), F32),
            ],
        ),
        out_shape=[sds((slots, 2 * cols), BF16), sds((mem, 2 * cols), BF16), sds((rows, 3 * cols), BF16)]
        + [sds((half, width), BF16)] * 2
        + [sds((2, slots, cols), BF16)] * 2,
        compiler_params=params(1),
        cost_estimate=cost(
            20 * heads * rows * n_keys * HEAD_DIM + 8 * rows * width * cols,
            8 * n_keys * cols + 12 * rows * width,
            heads * rows * n_keys,
        ),
    )(place, branch, q, *k, *v, lse, ga_own, ga_oth, w_out, w_query, w_key, w_value, prompt, cont,
      squeezed, gain, wait)


def half_specs(group, half_p, half_c, width):
    def part(j, s):
        core = s[0] & 1
        return jnp.where(j == 0, 1 - core, core)

    tok = lambda n: pl.BlockSpec((1, n, width), lambda j, s: (group, part(j, s), 0))
    moving = lambda n: pl.BlockSpec((half_p + half_c, n), lambda j, s: (part(j, s), 0))
    fixed = lambda n: pl.BlockSpec((half_p + half_c, n), lambda j, s: (0, 0))
    full = lambda *shape: pl.BlockSpec(shape, lambda j, s: (0, 0), pipeline_mode=pl.Buffered(1))
    return tok, moving, fixed, full


def ffn_kernel(core_ref, p_ref, c_ref, cp_ref, cc_ref, m0_ref, m2_ref, m1_ref, m3_ref,
               w0_ref, w2_ref, w1_ref, w3_ref, gain_ref, up_ref, down_ref, wait_ref,
               hid_ref, cot_ref, nf_ref, act_ref, pre_ref, gsend_ref, gkeep_ref, fsend_ref, fkeep_ref):
    j = pl.program_id(0)
    gain = gain_ref[...]
    tokens = jnp.concatenate([p_ref[0], c_ref[0]], axis=0).astype(F32)
    cot = jnp.concatenate([cp_ref[0], cc_ref[0]], axis=0)
    attended = (dot(m0_ref[...], w0_ref[...]) + dot(m2_ref[...], w2_ref[...])) + (
        dot(m1_ref[...], w1_ref[...]) + dot(m3_ref[...], w3_ref[...])
    )
    hidden = tokens + attended
    hid_ref[...] = hidden
    cot_ref[...] = cot
    scaled, inv_std = normalize(hidden)
    normed = (scaled * gain).astype(BF16)
    nf_ref[...] = normed
    units = up_ref.shape[1]
    chunk = 256
    for a in range(0, units, chunk):
        cut = slice(a, a + chunk)
        active, slope = gelu_both(dot(normed, up_ref[:, cut]))
        act_ref[:, cut] = active.astype(BF16)
        pre_ref[:, cut] = (dot_nt(cot, down_ref[cut, :]) * slope).astype(BF16)
    grad = dot_nt(pre_ref[...], up_ref[...])
    grad = norm_pull(grad, gain, scaled, inv_std).astype(BF16)
    term = dot(act_ref[...], down_ref[...]).astype(BF16)

    @pl.when(j == 0)
    def _():
        gsend_ref[...] = grad
        fsend_ref[...] = term

    @pl.when(j == 1)
    def _():
        gkeep_ref[...] = grad
        fkeep_ref[...] = term


def ffn_call(group, place, prompt, cont, cot_p, cot_c, mixed, w_out, gain, w_up, w_down, wait):
    half_p, half_c = prompt.shape[1] // 2, cont.shape[1] // 2
    half, width, units = half_p + half_c, prompt.shape[2], w_up.shape[1]
    cols = mixed[0].shape[1]
    tok, moving, fixed, full = half_specs(group, half_p, half_c, width)
    sds = jax.ShapeDtypeStruct
    return pl.pallas_call(
        ffn_kernel,
        name=f"ffn{group}",
        grid_spec=pltpu.PrefetchScalarGridSpec(
            num_scalar_prefetch=1,
            grid=(2,),
            in_specs=[tok(half_p), tok(half_c), tok(half_p), tok(half_c)]
            + [moving(cols)] * 4
            + [full(cols, width)] * 4
            + [full(1, width), full(width, units), full(units, width), ANY],
            out_specs=[fixed(width), fixed(width), moving(width), moving(units), moving(units)]
            + [fixed(width)] * 4,
        ),
        out_shape=[
            sds((half, width), F32),
            sds((half, width), BF16),
            sds((2 * half, width), BF16),
            sds((2 * half, units), BF16),
            sds((2 * half, units), BF16),
        ]
        + [sds((half, width), BF16)] * 4,
        compiler_params=params(1),
        cost_estimate=cost(
            4 * half * width * (4 * units + 4 * cols), 2 * half * (12 * width), 4 * half * units
        ),
    )(place, prompt, cont, cot_p, cot_c, *mixed, *w_out, gain, w_up, w_down, wait)


def up_weights_kernel(groups, *refs):
    nf, pre = refs[:groups], refs[groups:2 * groups]
    up_ref, wait_ref, out_ref, gain_ref = refs[2 * groups:]
    up = None
    for g in range(groups):
        part = dot_tn(nf[g][...], pre[g][...])
        up = part if up is None else up + part
    out_ref[...] = up.astype(BF16)
    gain = jnp.sum(up * up_ref[...].astype(F32), axis=1, keepdims=True)
    gain_ref[...] = jnp.broadcast_to(gain, gain_ref.shape).astype(BF16)


def up_weights_call(nf, pre, w_up, wait):
    groups = len(nf)
    rows, width = nf[0].shape
    units = w_up.shape[1]
    block = min(256, width)
    col = pl.BlockSpec((rows, block), lambda i: (0, i))
    full = pl.BlockSpec((rows, units), lambda i: (0, 0), pipeline_mode=pl.Buffered(1))
    return pl.pallas_call(
        functools.partial(up_weights_kernel, groups),
        name="upweights",
        grid=(width // block,),
        in_specs=[col] * groups + [full] * groups + [pl.BlockSpec((block, units), lambda i: (i, 0)), ANY],
        out_specs=[
            pl.BlockSpec((block, units), lambda i: (i, 0)),
            pl.BlockSpec((block, 128), lambda i: (i, 0)),
        ],
        out_shape=[
            jax.ShapeDtypeStruct((width, 2 * units + 128), BF16),
            jax.ShapeDtypeStruct((width, 128), BF16),
        ],
        compiler_params=params(1),
        cost_estimate=cost(2 * groups * rows * width * units, 6 * groups * rows * width),
    )(*nf, *pre, w_up, wait)


def down_weights_kernel(groups, *refs):
    act = refs[:groups]
    cp_ref, cc_ref, gain_ref, base_ref, wait_ref, out_ref, stage, sem = refs[groups:]
    i = pl.program_id(0)
    half_p, half_c = cp_ref.shape[1] // 2, cc_ref.shape[1] // 2
    down = None
    for g in range(groups):
        cot = jnp.concatenate(
            [cp_ref[g, :half_p], cc_ref[g, :half_c], cp_ref[g, half_p:], cc_ref[g, half_c:]], axis=0
        )
        part = dot_tn(cot, act[g][...])
        down = part if down is None else down + part
    units = down.shape[1]
    block = down.shape[0]
    stage[:, :units] = down.astype(BF16)
    stage[:, units:] = gain_ref[...]
    rows = pl.ds(pl.multiple_of(i * block, block), block)
    copy = pltpu.make_async_copy(stage, out_ref.at[rows, pl.ds(units, units + 128)], sem)
    copy.start()
    copy.wait()


def down_weights_call(act, cot_p, cot_c, gain, base, wait):
    groups = len(act)
    rows, units = act[0].shape
    width = cot_p.shape[2]
    block = min(256, width)
    full = pl.BlockSpec((rows, units), lambda i: (0, 0), pipeline_mode=pl.Buffered(1))
    cot = lambda a: pl.BlockSpec((groups, a.shape[1], block), lambda i: (0, 0, i))
    return pl.pallas_call(
        functools.partial(down_weights_kernel, groups),
        name="downweights",
        grid=(width // block,),
        in_specs=[full] * groups
        + [cot(cot_p), cot(cot_c), pl.BlockSpec((block, 128), lambda i: (i, 0)), ANY, ANY],
        out_specs=ANY,
        out_shape=jax.ShapeDtypeStruct(base.shape, base.dtype),
        scratch_shapes=[pltpu.VMEM((block, units + 128), BF16), pltpu.SemaphoreType.DMA],
        input_output_aliases={groups + 3: 0},
        compiler_params=params(1),
        cost_estimate=cost(2 * groups * rows * width * units, 6 * groups * rows * width),
    )(*act, cot_p, cot_c, gain, base, wait)


def block_of(p, send, order, place_ref):
    first = place_ref[1 + order[0]] ^ send
    return (first << order[0]) + ((p >> 1) << order[1]) + ((p & 1) << order[2])


def attn_weights_kernel(groups, keep_query, half, place_ref, *refs):
    take = iter(refs)
    pair = lambda: (next(take), next(take))
    n_mem, n_tok = pair(), pair()
    n_sq = [pair() for _ in range(groups)]
    grads = [[next(take) for _ in range(3)] for _ in range(groups)]
    w_lead = pair()
    if keep_query:
        w_query = pair()
    else:
        ga = [(pair(), pair()) for _ in range(groups)]
        mixed = [next(take) for _ in range(groups)]
    wait_ref, out_ref = next(take), next(take)
    core = place_ref[0] & 1
    cols = w_lead[0].shape[1]
    join = lambda p, *at: jnp.concatenate([r[at] if at else r[...] for r in p], axis=1)
    down = lambda p: jnp.concatenate([r[...] for r in p], axis=0).astype(F32)
    plus = lambda a, b: b if a is None else a + b
    other = lead = tok = None
    for g in range(groups):
        ds, dm, dt = grads[g]
        lead = plus(lead, dot_tn(join(n_sq[g]), ds[...]))
        lead = plus(lead, dot_tn(join(n_mem, g), dm[...]))
        tok = plus(tok, dot_tn(join(n_tok, g), dt[...]))
        if not keep_query:
            for pair_refs, part in ((ga[g][0], core), (ga[g][1], 1 - core)):
                rows = pl.ds(pl.multiple_of(part * half, half), half)
                other = plus(other, dot_tn(join(pair_refs), mixed[g][rows, :]))
    if keep_query:
        other = tok[:, :cols]
        lead = lead + tok[:, cols:]
        gain = jnp.sum(other * down(w_query) + lead * down(w_lead), axis=1, keepdims=True)
    else:
        lead = lead + tok
        gain = jnp.sum(lead * down(w_lead), axis=1, keepdims=True)
    size = out_ref.shape[2]
    for n in range(2):
        rows = slice(n * size, (n + 1) * size)
        out_ref[0, n, :, :cols] = other[rows].astype(BF16)
        out_ref[0, n, :, cols:2 * cols] = lead[rows].astype(BF16)
        out_ref[0, n, :, 2 * cols:] = jnp.broadcast_to(gain[rows], (size, 128)).astype(BF16)


def attn_weights_call(keep_query, order, place, n_sq, n_mem, n_tok, grads, w_lead, rest, wait):
    groups = len(n_sq)
    width, cols = w_lead.shape
    size = width // 8
    block = lambda n: lambda i, s: block_of(2 * (i & 1) + n, 1 - (i >> 1), order, s)
    lane3 = lambda a, n: pl.BlockSpec((groups, a.shape[1], size), lambda i, s: (0, 0, block(n)(i, s)))
    lane2 = lambda a, n: pl.BlockSpec((a.shape[0], size), lambda i, s: (0, block(n)(i, s)))
    row2 = lambda a, n: pl.BlockSpec((size, cols), lambda i, s: (block(n)(i, s), 0))
    specs, args = [], []

    def twice(make, a):
        for n in range(2):
            specs.append(make(a, n))
            args.append(a)

    def whole(a, width, column):
        specs.append(
            pl.BlockSpec((a.shape[0], width), lambda i, s: (0, column), pipeline_mode=pl.Buffered(1))
        )
        args.append(a)

    twice(lane3, n_mem)
    twice(lane3, n_tok)
    for a in n_sq:
        twice(lane2, a)
    for ds, dm, dt in grads:
        whole(ds, cols, 0 if keep_query else 1)
        whole(dm, cols, 0 if keep_query else 1)
        whole(dt, 2 * cols if keep_query else cols, 0 if keep_query else 2)
    twice(row2, w_lead)
    half = 0
    if keep_query:
        twice(row2, rest)
    else:
        ga, mixed = rest
        half = ga[0][0].shape[0]
        for own, oth in ga:
            twice(lane2, own)
            twice(lane2, oth)
        for a in mixed:
            whole(a, cols, 0)
    rows = n_sq[0].shape[0] + n_mem.shape[1] + 2 * n_tok.shape[1]
    return pl.pallas_call(
        functools.partial(attn_weights_kernel, groups, keep_query, half),
        name="querykey" if keep_query else "outvalue",
        grid_spec=pltpu.PrefetchScalarGridSpec(
            num_scalar_prefetch=1,
            grid=(4,),
            in_specs=specs + [ANY],
            out_specs=pl.BlockSpec((1, 2, size, 2 * cols + 128), lambda i, s: (i >> 1, i & 1, 0, 0)),
        ),
        out_shape=jax.ShapeDtypeStruct((2, 4, size, 2 * cols + 128), BF16),
        compiler_params=params(1),
        cost_estimate=cost(2 * groups * rows * width * cols, 4 * groups * rows * width),
    )(place, *args, wait)


def conv_weights_kernel(place_ref, *refs):
    taps, grad_ref, wait_ref, out_ref = refs[:8], refs[8], refs[9], refs[10]
    groups, slots, cols = grad_ref.shape
    size = out_ref.shape[2]
    grad = grad_ref[...].reshape(groups * slots, cols)
    for part in range(2):
        lanes = [
            jnp.concatenate([taps[4 * part + n][0, g] for g in range(groups)], axis=0) for n in range(4)
        ]
        value = dot_tn(jnp.concatenate(lanes, axis=1), grad).astype(BF16)
        for n in range(4):
            out_ref[part, n] = value[n * size:(n + 1) * size]


def conv_weights_call(order, place, taps, grad, wait):
    rate, groups, slots, width = taps.shape
    cols = grad.shape[2]
    size = width // 8
    lane = lambda part, n: pl.BlockSpec(
        (1, groups, slots, size), lambda t, s: (t, 0, 0, block_of(n, 1 - part, order, s))
    )
    return pl.pallas_call(
        conv_weights_kernel,
        name="convweights",
        grid_spec=pltpu.PrefetchScalarGridSpec(
            num_scalar_prefetch=1,
            grid=(rate,),
            in_specs=[lane(part, n) for part in range(2) for n in range(4)]
            + [pl.BlockSpec((groups, slots, cols), lambda t, s: (0, 0, 0)), ANY],
            out_specs=pl.BlockSpec((2, 4, size, cols), lambda t, s: (0, 0, 0, t)),
        ),
        out_shape=jax.ShapeDtypeStruct((2, 4, size, rate * cols), BF16),
        compiler_params=params(1),
        cost_estimate=cost(2 * rate * groups * slots * width * cols, 8 * rate * width * cols),
    )(place, *([taps] * 8), grad, wait)


def assemble_kernel(group, place_ref, own_ref, oth_ref, wait_ref, *refs):
    p_ref, c_ref = refs[-2:]
    half_p = p_ref.shape[1]
    mine = pl.program_id(0) == (place_ref[0] & 1)
    for ref, hit in ((own_ref, mine), (oth_ref, jnp.logical_not(mine))):

        @pl.when(hit)
        def _(ref=ref):
            p_ref[0] = ref[:half_p]
            c_ref[0] = ref[half_p:]


def assemble_call(group, groups, place, own, oth, half_p, wait, base):
    half, width = own.shape
    full = pl.BlockSpec((half, width), lambda j, s: (0, 0), pipeline_mode=pl.Buffered(1))
    sds = jax.ShapeDtypeStruct
    block = lambda n: pl.BlockSpec((1, n, width), lambda j, s: (group, j, 0))
    base = [] if base is None else list(base)
    return pl.pallas_call(
        functools.partial(assemble_kernel, group),
        name=f"assemble{group}",
        grid_spec=pltpu.PrefetchScalarGridSpec(
            num_scalar_prefetch=1,
            grid=(2,),
            in_specs=[full] * 2 + [ANY] * (1 + len(base)),
            out_specs=[block(half_p), block(half - half_p)],
        ),
        out_shape=[
            sds((groups, 2 * half_p, width), BF16),
            sds((groups, 2 * (half - half_p), width), BF16),
        ],
        input_output_aliases={4: 0, 5: 1} if base else {},
        compiler_params=params(1),
        cost_estimate=cost(0, 8 * half * width),
    )(place, own, oth, wait, *base)


def sum_kernel(a_ref, b_ref, wait_ref, out_ref):
    out_ref[...] = (a_ref[...].astype(F32) + b_ref[...].astype(F32)).astype(BF16)


def sum_call(a, b, wait):
    rows, width = a.shape
    spec = pl.BlockSpec((rows // 2, width), lambda i: (i, 0))
    return pl.pallas_call(
        sum_kernel,
        name="sum",
        grid=(2,),
        in_specs=[spec, spec, ANY],
        out_specs=spec,
        out_shape=jax.ShapeDtypeStruct(a.shape, BF16),
        compiler_params=params(1),
        cost_estimate=cost(rows * width, 6 * rows * width),
    )(a, b, wait)


def swap(x, flip, name, axis="tensor"):
    with jax.named_scope("x_" + name):
        return lax.ppermute(x, axis, [(i, i ^ flip) for i in range(lax.axis_size(axis))])


def tie(*arrays):
    return lax.optimization_barrier(arrays)


def add_low(a, b):
    return (a.astype(F32) + b.astype(F32)).astype(BF16)


class Spread:
    def __init__(self, name, payload, order, low_bits):
        self.name = name
        self.bits = [b + low_bits for b in order] + list(range(low_bits - 1, -1, -1))
        self.me = lax.axis_index("dp")
        size, cols = payload.shape[2:]
        self.send, self.keep = (payload[n].reshape(4 * size, cols) for n in (0, 1))
        self.step = 0

    def start(self):
        bit = self.bits[self.step]
        self.got = swap(self.send, 1 << bit, f"{self.name}{self.step}", "dp")
        return self

    def end(self):
        self.step += 1
        total = self.keep.astype(F32) + self.got.astype(F32)
        if self.step == len(self.bits):
            self.total = total
            return self
        mine = (self.me >> self.bits[self.step]) & 1
        total = total.astype(BF16).reshape(2, total.shape[0] // 2, total.shape[1])
        self.send, self.keep = (
            lax.dynamic_index_in_dim(total, n, 0, keepdims=False) for n in (1 - mine, mine)
        )
        return self

    def rest(self):
        while self.step < len(self.bits):
            self.start().end()
        return self.total


def per_device(prompt, cont, memory, old_memory, branch_at, gain_attn, w_query, w_key, w_value, w_out,
               gain_ffn, w_up, w_down, w_conv, cot_prompt, cot_cont):
    groups, prompt_len, width = prompt.shape
    half_p, half_c = prompt_len // 2, cont.shape[1] // 2
    units, cols = w_up.shape[1], w_query.shape[1]
    me = lax.axis_index("tensor")
    dp = lax.axis_index("dp")
    low_bits = lax.axis_size("dp").bit_length() - 4
    place = jnp.stack([me] + [(dp >> (low_bits + n)) & 1 for n in range(3)]).astype(jnp.int32)
    gain_a = gain_attn.reshape(1, width)
    gain_f = gain_ffn.reshape(1, width)

    sq_own = conv_call(old_memory, w_conv)
    sq_far = swap(sq_own, 2, "sqfar")
    sq_near = swap(sq_own, 1, "sqnear")
    n_mem, k_mem, v_mem, n_tok, q_tok, k_tok, v_tok = qkv_call(
        memory, prompt, cont, gain_a, w_query, w_key, w_value, sq_own
    )
    n_mem, sq_far, w_out = tie(n_mem, sq_far, w_out)
    sq_diag = swap(sq_far, 1, "sqdiag")
    w_far = swap(w_out, 2, "wfar")
    w_near = swap(w_out, 1, "wnear")

    lead, mixed, lse, far = [], [], [], []
    wait = n_mem
    for g in range(groups):
        squeezed, n_sq, k_sq, v_sq, m, l = attn_call(
            g, place, branch_at, (sq_own, sq_far, sq_near, sq_diag), gain_a, w_key, w_value, q_tok,
            (k_mem, k_tok), (v_mem, v_tok), half_p, half_c, wait,
        )
        if g == 0:
            m, w_far = tie(m, w_far)
            w_diag = swap(w_far, 1, "wdiag")
        else:
            m, far[-1] = tie(m, far[-1])
        far.append(swap(m, 2, f"mfar{g}"))
        lead.append((squeezed, n_sq, k_sq, v_sq))
        mixed.append(m)
        lse.append(l)
        wait = m
    w_all = (w_out, w_far, w_near, w_diag)

    def run_ffn(g, wait):
        blocks = (mixed[g], far[g], swap(mixed[g], 1, f"mnear{g}"), swap(far[g], 1, f"mdiag{g}"))
        return list(ffn_call(
            g, place, prompt, cont, cot_prompt, cot_cont, blocks, w_all, gain_f, w_up, w_down, wait
        ))

    def combine(g, chip, other):
        hidden = ffn[g][1].astype(F32) + (chip.astype(F32) + other.astype(F32))
        low = hidden.astype(BF16)
        return hidden, low, swap(low, 1, f"ga{g}")

    def run_back(g, grad, wait):
        squeezed, _, k_sq, v_sq = lead[g]
        return list(attn_back_call(
            g, place, branch_at, q_tok, (k_sq, k_mem, k_tok), (v_sq, v_mem, v_tok), lse[g], grad[1], grad[2],
            w_out, w_query, w_key, w_value, prompt, cont, squeezed, gain_a, wait,
        ))

    last = groups - 1
    ffn, chips, others, grads, back = [], [], [], [], []
    taps = None
    for g in range(groups):
        ffn.append(run_ffn(g, wait))
        if g == 0:
            for n in range(1, groups):
                ffn[0][5], far[n] = tie(ffn[0][5], far[n])
        else:
            ffn[g][5], others[g - 1] = tie(ffn[g][5], others[g - 1])
        got = swap(ffn[g][5], 1, f"gsend{g}")
        if g == 0:
            wait = taps = taps_call(old_memory, ffn[0][5])
        else:
            grads.append(combine(g - 1, chips[g - 1], others[g - 1]))
            wait = grads[g - 1][1]
        wait = sum_call(ffn[g][6], got, wait)
        chips.append(wait)
        others.append(swap(wait, 2, f"gfar{g}"))
    first, gain_part = up_weights_call([f[2] for f in ffn], [f[4] for f in ffn], w_up, wait)
    out_chip = []
    for g in range(groups):
        out_chip.append(sum_call(ffn[g][8], swap(ffn[g][7], 1, f"outsend{g}"), gain_part))
    first = down_weights_call([f[3] for f in ffn], cot_prompt, cot_cont, gain_part, first, out_chip[-1])
    first, others[last] = tie(first, others[last])
    wait = first
    out_far, tok_chip, tok_far = [], [], []
    for g in range(groups):
        if g == 0:
            out_chip[0], wait = tie(out_chip[0], wait)
            out_far.append(swap(out_chip[0], 2, "outfar0"))
        if g == last:
            grads.append(combine(last, chips[last], others[last]))
        back.append(run_back(g, grads[g], wait))
        if g == 0:
            *back[0], out_far[0] = tie(*back[0], out_far[0])
        else:
            *back[g], tok_far[-1] = tie(*back[g], tok_far[-1])
        wait = sum_call(back[g][4], swap(back[g][3], 1, f"toksend{g}"), back[g][0])
        tok_chip.append(wait)
        tok_far.append(swap(wait, 2, f"tokfar{g}"))
    sq_send = jnp.stack([back[g][5] for g in range(groups)])
    sq_keep = jnp.stack([back[g][6] for g in range(groups)])
    chip_sq = add_low(sq_keep, swap(sq_send, 1, "sqsend"))
    sq_back = swap(chip_sq[:, 1], 2, "sqback")

    first = lax.psum_scatter(first, "dp", scatter_dimension=0, tiled=True).astype(F32)
    n_sq = [x[1] for x in lead]
    dqkv = [x[:3] for x in back]
    x_first, z_first = (0, 1, 2), (1, 0, 2)
    query_key = attn_weights_call(True, x_first, place, n_sq, n_mem, n_tok, dqkv, w_key, w_query, wait)
    query_key = Spread("qk", query_key, x_first, low_bits).start()
    out_value = attn_weights_call(
        False, z_first, place, n_sq, n_mem, n_tok, dqkv, w_value, ([x[1:] for x in grads], mixed), query_key.send
    )
    out_value, sq_back = tie(out_value, sq_back)
    wait = out_value
    out_value = Spread("ov", out_value, z_first, low_bits).start()
    grad_sq = add_low(chip_sq[:, 0], sq_back)
    conv = conv_weights_call(z_first, place, taps, grad_sq, wait)
    conv, query_key.got, tok_far[last] = tie(conv, query_key.got, tok_far[last])
    conv_payload = conv
    conv = Spread("conv", conv, z_first, low_bits).start()
    query_key = query_key.end().rest()
    out_value = out_value.end().rest()
    conv = conv.end().rest()

    def finish(name, base, chip, far):
        done = None
        for g in range(groups):
            own = (base[g] + (chip[g].astype(F32) + far[g].astype(F32))).astype(BF16)
            done = assemble_call(g, groups, place, own, swap(own, 1, f"{name}own{g}"), half_p, conv_payload, done)
        return done

    for g in range(1, groups):
        out_chip[g], tok_far[last] = tie(out_chip[g], tok_far[last])
        out_far.append(swap(out_chip[g], 2, f"outfar{g}"))
    grad_tok = finish("tok", [x[0] for x in grads], tok_chip, tok_far)
    out = finish("out", [x[0] for x in ffn], out_chip, out_far)

    rows = width // lax.axis_size("dp")
    gains = jnp.stack([query_key[:, 2 * cols] + out_value[:, 2 * cols], first[:, 2 * units]])
    gains = gains + swap(gains, 1, "gain1")
    gains = gains + swap(gains, 2, "gain2")
    gains = gains / lax.dynamic_slice_in_dim(jnp.stack([gain_attn, gain_ffn]), dp * rows, rows, 1)
    return (
        out[0],
        out[1],
        grad_tok[0],
        grad_tok[1],
        query_key[:, :cols],
        query_key[:, cols:2 * cols],
        out_value[:, cols:2 * cols],
        out_value[:, :cols].T,
        first[:, :units],
        first[:, units:2 * units].T,
        jnp.stack([conv[:, t * cols:(t + 1) * cols] for t in range(RATE)]),
        gains[0],
        gains[1],
    )


def solution(mesh):
    tokens = P("dp", None, None)
    split = P(None, "tensor")
    in_specs = (
        tokens, tokens, tokens, tokens, P("dp", None), P(), split, split, split, P("tensor", None), P(),
        split, P("tensor", None), P(None, None, "tensor"), tokens, tokens,
    )
    both = P("dp", "tensor")
    out_specs = (
        tokens, tokens, tokens, tokens, both, both, both, P("tensor", "dp"), both, P("tensor", "dp"),
        P(None, "dp", "tensor"), P("dp"), P("dp"),
    )
    return jax.shard_map(per_device, mesh=mesh, in_specs=in_specs, out_specs=out_specs, check_vma=False)
```

```python
import functools
import math

import jax
import jax.numpy as jnp
from jax import lax
from jax.experimental import pallas as pl
from jax.experimental.pallas import tpu as pltpu
from jax.sharding import PartitionSpec as P

F32 = jnp.float32
BF16 = jnp.bfloat16
HEAD_DIM = 128
RATE = 3
EPSILON = 1e-05
NEGATIVE = -1e30
SCALE = HEAD_DIM**-0.5
LOG2E = math.log2(math.e)
SCALE2 = SCALE * LOG2E
COST = 0.05
ANY = pl.BlockSpec(memory_space=pl.ANY)
VMEM = pl.BlockSpec(memory_space=pltpu.VMEM)

TAIL_P = 0.3
TAIL = (
    0.11962927179738114,
    0.12075437242074172,
    0.09991089342247686,
    0.12857016178217745,
    -0.0536996295580258,
    0.20637064487815027,
    -0.15721286180378366,
    0.035677073905512405,
)


def dot(a, b):
    return lax.dot_general(a, b, (((1,), (0,)), ((), ())), preferred_element_type=F32)


def dot_nt(a, b):
    return lax.dot_general(a, b, (((1,), (1,)), ((), ())), preferred_element_type=F32)


def dot_tn(a, b):
    return lax.dot_general(a, b, (((0,), (0,)), ((), ())), preferred_element_type=F32)


def params(n, mib=16):
    return pltpu.CompilerParams(dimension_semantics=("arbitrary",) * n, vmem_limit_bytes=mib << 20)


def near(*arrays):
    return [pltpu.with_memory_space_constraint(x, pltpu.VMEM) for x in arrays]


def held(*shape):
    return pltpu.VMEM(shape, BF16)


def at_rows(part, n):
    return pl.ds(pl.multiple_of(part * n, n), n)


def cost(flops, nbytes, trans=0):
    return pl.CostEstimate(
        flops=int(flops * COST), bytes_accessed=int(nbytes * COST), transcendentals=int(trans * COST)
    )


def normalize(values):
    center = values - jnp.mean(values, axis=-1, keepdims=True)
    inv_std = lax.rsqrt(jnp.mean(center * center, axis=-1, keepdims=True) + EPSILON)
    return center * inv_std, inv_std


def norm_pull(grad_outer, gain, scaled, inv_std):
    grad_scaled = grad_outer * gain
    mean_a = jnp.mean(grad_scaled, axis=-1, keepdims=True)
    mean_b = jnp.mean(grad_scaled * scaled, axis=-1, keepdims=True)
    return inv_std * (grad_scaled - mean_a - scaled * mean_b)


def gelu_both(x):
    a = jnp.abs(x)
    t = 1.0 / (1.0 + TAIL_P * a)
    poly = TAIL[7]
    for k in range(6, -1, -1):
        poly = poly * t + TAIL[k]
    bell = jnp.exp2((x * x) * (-0.5 * LOG2E))
    tail = bell * (t * poly)
    cdf = jnp.where(x >= 0.0, 1.0 - tail, tail)
    return x * cdf, cdf + x * (bell * (1.0 / math.sqrt(2.0 * math.pi)))


def tap_rows(old_ref, wide, group):
    lanes = wide.shape[2]
    slots = wide.shape[1] // RATE
    for n in range(wide.shape[0]):
        wide[n] = old_ref[group, :, n * lanes:(n + 1) * lanes].astype(F32)
    return [
        jnp.concatenate(
            [wide[n, pl.ds(t, slots, stride=RATE), :].astype(BF16) for n in range(wide.shape[0])], axis=1
        )
        for t in range(RATE)
    ]


def conv_kernel(place_ref, old_ref, w_ref, out_ref, wide):
    total = None
    for t, rows in enumerate(tap_rows(old_ref, wide, 0)):
        part = dot(rows, w_ref[t])
        total = part if total is None else total + part
    out_ref[pl.program_id(0)] = total.astype(BF16)


def conv_call(place, old, w_conv):
    groups, rows, width = old.shape
    slots = rows // RATE
    cols = w_conv.shape[2]
    return pl.pallas_call(
        conv_kernel,
        name="conv",
        grid_spec=pltpu.PrefetchScalarGridSpec(
            num_scalar_prefetch=1,
            grid=(groups,),
            in_specs=[
                pl.BlockSpec((1, rows, width), lambda g, s: (g, 0, 0)),
                pl.BlockSpec((RATE, width, cols), lambda g, s: (0, 0, 0)),
            ],
            out_specs=VMEM,
            scratch_shapes=[pltpu.VMEM((width // 128, rows, 128), F32)],
        ),
        out_shape=held(groups, slots, cols),
        compiler_params=params(1, 58),
        cost_estimate=cost(2 * groups * rows * width * cols, 2 * groups * rows * width),
    )(place, old, w_conv)


def taps_kernel(old_ref, wait_ref, out_ref, wide):
    for t, rows in enumerate(tap_rows(old_ref, wide, 0)):
        out_ref[t, 0] = rows


def taps_call(old, wait):
    groups, rows, width = old.shape
    slots = rows // RATE
    return pl.pallas_call(
        taps_kernel,
        name="taps",
        grid=(groups,),
        in_specs=[pl.BlockSpec((1, rows, width), lambda g: (g, 0, 0)), ANY],
        out_specs=pl.BlockSpec((RATE, 1, slots, width), lambda g: (0, g, 0, 0)),
        out_shape=jax.ShapeDtypeStruct((RATE, groups, slots, width), BF16),
        scratch_shapes=[pltpu.VMEM((width // 128, rows, 128), F32)],
        compiler_params=params(1),
        cost_estimate=cost(0, 4 * groups * rows * width),
    )(old, wait)


def qkv_kernel(mem_ref, p_ref, c_ref, gain_ref, wq_ref, wk_ref, wv_ref, wait_ref,
               nm_ref, km_ref, vm_ref, nt_ref, qt_ref, kt_ref, vt_ref):
    g, j = pl.program_id(0), pl.program_id(1)
    gain = gain_ref[...]

    @pl.when(j == 0)
    def _():
        scaled, _ = normalize(mem_ref[0].astype(F32))
        normed = (scaled * gain).astype(BF16)
        nm_ref[0] = normed
        km_ref[g] = dot(normed, wk_ref[...]).astype(BF16)
        vm_ref[g] = dot(normed, wv_ref[...]).astype(BF16)

    @pl.when(j > 0)
    def _():
        values = jnp.concatenate([p_ref[0], c_ref[0]], axis=0).astype(F32)
        scaled, _ = normalize(values)
        normed = (scaled * gain).astype(BF16)
        nt_ref[0] = normed
        rows = at_rows(j - 1, normed.shape[0])
        qt_ref[g, rows, :] = dot(normed, wq_ref[...]).astype(BF16)
        kt_ref[g, rows, :] = dot(normed, wk_ref[...]).astype(BF16)
        vt_ref[g, rows, :] = dot(normed, wv_ref[...]).astype(BF16)


def qkv_call(memory, prompt, cont, gain, w_query, w_key, w_value, wait):
    groups, mem, width = memory.shape
    half_p, half_c = prompt.shape[1] // 2, cont.shape[1] // 2
    half = half_p + half_c
    cols = w_query.shape[1]
    lead = lambda g, j: (g, 0, 0)
    later = lambda g, j: (g, jnp.maximum(j - 1, 0), 0)
    sds = jax.ShapeDtypeStruct
    return pl.pallas_call(
        qkv_kernel,
        name="qkv",
        grid=(groups, 3),
        in_specs=[
            pl.BlockSpec((1, mem, width), lead),
            pl.BlockSpec((1, half_p, width), later),
            pl.BlockSpec((1, half_c, width), later),
            pl.BlockSpec((1, width), lambda g, j: (0, 0)),
            VMEM,
            VMEM,
            VMEM,
            ANY,
        ],
        out_specs=[pl.BlockSpec((1, mem, width), lead), VMEM, VMEM, pl.BlockSpec((1, half, width), later)]
        + [VMEM] * 3,
        out_shape=[
            sds((groups, mem, width), BF16),
            held(groups, mem, cols),
            held(groups, mem, cols),
            sds((groups, 2 * half, width), BF16),
            held(groups, 2 * half, cols),
            held(groups, 2 * half, cols),
            held(groups, 2 * half, cols),
        ],
        compiler_params=params(2, 24),
        cost_estimate=cost(
            2 * groups * width * cols * (2 * mem + 6 * half), 8 * groups * (mem + 2 * half) * width
        ),
    )(memory, prompt, cont, gain, *near(w_query, w_key, w_value), wait)


def tiles(half_p, half_c, branch_ref, group):
    half = half_p + half_c

    def causal(shape):
        return lax.broadcasted_iota(jnp.int32, shape, 0) <= lax.broadcasted_iota(jnp.int32, shape, 1)

    def seen(offset):
        def mask(shape):
            key = lax.broadcasted_iota(jnp.int32, shape, 0) + offset
            query = lax.broadcasted_iota(jnp.int32, shape, 1)
            return key < jnp.where(query < half_c, branch_ref[group, 0], branch_ref[group, 1])

        return mask

    first, second = (0, half_p), (half, half + half_p)
    cont0, cont1 = (half_p, half), (half + half_p, 2 * half)
    lead = [("s", None, None), ("m", None, None)]
    return [
        ([first], lead + [("t", first, causal)], None),
        ([second], lead + [("t", first, None), ("t", second, causal)], None),
        ([cont0, cont1], lead + [("t", first, seen(0)), ("t", second, seen(half_p))], causal),
    ]


def rows_of(ref, ranges):
    parts = [ref[a:b, :] for a, b in ranges]
    return parts[0] if len(parts) == 1 else jnp.concatenate(parts, axis=0)


def attn_kernel(group, half_p, half_c, place_ref, branch_ref, own_ref, far_ref, near_ref, diag_ref, gain_ref,
                wk_ref, wv_ref, q_ref, km_ref, kt_ref, vm_ref, vt_ref, wait_ref,
                sq_ref, n_ref, ks_ref, vs_ref, mixed_ref, lse_ref):
    h = pl.program_id(0)
    cols = own_ref.shape[2]
    column = pl.ds(pl.multiple_of(h * HEAD_DIM, HEAD_DIM), HEAD_DIM)

    @pl.when(h == 0)
    def _():
        me = place_ref[0]
        for flip, block in ((0, own_ref), (2, far_ref), (1, near_ref), (3, diag_ref)):
            at = pl.multiple_of((me ^ flip) * cols, cols)
            sq_ref[:, pl.ds(at, cols)] = block[group]
        scaled, _ = normalize(sq_ref[...].astype(F32))
        normed = (scaled * gain_ref[...]).astype(BF16)
        n_ref[...] = normed
        ks_ref[...] = dot(normed, wk_ref[...]).astype(BF16)
        vs_ref[...] = dot(normed, wv_ref[...]).astype(BF16)

    view = lambda ref: ref.at[group, :, column]
    key_refs = {"m": view(km_ref), "t": view(kt_ref)}
    value_refs = {"m": view(vm_ref), "t": view(vt_ref)}
    query_ref = view(q_ref)
    vals = {("s", None): vs_ref[:, column].T, ("m", None): value_refs["m"][...].T}

    def key(source, span):
        if source == "s":
            return ks_ref[:, column]
        return key_refs[source][...] if span is None else key_refs[source][span[0]:span[1], :]

    def value_t(source, span):
        if (source, span) not in vals:
            vals[(source, span)] = value_refs[source][span[0]:span[1], :].T
        return vals[(source, span)]

    for spans, pieces, own in tiles(half_p, half_c, branch_ref, group):
        q = rows_of(query_ref, spans)
        scores = []
        for source, span, mask in pieces:
            s = dot_nt(key(source, span), q)
            if mask is not None:
                s = jnp.where(mask(s.shape), s, NEGATIVE)
            scores.append(s)
        top = functools.reduce(jnp.maximum, [jnp.max(s, axis=0, keepdims=True) for s in scores])
        owns = []
        if own is not None:
            for span in spans:
                s = dot_nt(key_refs["t"][span[0]:span[1], :], query_ref[span[0]:span[1], :])
                owns.append(jnp.where(own(s.shape), s, NEGATIVE))
            top = jnp.maximum(
                top, jnp.concatenate([jnp.max(s, axis=0, keepdims=True) for s in owns], axis=1)
            )
        total = None
        out = None
        for (source, span, mask), s in zip(pieces, scores):
            p = jnp.exp2((s - top) * SCALE2)
            part = jnp.sum(p, axis=0, keepdims=True)
            term = dot(value_t(source, span), p.astype(BF16))
            total = part if total is None else total + part
            out = term if out is None else out + term
        if own is not None:
            width = half_c
            sums, terms = [], []
            for n, (span, s) in enumerate(zip(spans, owns)):
                p = jnp.exp2((s - top[:, n * width:(n + 1) * width]) * SCALE2)
                sums.append(jnp.sum(p, axis=0, keepdims=True))
                terms.append(dot(value_t("t", span), p.astype(BF16)))
            total = total + jnp.concatenate(sums, axis=1)
            out = out + jnp.concatenate(terms, axis=1)
        lse = top * SCALE2 + jnp.log(total) * LOG2E
        out = (out * (1.0 / total)).T.astype(BF16)
        at = 0
        for a, b in spans:
            mixed_ref[a:b, column] = out[at:at + b - a, :]
            lse_ref[h, :, a:b] = lse[:, at:at + b - a]
            at += b - a


def attn_call(group, place, branch, blocks, gain, w_key, w_value, q, k, v, half_p, half_c, wait):
    rows, cols = q.shape[1:]
    heads = cols // HEAD_DIM
    slots = blocks[0].shape[1]
    width = w_key.shape[0]
    keys = sum(a.shape[1] for a in k)
    return pl.pallas_call(
        functools.partial(attn_kernel, group, half_p, half_c),
        name=f"attn{group}",
        grid_spec=pltpu.PrefetchScalarGridSpec(
            num_scalar_prefetch=2,
            grid=(heads,),
            in_specs=[VMEM] * 4 + [pl.BlockSpec((1, width), lambda h, *s: (0, 0))] + [VMEM] * 7 + [ANY],
            out_specs=[VMEM] * 6,
        ),
        out_shape=[
            held(slots, width),
            held(slots, width),
            held(slots, cols),
            held(slots, cols),
            held(rows, cols),
            pltpu.VMEM((heads, 1, rows), F32),
        ],
        compiler_params=params(1, 16),
        cost_estimate=cost(8 * heads * rows * keys * HEAD_DIM, 4 * keys * cols, heads * rows * keys),
    )(place, branch, *near(*blocks), gain, *near(w_key, w_value, q, *k, *v), wait)


def attn_back_kernel(group, half_p, half_c, core_ref, branch_ref, q_ref, ks_ref, km_ref, kt_ref, vs_ref,
                     vm_ref, vt_ref, lse_ref, ga_own_ref, ga_oth_ref, wo_ref, wq_ref, wk_ref, wv_ref,
                     p_ref, c_ref, sq_ref, gain_ref, wait_ref,
                     ds_ref, dm_ref, dt_ref, send_ref, keep_ref, sqsend_ref, sqown_ref, sqfar_ref,
                     do_ref, kacc, vacc, wide):
    h = pl.program_id(0)
    half = half_p + half_c
    cols = wq_ref.shape[1]
    slots, mem = ks_ref.shape[0], km_ref.shape[1]
    me = core_ref[0]
    core = me & 1
    wo = wo_ref[pl.ds(pl.multiple_of(h * HEAD_DIM, HEAD_DIM), HEAD_DIM), :]
    do_ref[pl.ds(pl.multiple_of(core * half, half), half), :] = dot_nt(ga_own_ref[...], wo).astype(BF16)
    do_ref[pl.ds(pl.multiple_of((1 - core) * half, half), half), :] = dot_nt(ga_oth_ref[...], wo).astype(BF16)
    head = pl.ds(pl.multiple_of(h * HEAD_DIM, HEAD_DIM), HEAD_DIM)
    view = lambda ref: ref.at[group, :, head]
    key_refs = {"s": ks_ref.at[:, head], "m": view(km_ref), "t": view(kt_ref)}
    value_refs = {"s": vs_ref.at[:, head], "m": view(vm_ref), "t": view(vt_ref)}
    starts = {"s": 0, "m": slots, "t": slots + mem}
    sizes = {"s": slots, "m": mem}
    query_ref = view(q_ref)
    column = lambda n: pl.ds(pl.multiple_of(n * cols + h * HEAD_DIM, HEAD_DIM), HEAD_DIM)
    done = set()

    def bounds(source, span):
        a, b = (0, sizes[source]) if span is None else span
        return starts[source] + a, starts[source] + b

    def gather(acc, source, span, value):
        a, b = bounds(source, span)
        if (id(acc), a) in done:
            acc[a:b, :] += value
        else:
            done.add((id(acc), a))
            acc[a:b, :] = value

    for spans, pieces, own in tiles(half_p, half_c, branch_ref, group):
        q = rows_of(query_ref, spans)
        do = rows_of(do_ref, spans)
        lse = [lse_ref[h, :, a:b] for a, b in spans]
        lse = lse[0] if len(lse) == 1 else jnp.concatenate(lse, axis=1)
        todo = [(source, span, mask, q, do, lse, None) for source, span, mask in pieces]
        if own is not None:
            for n, span in enumerate(spans):
                cut = slice(n * half_c, (n + 1) * half_c)
                todo.append(("t", span, own, q[cut, :], do[cut, :], lse[:, cut], n))
        kept = []
        row_dot = None
        own_dots = []
        for source, span, mask, qq, dd, ll, n in todo:
            k = key_refs[source][...] if span is None else key_refs[source][span[0]:span[1], :]
            v = value_refs[source][...] if span is None else value_refs[source][span[0]:span[1], :]
            s = dot_nt(k, qq)
            if mask is not None:
                s = jnp.where(mask(s.shape), s, NEGATIVE)
            p = jnp.exp2(s * SCALE2 - ll)
            dp = dot_nt(v, dd)
            part = jnp.sum(p * dp, axis=0, keepdims=True)
            if n is None:
                row_dot = part if row_dot is None else row_dot + part
            else:
                own_dots.append(part)
            kept.append((k, p, dp))
        if own_dots:
            row_dot = row_dot + jnp.concatenate(own_dots, axis=1)
        dq = None
        own_dq = []
        for (source, span, mask, qq, dd, ll, n), (k, p, dp) in zip(todo, kept):
            rd = row_dot if n is None else row_dot[:, n * half_c:(n + 1) * half_c]
            ds = (p * (dp - rd)).astype(BF16)
            gather(kacc, source, span, dot(ds, qq))
            gather(vacc, source, span, dot(p.astype(BF16), dd))
            term = dot_tn(k, ds)
            if n is None:
                dq = term if dq is None else dq + term
            else:
                own_dq.append(term)
        if own_dq:
            dq = dq + jnp.concatenate(own_dq, axis=1)
        dq = (dq * SCALE).T.astype(BF16)
        at = 0
        for a, b in spans:
            dt_ref[a:b, column(0)] = dq[at:at + b - a, :]
            at += b - a
    for source, ref, n, at in (("s", ds_ref, slots, 0), ("m", dm_ref, mem, 0), ("t", dt_ref, 2 * half, 1)):
        a = starts[source]
        ref[:, column(at)] = (kacc[a:a + n, :] * SCALE).astype(BF16)
        ref[:, column(at + 1)] = vacc[a:a + n, :].astype(BF16)

    @pl.when(h == pl.num_programs(0) - 1)
    def _():
        gain = gain_ref[...]
        grad = dot_nt(ds_ref[:, :cols], wk_ref[...]) + dot_nt(ds_ref[:, cols:], wv_ref[...])
        scaled, inv_std = normalize(sq_ref[...].astype(F32))
        wide[...] = norm_pull(grad, gain, scaled, inv_std)
        for ref, flip in ((sqown_ref, 0), (sqfar_ref, 2), (sqsend_ref.at[0], 1), (sqsend_ref.at[1], 3)):
            ref[...] = wide[:, at_rows(me ^ flip, cols)].astype(BF16)
        for ref, part in ((send_ref, 1 - core), (keep_ref, core)):
            rows = pl.ds(pl.multiple_of(part * half, half), half)
            grad = (
                dot_nt(dt_ref[rows, :cols], wq_ref[...])
                + dot_nt(dt_ref[rows, cols:2 * cols], wk_ref[...])
                + dot_nt(dt_ref[rows, 2 * cols:], wv_ref[...])
            )
            x = jnp.concatenate(
                [
                    p_ref[group, at_rows(part, half_p), :],
                    c_ref[group, at_rows(part, half_c), :],
                ],
                axis=0,
            ).astype(F32)
            scaled, inv_std = normalize(x)
            ref[...] = norm_pull(grad, gain, scaled, inv_std).astype(BF16)


def attn_back_call(group, place, branch, q, k, v, lse, ga_own, ga_oth, w_out, w_query, w_key, w_value,
                   prompt, cont, squeezed, gain, wait):
    rows, cols = q.shape[1:]
    heads = cols // HEAD_DIM
    half_p, half_c = prompt.shape[1] // 2, cont.shape[1] // 2
    half = half_p + half_c
    width = prompt.shape[2]
    slots, mem = k[0].shape[0], k[1].shape[1]
    n_keys = slots + mem + rows
    return pl.pallas_call(
        functools.partial(attn_back_kernel, group, half_p, half_c),
        name=f"attnback{group}",
        grid_spec=pltpu.PrefetchScalarGridSpec(
            num_scalar_prefetch=2,
            grid=(heads,),
            in_specs=[VMEM] * 17 + [pl.BlockSpec((1, width), lambda h, *s: (0, 0)), ANY],
            out_specs=[VMEM] * 8,
            scratch_shapes=[
                pltpu.VMEM((rows, HEAD_DIM), BF16),
                pltpu.VMEM((n_keys, HEAD_DIM), F32),
                pltpu.VMEM((n_keys, HEAD_DIM), F32),
                pltpu.VMEM((slots, width), F32),
            ],
        ),
        out_shape=[held(slots, 2 * cols), held(mem, 2 * cols), held(rows, 3 * cols)]
        + [held(half, width)] * 2
        + [held(2, slots, cols)]
        + [held(slots, cols)] * 2,
        compiler_params=params(1, 24),
        cost_estimate=cost(
            20 * heads * rows * n_keys * HEAD_DIM + 8 * rows * width * cols,
            8 * n_keys * cols + 12 * rows * width,
            heads * rows * n_keys,
        ),
    )(place, branch, *near(q, *k, *v, lse, ga_own, ga_oth, w_out, w_query, w_key, w_value, prompt, cont,
                           squeezed), gain, wait)


def ffn_kernel(group, core_ref, p_ref, c_ref, cp_ref, cc_ref, m0_ref, m2_ref, m1_ref, m3_ref,
               w0_ref, w2_ref, w1_ref, w3_ref, gain_ref, up_ref, down_ref, wait_ref,
               nf_ref, act_ref, pre_ref, gsend_ref, gkeep_ref, fsend_ref, fkeep_ref):
    j = pl.program_id(0)
    core = core_ref[0] & 1
    first = (core_ref[0] < 2).astype(F32)
    part = jnp.where(j == 0, 1 - core, core)
    half_p, half_c = p_ref.shape[1] // 2, c_ref.shape[1] // 2
    half = half_p + half_c
    both = lambda p, c: jnp.concatenate(
        [p[group, at_rows(part, half_p), :], c[group, at_rows(part, half_c), :]], axis=0
    )
    rows = at_rows(part, half)
    gain = gain_ref[...]
    cot = both(cp_ref, cc_ref)
    attended = (dot(m0_ref[rows, :], w0_ref[...]) + dot(m2_ref[rows, :], w2_ref[...])) + (
        dot(m1_ref[rows, :], w1_ref[...]) + dot(m3_ref[rows, :], w3_ref[...])
    )
    hidden = both(p_ref, c_ref).astype(F32) + attended
    scaled, inv_std = normalize(hidden)
    normed = (scaled * gain).astype(BF16)
    nf_ref[rows, :] = normed
    units = up_ref.shape[1]
    chunk = 256
    for a in range(0, units, chunk):
        cut = slice(a, a + chunk)
        active, slope = gelu_both(dot(normed, up_ref[:, cut]))
        act_ref[rows, cut] = active.astype(BF16)
        pre_ref[rows, cut] = (dot_nt(cot, down_ref[cut, :]) * slope).astype(BF16)
    grad = dot_nt(pre_ref[rows, :], up_ref[...])
    grad = norm_pull(grad, gain, scaled, inv_std)
    term = dot(act_ref[rows, :], down_ref[...])

    @pl.when(j == 0)
    def _():
        gsend_ref[...] = grad.astype(BF16)
        fsend_ref[...] = term.astype(BF16)

    @pl.when(j == 1)
    def _():
        gkeep_ref[...] = (grad + first * cot.astype(F32)).astype(BF16)
        fkeep_ref[...] = (term + first * hidden).astype(BF16)


def ffn_call(group, place, prompt, cont, cot_p, cot_c, mixed, w_out, gain, w_up, w_down, wait):
    half = (prompt.shape[1] + cont.shape[1]) // 2
    width, units = prompt.shape[2], w_up.shape[1]
    cols = mixed[0].shape[1]
    return pl.pallas_call(
        functools.partial(ffn_kernel, group),
        name=f"ffn{group}",
        grid_spec=pltpu.PrefetchScalarGridSpec(
            num_scalar_prefetch=1,
            grid=(2,),
            in_specs=[VMEM] * 12 + [pl.BlockSpec((1, width), lambda j, s: (0, 0)), VMEM, VMEM, ANY],
            out_specs=[VMEM] * 7,
        ),
        out_shape=[held(2 * half, width), held(2 * half, units), held(2 * half, units)]
        + [held(half, width)] * 4,
        compiler_params=params(1, 16),
        cost_estimate=cost(
            4 * half * width * (4 * units + 4 * cols), 2 * half * (12 * width), 4 * half * units
        ),
    )(place, *near(prompt, cont, cot_p, cot_c, *mixed, *w_out), gain, *near(w_up, w_down), wait)


def block_of(p, send, order, place_ref):
    first = place_ref[1 + order[0]] ^ send
    return (first << order[0]) + ((p >> 1) << order[1]) + ((p & 1) << order[2])


def lanes_of(i, order, place_ref, size):
    return [at_rows(block_of(2 * (i & 1) + n, 1 - (i >> 1), order, place_ref), size) for n in range(2)]


def put(i, outs, columns):
    size = outs[0].shape[1]
    for step in range(4):

        @pl.when(i == step)
        def _(step=step):
            if step > 1:
                ref, base = outs[-1], 2 * (step - 2)
            else:
                ref, base = (outs[step], 0) if len(outs) == 3 else (outs[0], 2 * step)
            for n in range(2):
                at = 0
                for value in columns:
                    width = value.shape[1]
                    ref[base + n, :, at:at + width] = value[n * size:(n + 1) * size].astype(BF16)
                    at += width


def store_gain(ref, lanes, gain):
    for n, rows in enumerate(lanes):
        ref[rows, :] = gain[n * rows.size:(n + 1) * rows.size]


def payload(size, cols, sends):
    return [held(4 // sends, size, cols)] * sends + [held(4, size, cols)]


def up_weights_kernel(groups, order, place_ref, *refs):
    nf, pre = refs[:groups], refs[groups:2 * groups]
    up_refs, gain_refs = refs[2 * groups:2 * groups + 2], refs[2 * groups + 2:2 * groups + 4]
    *outs, partial_ref = refs[2 * groups + 5:]
    i = pl.program_id(0)
    lanes = lanes_of(i, order, place_ref, outs[0].shape[1])
    up = None
    for g in range(groups):
        part = dot_tn(jnp.concatenate([nf[g][:, n] for n in lanes], axis=1), pre[g][...])
        up = part if up is None else up + part
    weight = jnp.concatenate([r[...] for r in up_refs], axis=0).astype(F32)
    gain = jnp.sum(up * weight, axis=1, keepdims=True) / jnp.concatenate([r[...] for r in gain_refs], axis=0)
    put(i, outs, [up])
    store_gain(partial_ref, lanes, gain)


def up_weights_call(order, place, nf, pre, w_up, gain, wait):
    groups = len(nf)
    rows, width = nf[0].shape
    units = w_up.shape[1]
    size = width // 8
    row = lambda n, cols: pl.BlockSpec(
        (size, cols), lambda i, s: (block_of(2 * (i & 1) + n, 1 - (i >> 1), order, s), 0)
    )
    return pl.pallas_call(
        functools.partial(up_weights_kernel, groups, order),
        name="upweights",
        grid_spec=pltpu.PrefetchScalarGridSpec(
            num_scalar_prefetch=1,
            grid=(4,),
            in_specs=[VMEM] * (2 * groups) + [row(n, units) for n in range(2)] + [row(n, 128) for n in range(2)]
            + [ANY],
            out_specs=[VMEM] * 4,
        ),
        out_shape=payload(size, units, 2) + [pltpu.VMEM((width, 128), F32)],
        compiler_params=params(1, 12),
        cost_estimate=cost(2 * groups * rows * width * units, 6 * groups * rows * width),
    )(place, *near(*nf, *pre), w_up, w_up, gain, gain, wait)


def down_weights_kernel(groups, order, place_ref, *refs):
    act = refs[:groups]
    cp_ref, cc_ref, wait_ref, *outs = refs[groups:]
    half_p, half_c = cp_ref.shape[1] // 2, cc_ref.shape[1] // 2
    i = pl.program_id(0)
    lanes = lanes_of(i, order, place_ref, outs[0].shape[1])
    down = None
    for g in range(groups):
        both = [
            jnp.concatenate(
                [cp_ref[g, :half_p, n], cc_ref[g, :half_c, n], cp_ref[g, half_p:, n], cc_ref[g, half_c:, n]], axis=0
            )
            for n in lanes
        ]
        part = dot_tn(jnp.concatenate(both, axis=1), act[g][...])
        down = part if down is None else down + part
    put(i, outs, [down])


def down_weights_call(order, place, act, cot_p, cot_c, wait):
    groups = len(act)
    rows, units = act[0].shape
    width = cot_p.shape[2]
    return pl.pallas_call(
        functools.partial(down_weights_kernel, groups, order),
        name="downweights",
        grid_spec=pltpu.PrefetchScalarGridSpec(
            num_scalar_prefetch=1, grid=(4,), in_specs=[VMEM] * (groups + 2) + [ANY], out_specs=[VMEM] * 3
        ),
        out_shape=payload(width // 8, units, 2),
        compiler_params=params(1, 12),
        cost_estimate=cost(2 * groups * rows * width * units, 6 * groups * rows * width),
    )(place, *near(*act, cot_p, cot_c), wait)


def attn_weights_kernel(groups, keep_query, order, half, place_ref, *refs):
    i = pl.program_id(0)
    take = iter(refs)
    pair = lambda: (next(take), next(take))
    n_mem, n_tok = pair(), pair()
    n_sq = [next(take) for _ in range(groups)]
    grads = [[next(take) for _ in range(3)] for _ in range(groups)]
    w_lead, gain_refs = pair(), pair()
    if keep_query:
        w_query = pair()
    else:
        partials = pair()
        ga = [pair() for _ in range(groups)]
        mixed = [next(take) for _ in range(groups)]
    next(take)
    outs = list(take)
    core = place_ref[0] & 1
    cols = w_lead[0].shape[1]
    join = lambda p, *at: jnp.concatenate([r[at] if at else r[...] for r in p], axis=1)
    down = lambda p: jnp.concatenate([r[...] for r in p], axis=0).astype(F32)
    plus = lambda a, b: b if a is None else a + b
    other = lead = tok = None
    lanes = lanes_of(i, order, place_ref, outs[0].shape[1])
    lead_cut = slice(0, cols) if keep_query else slice(cols, 2 * cols)
    tok_cut = slice(0, 2 * cols) if keep_query else slice(2 * cols, 3 * cols)
    for g in range(groups):
        ds, dm, dt = grads[g]
        lead = plus(lead, dot_tn(jnp.concatenate([n_sq[g][:, n] for n in lanes], axis=1), ds[:, lead_cut]))
        lead = plus(lead, dot_tn(join(n_mem, g), dm[:, lead_cut]))
        tok = plus(tok, dot_tn(join(n_tok, g), dt[:, tok_cut]))
        if not keep_query:
            for ref, part in ((ga[g][0], core), (ga[g][1], 1 - core)):
                grad = jnp.concatenate([ref[:, n] for n in lanes], axis=1)
                other = plus(other, dot_tn(grad, mixed[g][at_rows(part, half), :]))
    if keep_query:
        other = tok[:, :cols]
        lead = lead + tok[:, cols:]
        gain = jnp.sum(other * down(w_query) + lead * down(w_lead), axis=1, keepdims=True)
    else:
        lead = lead + tok
        gain = jnp.sum(lead * down(w_lead), axis=1, keepdims=True)
    gain = gain / jnp.concatenate([r[...] for r in gain_refs], axis=0)
    if keep_query:
        *outs, partial_ref = outs
        put(i, outs, [other, lead])
        store_gain(partial_ref, lanes, gain)
    else:
        attn, ffn = (jnp.concatenate([r[n, :] for n in lanes], axis=0) for r in partials)
        low = lax.broadcasted_iota(jnp.int32, attn.shape, 1) < 64
        put(i, outs, [other, lead, jnp.where(low, attn + gain, ffn)])


def attn_weights_call(keep_query, order, place, n_sq, n_mem, n_tok, grads, w_lead, gain, rest, wait):
    groups = len(n_sq)
    width, cols = w_lead.shape
    size = width // 8
    block = lambda n: lambda i, s: block_of(2 * (i & 1) + n, 1 - (i >> 1), order, s)
    lane3 = lambda a, n: pl.BlockSpec((groups, a.shape[1], size), lambda i, s: (0, 0, block(n)(i, s)))
    row2 = lambda a, n: pl.BlockSpec((size, a.shape[1]), lambda i, s: (block(n)(i, s), 0))
    specs, args = [], []

    def twice(make, a):
        for n in range(2):
            specs.append(make(a, n))
            args.append(a)

    def whole(a):
        specs.append(VMEM)
        args.extend(near(a))

    twice(lane3, n_mem)
    twice(lane3, n_tok)
    for a in n_sq:
        whole(a)
    for ds, dm, dt in grads:
        whole(ds)
        whole(dm)
        whole(dt)
    twice(row2, w_lead)
    twice(row2, gain)
    half = 0
    if keep_query:
        twice(row2, rest)
    else:
        partials, ga, mixed = rest
        for a in partials:
            whole(a)
        half = ga[0][0].shape[0]
        for own, oth in ga:
            whole(own)
            whole(oth)
        for a in mixed:
            whole(a)
    rows = n_sq[0].shape[0] + n_mem.shape[1] + 2 * n_tok.shape[1]
    return pl.pallas_call(
        functools.partial(attn_weights_kernel, groups, keep_query, order, half),
        name="querykey" if keep_query else "outvalue",
        grid_spec=pltpu.PrefetchScalarGridSpec(
            num_scalar_prefetch=1,
            grid=(4,),
            in_specs=specs + [ANY],
            out_specs=[VMEM] * (3 if keep_query else 2),
        ),
        out_shape=payload(size, 2 * cols, 1) + [pltpu.VMEM((width, 128), F32)]
        if keep_query
        else payload(size, 2 * cols + 128, 1),
        compiler_params=params(1, 20),
        cost_estimate=cost(2 * groups * rows * width * cols, 4 * groups * rows * width),
    )(place, *args, wait)


def conv_weights_kernel(groups, place_ref, *refs):
    taps, grads, outs = refs[:8], refs[8:8 + groups], refs[9 + groups:]
    columns = at_rows(pl.program_id(0), grads[0].shape[1])
    size = outs[0].shape[1]
    for part in range(2):
        value = None
        for g in range(groups):
            lanes = jnp.concatenate([taps[4 * part + n][0, g] for n in range(4)], axis=1)
            term = dot_tn(lanes, grads[g][...])
            value = term if value is None else value + term
        for n in range(4):
            outs[part][n, :, columns] = value[n * size:(n + 1) * size].astype(BF16)


def conv_weights_call(order, place, taps, grads, wait):
    rate, groups, slots, width = taps.shape
    cols = grads[0].shape[1]
    size = width // 8
    lane = lambda part, n: pl.BlockSpec(
        (1, groups, slots, size), lambda t, s: (t, 0, 0, block_of(n, 1 - part, order, s))
    )
    return pl.pallas_call(
        functools.partial(conv_weights_kernel, groups),
        name="convweights",
        grid_spec=pltpu.PrefetchScalarGridSpec(
            num_scalar_prefetch=1,
            grid=(rate,),
            in_specs=[lane(part, n) for part in range(2) for n in range(4)] + [VMEM] * groups + [ANY],
            out_specs=[VMEM] * 2,
        ),
        out_shape=payload(size, rate * cols, 1),
        compiler_params=params(1),
        cost_estimate=cost(2 * rate * groups * slots * width * cols, 8 * rate * width * cols),
    )(place, *([taps] * 8), *near(*grads), wait)


def split_kernel(bit, place_ref, keep_ref, *refs):
    got, (send_ref, next_ref) = refs[:-2], refs[-2:]
    mine = place_ref[1 + bit]
    rows = send_ref.shape[0]
    for ref, part in ((send_ref, 1 - mine), (next_ref, mine)):
        at = at_rows(part, rows)
        if len(got) == 1:
            ref[...] = (keep_ref[at, :].astype(F32) + got[0][at, :].astype(F32)).astype(BF16)
        else:
            for n in range(2):

                @pl.when(part == n)
                def _(n=n, ref=ref):
                    half = slice(n * rows, (n + 1) * rows)
                    ref[...] = (keep_ref[half, :].astype(F32) + got[n][...].astype(F32)).astype(BF16)


def split_call(bit, place, keep, got):
    rows, cols = keep.shape
    return pl.pallas_call(
        functools.partial(split_kernel, bit),
        name="split",
        grid_spec=pltpu.PrefetchScalarGridSpec(
            num_scalar_prefetch=1, grid=(1,), in_specs=[VMEM] * (1 + len(got)), out_specs=[VMEM] * 2
        ),
        out_shape=[held(rows // 2, cols)] * 2,
        compiler_params=params(1, 8),
        cost_estimate=cost(rows * cols, 6 * rows * cols),
    )(place, *near(keep, *got))


def finish_kernel(parts, keep_ref, got_ref, wait_ref, *refs):
    at = 0
    for (width, flipped), ref in zip(parts, refs):
        value = keep_ref[:, at:at + width].astype(F32) + got_ref[:, at:at + width].astype(F32)
        if len(ref.shape) == 3:
            cols = ref.shape[2]
            for n in range(ref.shape[0]):
                ref[n] = value[:, n * cols:(n + 1) * cols]
        elif ref.shape[0] == 2:
            ref[...] = jnp.concatenate([value.T[:1, :], value.T[64:65, :]], axis=0)
        else:
            ref[...] = value.T if flipped else value
        at += width


def finish_call(parts, keep, got, wait):
    return pl.pallas_call(
        functools.partial(finish_kernel, [(width, flipped) for width, _, flipped in parts]),
        name="finish",
        in_specs=[VMEM, VMEM, ANY],
        out_specs=[VMEM] * len(parts),
        out_shape=[jax.ShapeDtypeStruct(shape, F32) for _, shape, _ in parts],
        compiler_params=params(0, 8),
        cost_estimate=cost(keep.size, 8 * keep.size),
    )(*near(keep, got), wait)


def assemble_kernel(group, place_ref, own_ref, oth_ref, wait_ref, *refs):
    p_ref, c_ref = refs[-2:]
    half_p = p_ref.shape[1]
    mine = pl.program_id(0) == (place_ref[0] & 1)
    for ref, hit in ((own_ref, mine), (oth_ref, jnp.logical_not(mine))):

        @pl.when(hit)
        def _(ref=ref):
            p_ref[0] = ref[:half_p]
            c_ref[0] = ref[half_p:]


def assemble_call(group, groups, place, own, oth, half_p, wait, base):
    half, width = own.shape
    sds = jax.ShapeDtypeStruct
    block = lambda n: pl.BlockSpec((1, n, width), lambda j, s: (group, j, 0))
    base = [] if base is None else list(base)
    return pl.pallas_call(
        functools.partial(assemble_kernel, group),
        name=f"assemble{group}",
        grid_spec=pltpu.PrefetchScalarGridSpec(
            num_scalar_prefetch=1,
            grid=(2,),
            in_specs=[VMEM] * 2 + [ANY] * (1 + len(base)),
            out_specs=[block(half_p), block(half - half_p)],
        ),
        out_shape=[
            sds((groups, 2 * half_p, width), BF16),
            sds((groups, 2 * (half - half_p), width), BF16),
        ],
        input_output_aliases={4: 0, 5: 1} if base else {},
        compiler_params=params(1),
        cost_estimate=cost(0, 8 * half * width),
    )(place, *near(own, oth), wait, *base)


def swap(x, flip, name, axis="tensor"):
    with jax.named_scope("x_" + name):
        return lax.ppermute(x, axis, [(i, i ^ flip) for i in range(lax.axis_size(axis))])


def tie(*arrays):
    return lax.optimization_barrier(arrays)


class Pieces:
    def __init__(self, name, keep, got, count=2):
        rows = keep.shape[0] // count
        self.name = name
        self.own = [add_low(keep[n * rows:(n + 1) * rows], got[n * rows:(n + 1) * rows]) for n in range(count)]
        self.far = []

    def start(self, count=1):
        for _ in range(count):
            n = len(self.far)
            self.far.append(swap(self.own[n], 2, f"{self.name}{'abcd'[n]}"))
        return self

    def hold(self, n, *others):
        *others, self.far[n] = tie(*others, self.far[n])
        return others

    def total(self, base=None):
        far = jnp.concatenate(self.far, axis=0).astype(F32)
        value = jnp.concatenate(self.own, axis=0).astype(F32) + far
        return (value if base is None else value + base.astype(F32)).astype(BF16)


def add_low(a, b):
    return (a.astype(F32) + b.astype(F32)).astype(BF16)


class Spread:
    def __init__(self, name, payload, order, low_bits, place):
        self.name = name
        self.bits = [b + low_bits for b in order] + list(range(low_bits - 1, -1, -1))
        self.low_bits = low_bits
        self.place = place
        size, cols = payload[-1].shape[1:]
        *self.send, self.keep = (x.reshape(-1, cols) for x in payload)
        self.got = []
        self.step = 0

    def start(self, parts=(0, 1)):
        bit = self.bits[self.step]
        for n in parts[:len(self.send)]:
            name = f"{self.name}{self.step}" + ("ab"[n] if len(self.send) > 1 else "")
            self.got.append(swap(self.send[n], 1 << bit, name, "dp"))
        if len(self.got) == len(self.send):
            self.step += 1
        return self

    def hold(self, *others):
        *rest, = tie(*others, *self.got)
        self.got = rest[len(others):]
        return rest[:len(others)]

    def split(self):
        bit = self.bits[self.step]
        index = bit - self.low_bits if bit >= self.low_bits else 3 + bit
        send, self.keep = split_call(index, self.place, self.keep, self.got)
        self.send, self.got = [send], []
        return self

    def next(self):
        return self if self.step == len(self.bits) else self.split().start()

    def end(self, parts, wait=None):
        while self.step < len(self.bits):
            self.next()
        return finish_call(parts, self.keep, self.got[0], self.keep if wait is None else wait)


def meet(spreads, *others):
    arrays = tie(*others, *[x for s in spreads for x in s.got])
    at = len(others)
    for s in spreads:
        s.got = list(arrays[at:at + len(s.got)])
        at += len(s.got)
    return list(arrays[:len(others)])


def per_device(prompt, cont, memory, old_memory, branch_at, gain_attn, w_query, w_key, w_value, w_out,
               gain_ffn, w_up, w_down, w_conv, cot_prompt, cot_cont):
    groups, prompt_len, width = prompt.shape
    half_p, half_c = prompt_len // 2, cont.shape[1] // 2
    units, cols = w_up.shape[1], w_query.shape[1]
    me = lax.axis_index("tensor")
    dp = lax.axis_index("dp")
    low_bits = lax.axis_size("dp").bit_length() - 4
    place = [me] + [(dp >> (low_bits + n)) & 1 for n in range(3)] + [(dp >> n) & 1 for n in range(low_bits)]
    place = jnp.stack(place).astype(jnp.int32)
    gain_a = gain_attn.reshape(1, width)
    gain_f = gain_ffn.reshape(1, width)
    column_a = jnp.broadcast_to(gain_attn[:, None], (width, 128))
    column_f = jnp.broadcast_to(gain_ffn[:, None], (width, 128))
    x_first, z_first = (0, 1, 2), (1, 0, 2)

    sq_own = conv_call(place, old_memory, w_conv)
    sq_far = swap(sq_own, 2, "sqfar")
    sq_near = swap(sq_own, 1, "sqnear")
    n_mem, k_mem, v_mem, n_tok, q_tok, k_tok, v_tok = qkv_call(
        memory, prompt, cont, gain_a, w_query, w_key, w_value, sq_own
    )
    k_mem, sq_far, w_out = tie(k_mem, sq_far, w_out)
    sq_diag = swap(sq_far, 1, "sqdiag")
    w_far = swap(w_out, 2, "wfar")
    w_near = swap(w_out, 1, "wnear")

    lead, mixed, lse, far = [], [], [], []
    wait = k_mem
    for g in range(groups):
        squeezed, n_sq, k_sq, v_sq, m, l = attn_call(
            g, place, branch_at, (sq_own, sq_far, sq_near, sq_diag), gain_a, w_key, w_value, q_tok,
            (k_mem, k_tok), (v_mem, v_tok), half_p, half_c, wait,
        )
        if g == 0:
            m, w_far = tie(m, w_far)
            w_diag = swap(w_far, 1, "wdiag")
        else:
            m, far[-1] = tie(m, far[-1])
        far.append(swap(m, 2, f"mfar{g}"))
        lead.append((squeezed, n_sq, k_sq, v_sq))
        mixed.append(m)
        lse.append(l)
        wait = m
    w_all = (w_out, w_far, w_near, w_diag)

    def run_ffn(g, wait):
        blocks = (mixed[g], far[g], swap(mixed[g], 1, f"mnear{g}"), swap(far[g], 1, f"mdiag{g}"))
        return list(ffn_call(
            g, place, prompt, cont, cot_prompt, cot_cont, blocks, w_all, gain_f, w_up, w_down, wait
        ))

    def combine(g, chip, other):
        low = add_low(chip, other)
        return low, swap(low, 1, f"ga{g}")

    def run_back(g, grad, wait):
        squeezed, _, k_sq, v_sq = lead[g]
        return list(attn_back_call(
            g, place, branch_at, q_tok, (k_sq, k_mem, k_tok), (v_sq, v_mem, v_tok), lse[g], grad[0], grad[1],
            w_out, w_query, w_key, w_value, prompt, cont, squeezed, gain_a, wait,
        ))

    last = groups - 1
    ffn, chips, others, grads, back = [], [], [], [], []
    for g in range(groups):
        ffn.append(run_ffn(g, wait))
        if g == 0:
            for n in range(1, groups):
                ffn[0][3], far[n] = tie(ffn[0][3], far[n])
        else:
            ffn[g][3], others[g - 1] = tie(ffn[g][3], others[g - 1])
        got = swap(ffn[g][3], 1, f"gsend{g}")
        if g == 0:
            taps = taps_call(old_memory, ffn[0][3])
            taps, got = tie(taps, got)
        else:
            grads.append(combine(g - 1, chips[g - 1], others[g - 1]))
        wait = add_low(ffn[g][4], got)
        chips.append(wait)
        others.append(swap(wait, 2, f"gfar{g}"))
    up = up_weights_call(x_first, place, [f[0] for f in ffn], [f[2] for f in ffn], w_up, column_f, wait)
    out = [
        Pieces(f"out{g}", ffn[g][6], swap(ffn[g][5], 1, f"outsend{g}")) for g in range(groups)
    ]
    down = down_weights_call(z_first, place, [f[1] for f in ffn], cot_prompt, cot_cont, up[2])
    *up, gain_up = up
    up = Spread("up", up, x_first, low_bits, place).start((0,))
    wait = down[2]
    down = Spread("down", down, z_first, low_bits, place).start((0,))
    out[0].own[0], wait = tie(out[0].own[0], wait)
    out[0].start()
    tok, sq_own_grad, sq_back = [], [], []
    for g in range(groups):
        if g == last:
            grads.append(combine(last, chips[last], others[last]))
        back.append(run_back(g, grads[g], wait))
        if g == 0:
            back[g] = down.hold(*up.hold(*out[0].hold(0, *back[g])))
            up.start((1,))
            down.start((1,))
        if g == last - 1:
            *back[g], others[last] = tie(*back[g], others[last])
        if g > 0:
            *back[g], sq_back[-1] = tie(*tok[-1].hold(0, *back[g]), sq_back[-1])
            tok[-1].start()
        if g == last:
            back[g] = down.hold(*up.hold(*back[g]))
            up.next()
            down.next()
        got = swap(back[g][5], 1, f"sqsend{g}")
        sq_own_grad.append(add_low(back[g][6], got[0]))
        sq_back.append(swap(add_low(back[g][7], got[1]), 2, f"sqback{g}"))
        tok.append(Pieces(f"tok{g}", back[g][4], swap(back[g][3], 1, f"toksend{g}")))
        wait = tok[g].own[0]
        if g < last:
            tok[g].start()

    n_sq = [x[1] for x in lead]
    dqkv = [x[:3] for x in back]
    up.send[0], down.send[0], wait = tie(up.send[0], down.send[0], wait)
    query_key = attn_weights_call(
        True, x_first, place, n_sq, n_mem, n_tok, dqkv, w_key, column_a, w_query, wait
    )
    if last > 0:
        query_key = tok[last - 1].hold(1, *query_key)
    *query_key, gain_qk = query_key
    wait = query_key[-1]
    query_key = Spread("qk", query_key, x_first, low_bits, place).start()
    out_value = attn_weights_call(
        False, z_first, place, n_sq, n_mem, n_tok, dqkv, w_value, column_a, ((gain_qk, gain_up), grads, mixed), wait
    )
    *out_value, sq_back[last] = down.hold(*up.hold(*out_value, sq_back[last]))
    out_value = Spread("ov", out_value, z_first, low_bits, place).start()
    up.next()
    down.next()
    tok[last].start()
    conv = conv_weights_call(
        x_first, place, taps, [add_low(a, b) for a, b in zip(sq_own_grad, sq_back)], down.keep
    )
    conv = tok[last].hold(0, *query_key.hold(*conv))
    conv_payload = conv[-1]
    conv = Spread("conv", conv, x_first, low_bits, place).start()
    query_key.next()
    tok[last].start()
    out[0].start()
    tok[last].far[1], out[0].far[1] = meet(
        (query_key, out_value, conv), tok[last].far[1], out[0].far[1]
    )
    for round in range(2):
        query_key.next()
        out_value.next()
        conv.next()
        for g in range(1, groups):
            out[g].own[round], conv.send[0] = tie(out[g].own[round], conv.send[0])
            out[g].start()
        if round == 0:
            others = meet((query_key, out_value, conv, up, down), *[out[g].far[0] for g in range(1, groups)])
            for g in range(1, groups):
                out[g].far[0] = others[g - 1]
    rows = width // lax.axis_size("dp")
    grad_up, = up.end([(units, (rows, units), False)], conv.keep)
    grad_down, = down.end([(units, (units, rows), True)], conv.keep)
    grad_q, grad_k = query_key.end([(cols, (rows, cols), False)] * 2)
    grad_o, grad_v, gains = out_value.end(
        [(cols, (cols, rows), True), (cols, (rows, cols), False), (128, (2, rows), True)]
    )
    grad_conv, = conv.end([(RATE * cols, (RATE, rows, cols), False)])

    def finish(name, pieces, base):
        done = None
        for g in range(groups):
            own = pieces[g].total(base and base[g])
            done = assemble_call(g, groups, place, own, swap(own, 1, f"{name}own{g}"), half_p, conv_payload, done)
        return done

    grad_tok = finish("tok", tok, [x[0] for x in grads])
    out = finish("out", out, None)

    gains = gains + swap(gains, 1, "gain1")
    gains = gains + swap(gains, 2, "gain2")
    return (
        out[0],
        out[1],
        grad_tok[0],
        grad_tok[1],
        grad_q,
        grad_k,
        grad_v,
        grad_o,
        grad_up,
        grad_down,
        grad_conv,
        gains[0],
        gains[1],
    )


def solution(mesh):
    tokens = P("dp", None, None)
    split = P(None, "tensor")
    in_specs = (
        tokens, tokens, tokens, tokens, P("dp", None), P(), split, split, split, P("tensor", None), P(),
        split, P("tensor", None), P(None, None, "tensor"), tokens, tokens,
    )
    both = P("dp", "tensor")
    out_specs = (
        tokens, tokens, tokens, tokens, both, both, both, P("tensor", "dp"), both, P("tensor", "dp"),
        P(None, "dp", "tensor"), P("dp"), P("dp"),
    )
    return jax.shard_map(per_device, mesh=mesh, in_specs=in_specs, out_specs=out_specs, check_vma=False)
```

```python
import functools
import math

import jax
import jax.numpy as jnp
from jax import lax
from jax.experimental import pallas as pl
from jax.experimental.pallas import tpu as pltpu
from jax.sharding import PartitionSpec as P

F32 = jnp.float32
BF16 = jnp.bfloat16
HEAD_DIM = 128
RATE = 3
EPSILON = 1e-05
NEGATIVE = -1e30
SCALE = HEAD_DIM**-0.5
LOG2E = math.log2(math.e)
SCALE2 = SCALE * LOG2E
COST = 0.05
ANY = pl.BlockSpec(memory_space=pl.ANY)
VMEM = pl.BlockSpec(memory_space=pltpu.VMEM)

TAIL_P = 0.3
TAIL = (
    0.11962927179738114,
    0.12075437242074172,
    0.09991089342247686,
    0.12857016178217745,
    -0.0536996295580258,
    0.20637064487815027,
    -0.15721286180378366,
    0.035677073905512405,
)


def dot(a, b):
    return lax.dot_general(a, b, (((1,), (0,)), ((), ())), preferred_element_type=F32)


def dot_nt(a, b):
    return lax.dot_general(a, b, (((1,), (1,)), ((), ())), preferred_element_type=F32)


def dot_tn(a, b):
    return lax.dot_general(a, b, (((0,), (0,)), ((), ())), preferred_element_type=F32)


def params(n, mib=16):
    return pltpu.CompilerParams(dimension_semantics=("arbitrary",) * n, vmem_limit_bytes=mib << 20)


def near(*arrays):
    return [pltpu.with_memory_space_constraint(x, pltpu.VMEM) for x in arrays]


def held(*shape):
    return pltpu.VMEM(shape, BF16)


def at_rows(part, n):
    return pl.ds(pl.multiple_of(part * n, n), n)


def cost(flops, nbytes, trans=0):
    return pl.CostEstimate(
        flops=int(flops * COST), bytes_accessed=int(nbytes * COST), transcendentals=int(trans * COST)
    )


def normalize(values):
    center = values - jnp.mean(values, axis=-1, keepdims=True)
    inv_std = lax.rsqrt(jnp.mean(center * center, axis=-1, keepdims=True) + EPSILON)
    return center * inv_std, inv_std


def norm_pull(grad_outer, gain, scaled, inv_std):
    grad_scaled = grad_outer * gain
    mean_a = jnp.mean(grad_scaled, axis=-1, keepdims=True)
    mean_b = jnp.mean(grad_scaled * scaled, axis=-1, keepdims=True)
    return inv_std * (grad_scaled - mean_a - scaled * mean_b)


def gelu_both(x):
    a = jnp.abs(x)
    t = 1.0 / (1.0 + TAIL_P * a)
    poly = TAIL[7]
    for k in range(6, -1, -1):
        poly = poly * t + TAIL[k]
    bell = jnp.exp2((x * x) * (-0.5 * LOG2E))
    tail = bell * (t * poly)
    cdf = jnp.where(x >= 0.0, 1.0 - tail, tail)
    return x * cdf, cdf + x * (bell * (1.0 / math.sqrt(2.0 * math.pi)))


def tap_rows(old_ref, wide, group):
    lanes = wide.shape[2]
    slots = wide.shape[1] // RATE
    for n in range(wide.shape[0]):
        wide[n] = old_ref[group, :, n * lanes:(n + 1) * lanes].astype(F32)
    return [
        jnp.concatenate(
            [wide[n, pl.ds(t, slots, stride=RATE), :].astype(BF16) for n in range(wide.shape[0])], axis=1
        )
        for t in range(RATE)
    ]


def conv_kernel(place_ref, old_ref, w_ref, out_ref, wide):
    total = None
    for t, rows in enumerate(tap_rows(old_ref, wide, 0)):
        part = dot(rows, w_ref[t])
        total = part if total is None else total + part
    out_ref[pl.program_id(0)] = total.astype(BF16)


def conv_call(place, old, w_conv):
    groups, rows, width = old.shape
    slots = rows // RATE
    cols = w_conv.shape[2]
    return pl.pallas_call(
        conv_kernel,
        name="conv",
        grid_spec=pltpu.PrefetchScalarGridSpec(
            num_scalar_prefetch=1,
            grid=(groups,),
            in_specs=[
                pl.BlockSpec((1, rows, width), lambda g, s: (g, 0, 0)),
                pl.BlockSpec((RATE, width, cols), lambda g, s: (0, 0, 0)),
            ],
            out_specs=VMEM,
            scratch_shapes=[pltpu.VMEM((width // 128, rows, 128), F32)],
        ),
        out_shape=held(groups, slots, cols),
        compiler_params=params(1, 58),
        cost_estimate=cost(2 * groups * rows * width * cols, 2 * groups * rows * width),
    )(place, old, w_conv)


def taps_kernel(old_ref, wait_ref, out_ref, wide):
    for t, rows in enumerate(tap_rows(old_ref, wide, 0)):
        out_ref[t, 0] = rows


def taps_call(old, wait):
    groups, rows, width = old.shape
    slots = rows // RATE
    return pl.pallas_call(
        taps_kernel,
        name="taps",
        grid=(groups,),
        in_specs=[pl.BlockSpec((1, rows, width), lambda g: (g, 0, 0)), ANY],
        out_specs=pl.BlockSpec((RATE, 1, slots, width), lambda g: (0, g, 0, 0)),
        out_shape=jax.ShapeDtypeStruct((RATE, groups, slots, width), BF16),
        scratch_shapes=[pltpu.VMEM((width // 128, rows, 128), F32)],
        compiler_params=params(1),
        cost_estimate=cost(0, 4 * groups * rows * width),
    )(old, wait)


def qkv_kernel(mem_ref, p_ref, c_ref, gain_ref, wq_ref, wk_ref, wv_ref, wait_ref,
               nm_ref, km_ref, vm_ref, nt_ref, qt_ref, kt_ref, vt_ref):
    g, j = pl.program_id(0), pl.program_id(1)
    gain = gain_ref[...]

    @pl.when(j == 0)
    def _():
        scaled, _ = normalize(mem_ref[0].astype(F32))
        normed = (scaled * gain).astype(BF16)
        nm_ref[0] = normed
        km_ref[g] = dot(normed, wk_ref[...]).astype(BF16)
        vm_ref[g] = dot(normed, wv_ref[...]).astype(BF16)

    @pl.when(j > 0)
    def _():
        values = jnp.concatenate([p_ref[0], c_ref[0]], axis=0).astype(F32)
        scaled, _ = normalize(values)
        normed = (scaled * gain).astype(BF16)
        nt_ref[0] = normed
        rows = at_rows(j - 1, normed.shape[0])
        qt_ref[g, rows, :] = dot(normed, wq_ref[...]).astype(BF16)
        kt_ref[g, rows, :] = dot(normed, wk_ref[...]).astype(BF16)
        vt_ref[g, rows, :] = dot(normed, wv_ref[...]).astype(BF16)


def qkv_call(memory, prompt, cont, gain, w_query, w_key, w_value, wait):
    groups, mem, width = memory.shape
    half_p, half_c = prompt.shape[1] // 2, cont.shape[1] // 2
    half = half_p + half_c
    cols = w_query.shape[1]
    lead = lambda g, j: (g, 0, 0)
    later = lambda g, j: (g, jnp.maximum(j - 1, 0), 0)
    sds = jax.ShapeDtypeStruct
    return pl.pallas_call(
        qkv_kernel,
        name="qkv",
        grid=(groups, 3),
        in_specs=[
            pl.BlockSpec((1, mem, width), lead),
            pl.BlockSpec((1, half_p, width), later),
            pl.BlockSpec((1, half_c, width), later),
            pl.BlockSpec((1, width), lambda g, j: (0, 0)),
            VMEM,
            VMEM,
            VMEM,
            ANY,
        ],
        out_specs=[pl.BlockSpec((1, mem, width), lead), VMEM, VMEM, pl.BlockSpec((1, half, width), later)]
        + [VMEM] * 3,
        out_shape=[
            sds((groups, mem, width), BF16),
            held(groups, mem, cols),
            held(groups, mem, cols),
            sds((groups, 2 * half, width), BF16),
            held(groups, 2 * half, cols),
            held(groups, 2 * half, cols),
            held(groups, 2 * half, cols),
        ],
        compiler_params=params(2, 24),
        cost_estimate=cost(
            2 * groups * width * cols * (2 * mem + 6 * half), 8 * groups * (mem + 2 * half) * width
        ),
    )(memory, prompt, cont, gain, *near(w_query, w_key, w_value), wait)


def tiles(half_p, half_c, branch_ref, group):
    half = half_p + half_c

    def causal(shape):
        return lax.broadcasted_iota(jnp.int32, shape, 0) <= lax.broadcasted_iota(jnp.int32, shape, 1)

    def seen(offset):
        def mask(shape):
            key = lax.broadcasted_iota(jnp.int32, shape, 0) + offset
            query = lax.broadcasted_iota(jnp.int32, shape, 1)
            return key < jnp.where(query < half_c, branch_ref[group, 0], branch_ref[group, 1])

        return mask

    first, second = (0, half_p), (half, half + half_p)
    cont0, cont1 = (half_p, half), (half + half_p, 2 * half)
    lead = [("s", None, None), ("m", None, None)]
    return [
        ([first], lead + [("t", first, causal)], None),
        ([second], lead + [("t", first, None), ("t", second, causal)], None),
        ([cont0, cont1], lead + [("t", first, seen(0)), ("t", second, seen(half_p))], causal),
    ]


def rows_of(ref, ranges):
    parts = [ref[a:b, :] for a, b in ranges]
    return parts[0] if len(parts) == 1 else jnp.concatenate(parts, axis=0)


def attn_kernel(group, half_p, half_c, place_ref, branch_ref, own_ref, far_ref, near_ref, diag_ref, gain_ref,
                wk_ref, wv_ref, q_ref, km_ref, kt_ref, vm_ref, vt_ref, wait_ref,
                sq_ref, n_ref, ks_ref, vs_ref, mixed_ref, lse_ref):
    h = pl.program_id(0)
    cols = own_ref.shape[2]
    column = pl.ds(pl.multiple_of(h * HEAD_DIM, HEAD_DIM), HEAD_DIM)

    @pl.when(h == 0)
    def _():
        me = place_ref[0]
        for flip, block in ((0, own_ref), (2, far_ref), (1, near_ref), (3, diag_ref)):
            at = pl.multiple_of((me ^ flip) * cols, cols)
            sq_ref[:, pl.ds(at, cols)] = block[group]
        scaled, _ = normalize(sq_ref[...].astype(F32))
        normed = (scaled * gain_ref[...]).astype(BF16)
        n_ref[...] = normed
        ks_ref[...] = dot(normed, wk_ref[...]).astype(BF16)
        vs_ref[...] = dot(normed, wv_ref[...]).astype(BF16)

    view = lambda ref: ref.at[group, :, column]
    key_refs = {"m": view(km_ref), "t": view(kt_ref)}
    value_refs = {"m": view(vm_ref), "t": view(vt_ref)}
    query_ref = view(q_ref)
    vals = {("s", None): vs_ref[:, column].T, ("m", None): value_refs["m"][...].T}

    def key(source, span):
        if source == "s":
            return ks_ref[:, column]
        return key_refs[source][...] if span is None else key_refs[source][span[0]:span[1], :]

    def value_t(source, span):
        if (source, span) not in vals:
            vals[(source, span)] = value_refs[source][span[0]:span[1], :].T
        return vals[(source, span)]

    for spans, pieces, own in tiles(half_p, half_c, branch_ref, group):
        q = rows_of(query_ref, spans)
        scores = []
        for source, span, mask in pieces:
            s = dot_nt(key(source, span), q)
            if mask is not None:
                s = jnp.where(mask(s.shape), s, NEGATIVE)
            scores.append(s)
        top = functools.reduce(jnp.maximum, [jnp.max(s, axis=0, keepdims=True) for s in scores])
        owns = []
        if own is not None:
            for span in spans:
                s = dot_nt(key_refs["t"][span[0]:span[1], :], query_ref[span[0]:span[1], :])
                owns.append(jnp.where(own(s.shape), s, NEGATIVE))
            top = jnp.maximum(
                top, jnp.concatenate([jnp.max(s, axis=0, keepdims=True) for s in owns], axis=1)
            )
        total = None
        out = None
        for (source, span, mask), s in zip(pieces, scores):
            p = jnp.exp2((s - top) * SCALE2)
            part = jnp.sum(p, axis=0, keepdims=True)
            term = dot(value_t(source, span), p.astype(BF16))
            total = part if total is None else total + part
            out = term if out is None else out + term
        if own is not None:
            width = half_c
            sums, terms = [], []
            for n, (span, s) in enumerate(zip(spans, owns)):
                p = jnp.exp2((s - top[:, n * width:(n + 1) * width]) * SCALE2)
                sums.append(jnp.sum(p, axis=0, keepdims=True))
                terms.append(dot(value_t("t", span), p.astype(BF16)))
            total = total + jnp.concatenate(sums, axis=1)
            out = out + jnp.concatenate(terms, axis=1)
        lse = top * SCALE2 + jnp.log(total) * LOG2E
        out = (out * (1.0 / total)).T.astype(BF16)
        at = 0
        for a, b in spans:
            mixed_ref[a:b, column] = out[at:at + b - a, :]
            lse_ref[h, :, a:b] = lse[:, at:at + b - a]
            at += b - a


def attn_call(group, place, branch, blocks, gain, w_key, w_value, q, k, v, half_p, half_c, wait):
    rows, cols = q.shape[1:]
    heads = cols // HEAD_DIM
    slots = blocks[0].shape[1]
    width = w_key.shape[0]
    keys = sum(a.shape[1] for a in k)
    return pl.pallas_call(
        functools.partial(attn_kernel, group, half_p, half_c),
        name=f"attn{group}",
        grid_spec=pltpu.PrefetchScalarGridSpec(
            num_scalar_prefetch=2,
            grid=(heads,),
            in_specs=[VMEM] * 4 + [pl.BlockSpec((1, width), lambda h, *s: (0, 0))] + [VMEM] * 7 + [ANY],
            out_specs=[pl.BlockSpec((slots, width), lambda h, *s: (0, 0))] * 2 + [VMEM] * 4,
        ),
        out_shape=[
            jax.ShapeDtypeStruct((slots, width), BF16),
            jax.ShapeDtypeStruct((slots, width), BF16),
            held(slots, cols),
            held(slots, cols),
            held(rows, cols),
            pltpu.VMEM((heads, 1, rows), F32),
        ],
        compiler_params=params(1, 16),
        cost_estimate=cost(8 * heads * rows * keys * HEAD_DIM, 4 * keys * cols, heads * rows * keys),
    )(place, branch, *near(*blocks), gain, *near(w_key, w_value, q, *k, *v), wait)


def attn_back_kernel(group, half_p, half_c, core_ref, branch_ref, q_ref, ks_ref, km_ref, kt_ref, vs_ref,
                     vm_ref, vt_ref, lse_ref, ga_own_ref, ga_oth_ref, wo_ref, wq_ref, wk_ref, wv_ref,
                     p_ref, c_ref, sq_ref, gain_ref, wait_ref,
                     ds_ref, dm_ref, dt_ref, send_ref, keep_ref, sqsend_ref, sqown_ref, sqfar_ref,
                     do_ref, kacc, vacc, wide):
    h = pl.program_id(0)
    half = half_p + half_c
    cols = wq_ref.shape[1]
    slots, mem = ks_ref.shape[0], km_ref.shape[1]
    me = core_ref[0]
    core = me & 1
    wo = wo_ref[pl.ds(pl.multiple_of(h * HEAD_DIM, HEAD_DIM), HEAD_DIM), :]
    do_ref[pl.ds(pl.multiple_of(core * half, half), half), :] = dot_nt(ga_own_ref[...], wo).astype(BF16)
    do_ref[pl.ds(pl.multiple_of((1 - core) * half, half), half), :] = dot_nt(ga_oth_ref[...], wo).astype(BF16)
    head = pl.ds(pl.multiple_of(h * HEAD_DIM, HEAD_DIM), HEAD_DIM)
    view = lambda ref: ref.at[group, :, head]
    key_refs = {"s": ks_ref.at[:, head], "m": view(km_ref), "t": view(kt_ref)}
    value_refs = {"s": vs_ref.at[:, head], "m": view(vm_ref), "t": view(vt_ref)}
    starts = {"s": 0, "m": slots, "t": slots + mem}
    sizes = {"s": slots, "m": mem}
    query_ref = view(q_ref)
    column = lambda n: pl.ds(pl.multiple_of(n * cols + h * HEAD_DIM, HEAD_DIM), HEAD_DIM)
    done = set()

    def bounds(source, span):
        a, b = (0, sizes[source]) if span is None else span
        return starts[source] + a, starts[source] + b

    def gather(acc, source, span, value):
        a, b = bounds(source, span)
        if (id(acc), a) in done:
            acc[a:b, :] += value
        else:
            done.add((id(acc), a))
            acc[a:b, :] = value

    for spans, pieces, own in tiles(half_p, half_c, branch_ref, group):
        q = rows_of(query_ref, spans)
        do = rows_of(do_ref, spans)
        lse = [lse_ref[h, :, a:b] for a, b in spans]
        lse = lse[0] if len(lse) == 1 else jnp.concatenate(lse, axis=1)
        todo = [(source, span, mask, q, do, lse, None) for source, span, mask in pieces]
        if own is not None:
            for n, span in enumerate(spans):
                cut = slice(n * half_c, (n + 1) * half_c)
                todo.append(("t", span, own, q[cut, :], do[cut, :], lse[:, cut], n))
        kept = []
        row_dot = None
        own_dots = []
        for source, span, mask, qq, dd, ll, n in todo:
            k = key_refs[source][...] if span is None else key_refs[source][span[0]:span[1], :]
            v = value_refs[source][...] if span is None else value_refs[source][span[0]:span[1], :]
            s = dot_nt(k, qq)
            if mask is not None:
                s = jnp.where(mask(s.shape), s, NEGATIVE)
            p = jnp.exp2(s * SCALE2 - ll)
            dp = dot_nt(v, dd)
            part = jnp.sum(p * dp, axis=0, keepdims=True)
            if n is None:
                row_dot = part if row_dot is None else row_dot + part
            else:
                own_dots.append(part)
            kept.append((k, p, dp))
        if own_dots:
            row_dot = row_dot + jnp.concatenate(own_dots, axis=1)
        dq = None
        own_dq = []
        for (source, span, mask, qq, dd, ll, n), (k, p, dp) in zip(todo, kept):
            rd = row_dot if n is None else row_dot[:, n * half_c:(n + 1) * half_c]
            ds = (p * (dp - rd)).astype(BF16)
            gather(kacc, source, span, dot(ds, qq))
            gather(vacc, source, span, dot(p.astype(BF16), dd))
            term = dot_tn(k, ds)
            if n is None:
                dq = term if dq is None else dq + term
            else:
                own_dq.append(term)
        if own_dq:
            dq = dq + jnp.concatenate(own_dq, axis=1)
        dq = (dq * SCALE).T.astype(BF16)
        at = 0
        for a, b in spans:
            dt_ref[a:b, column(0)] = dq[at:at + b - a, :]
            at += b - a
    for source, ref, n, at in (("s", ds_ref, slots, 0), ("m", dm_ref, mem, 0), ("t", dt_ref, 2 * half, 1)):
        a = starts[source]
        ref[:, column(at)] = (kacc[a:a + n, :] * SCALE).astype(BF16)
        ref[:, column(at + 1)] = vacc[a:a + n, :].astype(BF16)

    @pl.when(h == pl.num_programs(0) - 1)
    def _():
        gain = gain_ref[...]
        grad = dot_nt(ds_ref[:, :cols], wk_ref[...]) + dot_nt(ds_ref[:, cols:], wv_ref[...])
        scaled, inv_std = normalize(sq_ref[...].astype(F32))
        wide[...] = norm_pull(grad, gain, scaled, inv_std)
        for ref, flip in ((sqown_ref, 0), (sqfar_ref, 2), (sqsend_ref.at[0], 1), (sqsend_ref.at[1], 3)):
            ref[...] = wide[:, at_rows(me ^ flip, cols)].astype(BF16)
        for ref, part in ((send_ref, 1 - core), (keep_ref, core)):
            rows = pl.ds(pl.multiple_of(part * half, half), half)
            grad = (
                dot_nt(dt_ref[rows, :cols], wq_ref[...])
                + dot_nt(dt_ref[rows, cols:2 * cols], wk_ref[...])
                + dot_nt(dt_ref[rows, 2 * cols:], wv_ref[...])
            )
            x = jnp.concatenate(
                [
                    p_ref[group, at_rows(part, half_p), :],
                    c_ref[group, at_rows(part, half_c), :],
                ],
                axis=0,
            ).astype(F32)
            scaled, inv_std = normalize(x)
            ref[...] = norm_pull(grad, gain, scaled, inv_std).astype(BF16)


def attn_back_call(group, place, branch, q, k, v, lse, ga_own, ga_oth, w_out, w_query, w_key, w_value,
                   prompt, cont, squeezed, gain, wait):
    rows, cols = q.shape[1:]
    heads = cols // HEAD_DIM
    half_p, half_c = prompt.shape[1] // 2, cont.shape[1] // 2
    half = half_p + half_c
    width = prompt.shape[2]
    slots, mem = k[0].shape[0], k[1].shape[1]
    n_keys = slots + mem + rows
    return pl.pallas_call(
        functools.partial(attn_back_kernel, group, half_p, half_c),
        name=f"attnback{group}",
        grid_spec=pltpu.PrefetchScalarGridSpec(
            num_scalar_prefetch=2,
            grid=(heads,),
            in_specs=[VMEM] * 17 + [pl.BlockSpec((1, width), lambda h, *s: (0, 0)), ANY],
            out_specs=[VMEM] * 8,
            scratch_shapes=[
                pltpu.VMEM((rows, HEAD_DIM), BF16),
                pltpu.VMEM((n_keys, HEAD_DIM), F32),
                pltpu.VMEM((n_keys, HEAD_DIM), F32),
                pltpu.VMEM((slots, width), F32),
            ],
        ),
        out_shape=[held(slots, 2 * cols), held(mem, 2 * cols), held(rows, 3 * cols)]
        + [held(half, width)] * 2
        + [held(2, slots, cols)]
        + [held(slots, cols)] * 2,
        compiler_params=params(1, 24),
        cost_estimate=cost(
            20 * heads * rows * n_keys * HEAD_DIM + 8 * rows * width * cols,
            8 * n_keys * cols + 12 * rows * width,
            heads * rows * n_keys,
        ),
    )(place, branch, *near(q, *k, *v, lse, ga_own, ga_oth, w_out, w_query, w_key, w_value, prompt, cont,
                           squeezed), gain, wait)


def ffn_kernel(group, core_ref, p_ref, c_ref, cp_ref, cc_ref, m0_ref, m2_ref, m1_ref, m3_ref,
               w0_ref, w2_ref, w1_ref, w3_ref, gain_ref, up_ref, down_ref, wait_ref,
               nf_ref, act_ref, pre_ref, gsend_ref, gkeep_ref, fsend_ref, fkeep_ref):
    j = pl.program_id(0)
    core = core_ref[0] & 1
    first = (core_ref[0] < 2).astype(F32)
    part = jnp.where(j == 0, 1 - core, core)
    half_p, half_c = p_ref.shape[1] // 2, c_ref.shape[1] // 2
    half = half_p + half_c
    both = lambda p, c: jnp.concatenate(
        [p[group, at_rows(part, half_p), :], c[group, at_rows(part, half_c), :]], axis=0
    )
    rows = at_rows(part, half)
    gain = gain_ref[...]
    cot = both(cp_ref, cc_ref)
    attended = (dot(m0_ref[rows, :], w0_ref[...]) + dot(m2_ref[rows, :], w2_ref[...])) + (
        dot(m1_ref[rows, :], w1_ref[...]) + dot(m3_ref[rows, :], w3_ref[...])
    )
    hidden = both(p_ref, c_ref).astype(F32) + attended
    scaled, inv_std = normalize(hidden)
    normed = (scaled * gain).astype(BF16)
    nf_ref[rows, :] = normed
    units = up_ref.shape[1]
    chunk = 256
    for a in range(0, units, chunk):
        cut = slice(a, a + chunk)
        active, slope = gelu_both(dot(normed, up_ref[:, cut]))
        act_ref[rows, cut] = active.astype(BF16)
        pre_ref[rows, cut] = (dot_nt(cot, down_ref[cut, :]) * slope).astype(BF16)
    grad = dot_nt(pre_ref[rows, :], up_ref[...])
    grad = norm_pull(grad, gain, scaled, inv_std)
    term = dot(act_ref[rows, :], down_ref[...])

    @pl.when(j == 0)
    def _():
        gsend_ref[...] = grad.astype(BF16)
        fsend_ref[...] = term.astype(BF16)

    @pl.when(j == 1)
    def _():
        gkeep_ref[...] = (grad + first * cot.astype(F32)).astype(BF16)
        fkeep_ref[...] = (term + first * hidden).astype(BF16)


def ffn_call(group, place, prompt, cont, cot_p, cot_c, mixed, w_out, gain, w_up, w_down, wait):
    half = (prompt.shape[1] + cont.shape[1]) // 2
    width, units = prompt.shape[2], w_up.shape[1]
    cols = mixed[0].shape[1]
    return pl.pallas_call(
        functools.partial(ffn_kernel, group),
        name=f"ffn{group}",
        grid_spec=pltpu.PrefetchScalarGridSpec(
            num_scalar_prefetch=1,
            grid=(2,),
            in_specs=[VMEM] * 12 + [pl.BlockSpec((1, width), lambda j, s: (0, 0)), VMEM, VMEM, ANY],
            out_specs=[VMEM] * 7,
        ),
        out_shape=[held(2 * half, width), held(2 * half, units), held(2 * half, units)]
        + [held(half, width)] * 4,
        compiler_params=params(1, 16),
        cost_estimate=cost(
            4 * half * width * (4 * units + 4 * cols), 2 * half * (12 * width), 4 * half * units
        ),
    )(place, *near(prompt, cont, cot_p, cot_c, *mixed, *w_out), gain, *near(w_up, w_down), wait)


def block_of(p, send, order, place_ref):
    first = place_ref[1 + order[0]] ^ send
    return (first << order[0]) + ((p >> 1) << order[1]) + ((p & 1) << order[2])


def lanes_of(i, order, place_ref, size):
    return [at_rows(block_of(n, 1 - i, order, place_ref), size) for n in range(4)]


def row_specs(order, *arrays):
    spec = lambda a, n: pl.BlockSpec((a.shape[0] // 8, a.shape[1]), lambda i, s: (block_of(n, 1 - i, order, s), 0))
    return [spec(a, n) for a in arrays for n in range(4)]


def side_by_side(ref, lanes, *at):
    return jnp.concatenate([ref[(*at, slice(None), n)] for n in lanes], axis=1)


def stacked(refs):
    return jnp.concatenate([r[...] for r in refs], axis=0)


def put(i, outs, columns):
    size = outs[0].shape[1]
    for step in range(2):

        @pl.when(i == step)
        def _(step=step):
            for n in range(4):
                ref, row = (outs[-1], n) if step else (outs[n * (len(outs) - 1) // 4], n % outs[0].shape[0])
                at = 0
                for value in columns:
                    width = value.shape[1]
                    ref[row, :, at:at + width] = value[n * size:(n + 1) * size].astype(BF16)
                    at += width


def store_gain(ref, lanes, gain):
    for n, rows in enumerate(lanes):
        ref[rows, :] = gain[n * rows.size:(n + 1) * rows.size]


def payload(size, cols, sends):
    return [held(4 // sends, size, cols)] * sends + [held(4, size, cols)]


def up_weights_kernel(groups, order, place_ref, *refs):
    nf, pre = refs[:groups], refs[groups:2 * groups]
    up_refs, gain_refs = refs[2 * groups:2 * groups + 4], refs[2 * groups + 4:2 * groups + 8]
    *outs, partial_ref = refs[2 * groups + 9:]
    i = pl.program_id(0)
    lanes = lanes_of(i, order, place_ref, outs[0].shape[1])
    up = None
    for g in range(groups):
        part = dot_tn(side_by_side(nf[g], lanes), pre[g][...])
        up = part if up is None else up + part
    gain = jnp.sum(up * stacked(up_refs).astype(F32), axis=1, keepdims=True) / stacked(gain_refs)
    put(i, outs, [up])
    store_gain(partial_ref, lanes, gain)


def up_weights_call(order, place, nf, pre, w_up, gain, wait):
    groups = len(nf)
    rows, width = nf[0].shape
    units = w_up.shape[1]
    size = width // 8
    return pl.pallas_call(
        functools.partial(up_weights_kernel, groups, order),
        name="upweights",
        grid_spec=pltpu.PrefetchScalarGridSpec(
            num_scalar_prefetch=1,
            grid=(2,),
            in_specs=[VMEM] * (2 * groups) + row_specs(order, w_up, gain) + [ANY],
            out_specs=[VMEM] * 4,
        ),
        out_shape=payload(size, units, 2) + [pltpu.VMEM((width, 128), F32)],
        compiler_params=params(1, 14),
        cost_estimate=cost(2 * groups * rows * width * units, 6 * groups * rows * width),
    )(place, *near(*nf, *pre), *([w_up] * 4), *([gain] * 4), wait)


def down_weights_kernel(groups, order, place_ref, *refs):
    act = refs[:groups]
    cp_ref, cc_ref, wait_ref, *outs = refs[groups:]
    half_p, half_c = cp_ref.shape[1] // 2, cc_ref.shape[1] // 2
    i = pl.program_id(0)
    lanes = lanes_of(i, order, place_ref, outs[0].shape[1])
    down = None
    for g in range(groups):
        p, c = side_by_side(cp_ref, lanes, g), side_by_side(cc_ref, lanes, g)
        both = jnp.concatenate([p[:half_p], c[:half_c], p[half_p:], c[half_c:]], axis=0)
        part = dot_tn(both, act[g][...])
        down = part if down is None else down + part
    put(i, outs, [down])


def down_weights_call(order, place, act, cot_p, cot_c, wait):
    groups = len(act)
    rows, units = act[0].shape
    width = cot_p.shape[2]
    return pl.pallas_call(
        functools.partial(down_weights_kernel, groups, order),
        name="downweights",
        grid_spec=pltpu.PrefetchScalarGridSpec(
            num_scalar_prefetch=1, grid=(2,), in_specs=[VMEM] * (groups + 2) + [ANY], out_specs=[VMEM] * 3
        ),
        out_shape=payload(width // 8, units, 2),
        compiler_params=params(1, 14),
        cost_estimate=cost(2 * groups * rows * width * units, 6 * groups * rows * width),
    )(place, *near(*act, cot_p, cot_c), wait)


def attn_weights_kernel(groups, order, place_ref, *refs):
    i = pl.program_id(0)
    take = iter(refs)
    some = lambda n: [next(take) for _ in range(n)]
    n_mem, n_tok = some(4), some(4)
    n_sq = some(groups)
    grads = [some(3) for _ in range(groups)]
    weights, gain_refs = [some(4) for _ in range(3)], some(4)
    partial_ref, _, *outs = take
    cols = weights[0][0].shape[1]
    join = lambda p, g: jnp.concatenate([r[g] for r in p], axis=1)
    plus = lambda a, b: b if a is None else a + b
    lead = tok = None
    lanes = lanes_of(i, order, place_ref, outs[0].shape[1])
    for g in range(groups):
        ds, dm, dt = grads[g]
        lead = plus(lead, dot_tn(side_by_side(n_sq[g], lanes), ds[...]))
        lead = plus(lead, dot_tn(join(n_mem, g), dm[...]))
        tok = plus(tok, dot_tn(join(n_tok, g), dt[...]))
    values = [tok[:, :cols], tok[:, cols:2 * cols] + lead[:, :cols], tok[:, 2 * cols:] + lead[:, cols:]]
    gain = sum(v * stacked(w).astype(F32) for v, w in zip(values, weights))
    gain = jnp.sum(gain, axis=1, keepdims=True) / stacked(gain_refs)
    ffn = jnp.concatenate([partial_ref[n, :] for n in lanes], axis=0)
    low = lax.broadcasted_iota(jnp.int32, ffn.shape, 1) < 64
    put(i, outs, values + [jnp.where(low, gain, ffn)])


def attn_weights_call(order, place, n_sq, n_mem, n_tok, grads, weights, gain, partial, wait):
    groups = len(n_sq)
    width, cols = weights[0].shape
    size = width // 8
    lane3 = lambda a, n: pl.BlockSpec(
        (groups, a.shape[1], size), lambda i, s: (0, 0, block_of(n, 1 - i, order, s))
    )
    specs = [lane3(a, n) for a in (n_mem, n_tok) for n in range(4)]
    whole = near(*n_sq, *[x for group in grads for x in group])
    rows = n_sq[0].shape[0] + n_mem.shape[1] + 2 * n_tok.shape[1]
    return pl.pallas_call(
        functools.partial(attn_weights_kernel, groups, order),
        name="qkvweights",
        grid_spec=pltpu.PrefetchScalarGridSpec(
            num_scalar_prefetch=1,
            grid=(2,),
            in_specs=specs + [VMEM] * len(whole) + row_specs(order, *weights, gain) + [VMEM, ANY],
            out_specs=[VMEM] * 2,
        ),
        out_shape=payload(size, 3 * cols + 128, 1),
        compiler_params=params(1, 24),
        cost_estimate=cost(4 * groups * rows * width * cols, 4 * groups * rows * width),
    )(
        place, *([n_mem] * 4), *([n_tok] * 4), *whole, *[w for w in weights for _ in range(4)], *([gain] * 4),
        *near(partial), wait,
    )


def conv_weights_kernel(groups, half, order, place_ref, *refs):
    i = pl.program_id(0)
    take = iter(refs)
    some = lambda n: [next(take) for _ in range(n)]
    taps, grads = some(4), some(groups)
    ga = [some(2) for _ in range(groups)]
    mixed = some(groups)
    _, *outs = take
    core = place_ref[0] & 1
    lanes = lanes_of(i, order, place_ref, outs[0].shape[1])
    plus = lambda a, b: b if a is None else a + b
    conv = [None] * taps[0].shape[0]
    out = None
    for g in range(groups):
        for t in range(len(conv)):
            rows = jnp.concatenate([r[t, g] for r in taps], axis=1)
            conv[t] = plus(conv[t], dot_tn(rows, grads[g][...]))
        for ref, part in ((ga[g][0], core), (ga[g][1], 1 - core)):
            out = plus(out, dot_tn(side_by_side(ref, lanes), mixed[g][at_rows(part, half), :]))
    put(i, outs, conv + [out])


def conv_weights_call(order, place, taps, grads, ga, mixed, wait):
    rate, groups, slots, width = taps.shape
    cols = grads[0].shape[1]
    size = width // 8
    half = ga[0][0].shape[0]
    lane = lambda n: pl.BlockSpec(
        (rate, groups, slots, size), lambda i, s: (0, 0, 0, block_of(n, 1 - i, order, s))
    )
    whole = near(*grads, *[x for pair in ga for x in pair], *mixed)
    return pl.pallas_call(
        functools.partial(conv_weights_kernel, groups, half, order),
        name="convweights",
        grid_spec=pltpu.PrefetchScalarGridSpec(
            num_scalar_prefetch=1,
            grid=(2,),
            in_specs=[lane(n) for n in range(4)] + [VMEM] * len(whole) + [ANY],
            out_specs=[VMEM] * 2,
        ),
        out_shape=payload(size, (rate + 1) * cols, 1),
        compiler_params=params(1, 24),
        cost_estimate=cost(2 * rate * groups * slots * width * cols, 8 * rate * width * cols),
    )(place, *([taps] * 4), *whole, wait)


def split_kernel(bit, place_ref, keep_ref, *refs):
    got, (send_ref, next_ref) = refs[:-3], refs[-2:]
    mine = place_ref[1 + bit]
    rows = send_ref.shape[0]
    for ref, part in ((send_ref, 1 - mine), (next_ref, mine)):
        at = at_rows(part, rows)
        if len(got) == 1:
            ref[...] = (keep_ref[at, :].astype(F32) + got[0][at, :].astype(F32)).astype(BF16)
        else:
            for n in range(2):

                @pl.when(part == n)
                def _(n=n, ref=ref):
                    half = slice(n * rows, (n + 1) * rows)
                    ref[...] = (keep_ref[half, :].astype(F32) + got[n][...].astype(F32)).astype(BF16)


def split_call(bit, place, keep, got, wait):
    rows, cols = keep.shape
    return pl.pallas_call(
        functools.partial(split_kernel, bit),
        name="split",
        grid_spec=pltpu.PrefetchScalarGridSpec(
            num_scalar_prefetch=1, grid=(1,), in_specs=[VMEM] * (1 + len(got)) + [ANY], out_specs=[VMEM] * 2
        ),
        out_shape=[held(rows // 2, cols)] * 2,
        compiler_params=params(1, 8),
        cost_estimate=cost(rows * cols, 6 * rows * cols),
    )(place, *near(keep, *got), wait)


def pause_kernel(*refs):
    refs[-1][...] = jnp.zeros(refs[-1].shape, F32)


def pause_call(arrays):
    return pl.pallas_call(
        pause_kernel,
        name="pause",
        in_specs=[ANY] * len(arrays),
        out_specs=VMEM,
        out_shape=pltpu.VMEM((8, 128), F32),
        compiler_params=params(0, 1),
        cost_estimate=pl.CostEstimate(flops=10**10, bytes_accessed=10**8, transcendentals=0),
    )(*arrays)


def finish_kernel(parts, keep_ref, got_ref, wait_ref, *refs):
    at = 0
    for (width, flipped), ref in zip(parts, refs):
        value = keep_ref[:, at:at + width].astype(F32) + got_ref[:, at:at + width].astype(F32)
        if len(ref.shape) == 3:
            cols = ref.shape[2]
            for n in range(ref.shape[0]):
                ref[n] = value[:, n * cols:(n + 1) * cols]
        elif ref.shape[0] == 2:
            ref[...] = jnp.concatenate([value.T[:1, :], value.T[64:65, :]], axis=0)
        else:
            ref[...] = value.T if flipped else value
        at += width


def finish_call(parts, keep, got, wait):
    return pl.pallas_call(
        functools.partial(finish_kernel, [(width, flipped) for width, _, flipped in parts]),
        name="finish",
        in_specs=[VMEM, VMEM, ANY],
        out_specs=[VMEM] * len(parts),
        out_shape=[jax.ShapeDtypeStruct(shape, F32) for _, shape, _ in parts],
        compiler_params=params(0, 8),
        cost_estimate=cost(keep.size, 8 * keep.size),
    )(*near(keep, got), wait)


def assemble_kernel(count, place_ref, *refs):
    own, oth = refs[:count], refs[count:2 * count]
    p_ref, c_ref = refs[-2:]
    half_p = p_ref.shape[1]
    mine = pl.program_id(1) == (place_ref[0] & 1)
    for n in range(count):
        for ref, hit in ((own[n], mine), (oth[n], jnp.logical_not(mine))):

            @pl.when(jnp.logical_and(pl.program_id(0) == n, hit))
            def _(ref=ref):
                p_ref[0] = ref[:half_p]
                c_ref[0] = ref[half_p:]


def assemble_call(place, own, oth, half_p, wait):
    half, width = own[0].shape
    groups = len(own)
    sds = jax.ShapeDtypeStruct
    block = lambda n: pl.BlockSpec((1, n, width), lambda i, j, s: (i, j, 0))
    return pl.pallas_call(
        functools.partial(assemble_kernel, groups),
        name="assemble",
        grid_spec=pltpu.PrefetchScalarGridSpec(
            num_scalar_prefetch=1,
            grid=(groups, 2),
            in_specs=[VMEM] * (2 * groups) + [ANY],
            out_specs=[block(half_p), block(half - half_p)],
        ),
        out_shape=[
            sds((groups, 2 * half_p, width), BF16),
            sds((groups, 2 * (half - half_p), width), BF16),
        ],
        compiler_params=params(2),
        cost_estimate=cost(0, 8 * groups * half * width),
    )(place, *near(*own, *oth), wait)


def swap(x, flip, name, axis="tensor"):
    with jax.named_scope("x_" + name):
        return lax.ppermute(x, axis, [(i, i ^ flip) for i in range(lax.axis_size(axis))])


def tie(*arrays):
    return lax.optimization_barrier(arrays)


class Pieces:
    def __init__(self, name, keep, got, count=2):
        rows = keep.shape[0] // count
        self.name = name
        self.own = [add_low(keep[n * rows:(n + 1) * rows], got[n * rows:(n + 1) * rows]) for n in range(count)]
        self.far = []

    def start(self, count=1):
        for _ in range(count):
            n = len(self.far)
            self.far.append(swap(self.own[n], 2, f"{self.name}{'abcd'[n]}"))
        return self

    def hold(self, n, *others):
        *others, self.far[n] = tie(*others, self.far[n])
        return others

    def total(self, base=None):
        far = jnp.concatenate(self.far, axis=0).astype(F32)
        value = jnp.concatenate(self.own, axis=0).astype(F32) + far
        return (value if base is None else value + base.astype(F32)).astype(BF16)


def add_low(a, b):
    return (a.astype(F32) + b.astype(F32)).astype(BF16)


class Spread:
    def __init__(self, name, payload, order, low_bits, place):
        self.name = name
        self.bits = [b + low_bits for b in order] + list(range(low_bits - 1, -1, -1))
        self.low_bits = low_bits
        self.place = place
        size, cols = payload[-1].shape[1:]
        *self.send, self.keep = (x.reshape(-1, cols) for x in payload)
        self.got = []
        self.step = 0

    def start(self, parts=(0, 1)):
        bit = self.bits[self.step]
        for n in parts[:len(self.send)]:
            name = f"{self.name}{self.step}" + ("ab"[n] if len(self.send) > 1 else "")
            self.got.append(swap(self.send[n], 1 << bit, name, "dp"))
        if len(self.got) == len(self.send):
            self.step += 1
        return self

    def hold(self, *others):
        *rest, = tie(*others, *self.got)
        self.got = rest[len(others):]
        return rest[:len(others)]

    def split(self, wait=None):
        bit = self.bits[self.step]
        index = bit - self.low_bits if bit >= self.low_bits else 3 + bit
        send, self.keep = split_call(index, self.place, self.keep, self.got, self.keep if wait is None else wait)
        self.send, self.got = [send], []
        return self

    def next(self):
        return self if self.step == len(self.bits) else self.split().start()

    def end(self, parts, wait=None):
        if not self.got:
            self.start()
        while self.step < len(self.bits):
            self.next()
        return finish_call(parts, self.keep, self.got[0], self.keep if wait is None else wait)


def meet(spreads, *others):
    arrays = tie(*others, *[x for s in spreads for x in s.got])
    at = len(others)
    for s in spreads:
        s.got = list(arrays[at:at + len(s.got)])
        at += len(s.got)
    return list(arrays[:len(others)])


def per_device(prompt, cont, memory, old_memory, branch_at, gain_attn, w_query, w_key, w_value, w_out,
               gain_ffn, w_up, w_down, w_conv, cot_prompt, cot_cont):
    groups, prompt_len, width = prompt.shape
    half_p, half_c = prompt_len // 2, cont.shape[1] // 2
    units, cols = w_up.shape[1], w_query.shape[1]
    me = lax.axis_index("tensor")
    dp = lax.axis_index("dp")
    low_bits = lax.axis_size("dp").bit_length() - 4
    place = [me] + [(dp >> (low_bits + n)) & 1 for n in range(3)] + [(dp >> n) & 1 for n in range(low_bits)]
    place = jnp.stack(place).astype(jnp.int32)
    gain_a = gain_attn.reshape(1, width)
    gain_f = gain_ffn.reshape(1, width)
    column_a = jnp.broadcast_to(gain_attn[:, None], (width, 128))
    column_f = jnp.broadcast_to(gain_ffn[:, None], (width, 128))
    x_first, z_first = (0, 1, 2), (1, 0, 2)

    sq_own = conv_call(place, old_memory, w_conv)
    sq_far = swap(sq_own, 2, "sqfar")
    sq_near = swap(sq_own, 1, "sqnear")
    n_mem, k_mem, v_mem, n_tok, q_tok, k_tok, v_tok = qkv_call(
        memory, prompt, cont, gain_a, w_query, w_key, w_value, sq_own
    )
    k_mem, sq_far, w_out = tie(k_mem, sq_far, w_out)
    sq_diag = swap(sq_far, 1, "sqdiag")
    w_far = swap(w_out, 2, "wfar")
    w_near = swap(w_out, 1, "wnear")

    lead, mixed, lse, far = [], [], [], []
    wait = k_mem
    for g in range(groups):
        squeezed, n_sq, k_sq, v_sq, m, l = attn_call(
            g, place, branch_at, (sq_own, sq_far, sq_near, sq_diag), gain_a, w_key, w_value, q_tok,
            (k_mem, k_tok), (v_mem, v_tok), half_p, half_c, wait,
        )
        if g == 0:
            m, w_far = tie(m, w_far)
            w_diag = swap(w_far, 1, "wdiag")
        else:
            m, far[-1] = tie(m, far[-1])
        far.append(swap(m, 2, f"mfar{g}"))
        lead.append((squeezed, n_sq, k_sq, v_sq))
        mixed.append(m)
        lse.append(l)
        wait = m
    w_all = (w_out, w_far, w_near, w_diag)

    def run_ffn(g, wait):
        blocks = (mixed[g], far[g], swap(mixed[g], 1, f"mnear{g}"), swap(far[g], 1, f"mdiag{g}"))
        return list(ffn_call(
            g, place, prompt, cont, cot_prompt, cot_cont, blocks, w_all, gain_f, w_up, w_down, wait
        ))

    def combine(g, chip, other):
        low = add_low(chip, other)
        return low, swap(low, 1, f"ga{g}")

    def run_back(g, grad, wait):
        squeezed, _, k_sq, v_sq = lead[g]
        return list(attn_back_call(
            g, place, branch_at, q_tok, (k_sq, k_mem, k_tok), (v_sq, v_mem, v_tok), lse[g], grad[0], grad[1],
            w_out, w_query, w_key, w_value, prompt, cont, squeezed, gain_a, wait,
        ))

    last = groups - 1
    ffn, chips, others, grads, back = [], [], [], [], []
    for g in range(groups):
        ffn.append(run_ffn(g, wait))
        if g == 0:
            for n in range(1, groups):
                ffn[0][3], far[n] = tie(ffn[0][3], far[n])
        else:
            ffn[g][3], others[g - 1] = tie(ffn[g][3], others[g - 1])
        got = swap(ffn[g][3], 1, f"gsend{g}")
        if g == 0:
            taps = taps_call(old_memory, ffn[0][3])
            taps, got = tie(taps, got)
        else:
            grads.append(combine(g - 1, chips[g - 1], others[g - 1]))
        wait = add_low(ffn[g][4], got)
        chips.append(wait)
        others.append(swap(wait, 2, f"gfar{g}"))
    up = up_weights_call(x_first, place, [f[0] for f in ffn], [f[2] for f in ffn], w_up, column_f, wait)
    out = [
        Pieces(f"out{g}", ffn[g][6], swap(ffn[g][5], 1, f"outsend{g}"), 2 if g == 0 else 1) for g in range(groups)
    ]
    down = down_weights_call(z_first, place, [f[1] for f in ffn], cot_prompt, cot_cont, up[2])
    *up, gain_up = up
    up = Spread("up", up, x_first, low_bits, place).start((0,))
    wait = down[2]
    down = Spread("down", down, z_first, low_bits, place).start((0,))
    out[0].own[0], wait = tie(out[0].own[0], wait)
    out[0].start()
    tok, sq_own_grad, sq_back = [], [], []
    for g in range(groups):
        if g == last:
            grads.append(combine(last, chips[last], others[last]))
        back.append(run_back(g, grads[g], wait))
        if g == 0:
            back[g] = down.hold(*up.hold(*out[0].hold(0, *back[g])))
            up.start((1,))
            down.start((1,))
        if g == last - 1:
            *back[g], others[last] = tie(*back[g], others[last])
        if g > 0:
            *back[g], sq_back[-1] = tie(*tok[-1].hold(0, *back[g]), sq_back[-1])
            tok[-1].start()
        if g == last:
            back[g] = down.hold(*up.hold(*back[g]))
            up.next()
            down.next()
        got = swap(back[g][5], 1, f"sqsend{g}")
        sq_own_grad.append(add_low(back[g][6], got[0]))
        sq_back.append(swap(add_low(back[g][7], got[1]), 2, f"sqback{g}"))
        tok.append(Pieces(f"tok{g}", back[g][4], swap(back[g][3], 1, f"toksend{g}")))
        wait = tok[g].own[0]
        if g < last:
            tok[g].start()

    n_sq = [x[1] for x in lead]
    dqkv = [x[:3] for x in back]
    up.send[0], down.send[0], wait = tie(up.send[0], down.send[0], wait)
    for g in range(1, groups):
        *out[g].own, wait = tie(*out[g].own, wait)
    qkv = attn_weights_call(
        x_first, place, n_sq, n_mem, n_tok, dqkv, (w_query, w_key, w_value), column_a, gain_up, wait
    )
    *qkv, sq_back[last] = tie(*qkv, sq_back[last])
    if last > 0:
        qkv = tok[last - 1].hold(1, *qkv)
    wait = qkv[-1]
    qkv = Spread("qkv", qkv, x_first, low_bits, place).start()
    tok[last].own[0], wait = tie(tok[last].own[0], wait)
    tok[last].start()
    conv = conv_weights_call(
        z_first, place, taps, [add_low(a, b) for a, b in zip(sq_own_grad, sq_back)], grads, mixed, wait
    )
    conv = down.hold(*up.hold(*conv))
    conv = Spread("conv", conv, z_first, low_bits, place).start()
    for spread in (up, down):
        if spread.step < len(spread.bits):
            spread.split()
    pairs = {}
    for g in range(groups):
        tok[g].base, out[g].base = grads[g][0], None

    def round(starting, waiting, pieces, ready=(), fillers=(), far=()):
        sends = [s for s in starting if s.step < len(s.bits) and not s.got]
        rest = [p.own[len(p.far)] for p in pieces]
        owns = [p.total(p.base) for p in ready]
        message = [jnp.concatenate(rest, axis=0)] if rest else []
        arrays = tie(*[x for s in sends for x in s.send], *message, *owns)
        wait = pause_call(arrays)
        hold = [wait]
        at = 0
        for s in sends:
            s.send = [arrays[at]]
            at += 1
            s.start()
        if message:
            hold.append(swap(arrays[at], 2, "rows"))
            at += 1
        for p, x in zip(ready, arrays[at:]):
            pairs[p.name] = (x, swap(x, 1, p.name + "own"))
        results = []
        for make in fillers:
            results.append(list(make(wait)))
            wait = results[-1][0]
        flat = [x for r in results for x in r]
        others = meet(list(starting) + list(waiting), *hold, *flat, *[p.far[-1] for p in far])
        at = 0
        for p, x in zip(far, others[len(hold) + len(flat):]):
            p.far[-1] = x
        for p, x in zip(pieces, rest):
            p.far.append(others[1][at:at + x.shape[0]])
            at += x.shape[0]
        flat = iter(others[len(hold):])
        return others[0], [[next(flat) for _ in r] for r in results]

    def place_rows(name):
        def make(wait):
            own, oth = zip(*[pairs[f"{name}{g}"] for g in range(groups)])
            return assemble_call(place, own, oth, half_p, wait)

        return make

    rows = width // lax.axis_size("dp")
    pause, _ = round((up,), (qkv, conv), (tok[last], out[0]), far=(tok[last],))
    for spread in (conv, qkv):
        spread.split(pause)
    fillers = [lambda wait: up.end([(units, (rows, units), False)], wait), place_rows("tok")]
    pause, ((grad_up,), grad_tok) = round((conv, qkv, down), (), out[1:], tok, fillers)
    for spread in (conv, qkv):
        spread.split(pause)
    fillers = [lambda wait: down.end([(units, (units, rows), True)], wait), place_rows("out")]
    pause, ((grad_down,), out) = round((conv, qkv), (), (), out, fillers)
    whole = (cols, (rows, cols), False)
    grad_q, grad_k, grad_v, gains = qkv.end([whole, whole, whole, (128, (2, rows), True)])
    grad_conv, grad_o = conv.end([(RATE * cols, (RATE, rows, cols), False), (cols, (cols, rows), True)])
    gains = gains + swap(gains, 1, "gain1")
    gains = gains + swap(gains, 2, "gain2")
    return (
        out[0],
        out[1],
        grad_tok[0],
        grad_tok[1],
        grad_q,
        grad_k,
        grad_v,
        grad_o,
        grad_up,
        grad_down,
        grad_conv,
        gains[0],
        gains[1],
    )


def solution(mesh):
    tokens = P("dp", None, None)
    split = P(None, "tensor")
    in_specs = (
        tokens, tokens, tokens, tokens, P("dp", None), P(), split, split, split, P("tensor", None), P(),
        split, P("tensor", None), P(None, None, "tensor"), tokens, tokens,
    )
    both = P("dp", "tensor")
    out_specs = (
        tokens, tokens, tokens, tokens, both, both, both, P("tensor", "dp"), both, P("tensor", "dp"),
        P(None, "dp", "tensor"), P("dp"), P("dp"),
    )
    return jax.shard_map(per_device, mesh=mesh, in_specs=in_specs, out_specs=out_specs, check_vma=False)
```

```python
import functools
import math

import jax
import jax.numpy as jnp
from jax import lax
from jax.experimental import pallas as pl
from jax.experimental.pallas import tpu as pltpu
from jax.sharding import PartitionSpec as P

F32 = jnp.float32
BF16 = jnp.bfloat16
HEAD_DIM = 128
RATE = 3
EPSILON = 1e-05
NEGATIVE = -1e30
SCALE = HEAD_DIM**-0.5
LOG2E = math.log2(math.e)
SCALE2 = SCALE * LOG2E
COST = 0.05
ANY = pl.BlockSpec(memory_space=pl.ANY)
VMEM = pl.BlockSpec(memory_space=pltpu.VMEM)

TAIL_P = 0.3
TAIL = (
    0.11962927179738114,
    0.12075437242074172,
    0.09991089342247686,
    0.12857016178217745,
    -0.0536996295580258,
    0.20637064487815027,
    -0.15721286180378366,
    0.035677073905512405,
)


def dot(a, b):
    return lax.dot_general(a, b, (((1,), (0,)), ((), ())), preferred_element_type=F32)


def dot_nt(a, b):
    return lax.dot_general(a, b, (((1,), (1,)), ((), ())), preferred_element_type=F32)


def dot_tn(a, b):
    return lax.dot_general(a, b, (((0,), (0,)), ((), ())), preferred_element_type=F32)


def params(n, mib=16):
    return pltpu.CompilerParams(dimension_semantics=("arbitrary",) * n, vmem_limit_bytes=mib << 20)


def near(*arrays):
    return [pltpu.with_memory_space_constraint(x, pltpu.VMEM) for x in arrays]


def held(*shape):
    return pltpu.VMEM(shape, BF16)


def at_rows(part, n):
    return pl.ds(pl.multiple_of(part * n, n), n)


def cost(flops, nbytes, trans=0):
    return pl.CostEstimate(
        flops=int(flops * COST), bytes_accessed=int(nbytes * COST), transcendentals=int(trans * COST)
    )


def normalize(values):
    center = values - jnp.mean(values, axis=-1, keepdims=True)
    inv_std = lax.rsqrt(jnp.mean(center * center, axis=-1, keepdims=True) + EPSILON)
    return center * inv_std, inv_std


def norm_pull(grad_outer, gain, scaled, inv_std):
    grad_scaled = grad_outer * gain
    mean_a = jnp.mean(grad_scaled, axis=-1, keepdims=True)
    mean_b = jnp.mean(grad_scaled * scaled, axis=-1, keepdims=True)
    return inv_std * (grad_scaled - mean_a - scaled * mean_b)


def gelu_both(x):
    a = jnp.abs(x)
    t = 1.0 / (1.0 + TAIL_P * a)
    poly = TAIL[7]
    for k in range(6, -1, -1):
        poly = poly * t + TAIL[k]
    bell = jnp.exp2((x * x) * (-0.5 * LOG2E))
    tail = bell * (t * poly)
    cdf = jnp.where(x >= 0.0, 1.0 - tail, tail)
    return x * cdf, cdf + x * (bell * (1.0 / math.sqrt(2.0 * math.pi)))


def tap_rows(old_ref, wide, group):
    lanes = wide.shape[2]
    slots = wide.shape[1] // RATE
    for n in range(wide.shape[0]):
        wide[n] = old_ref[group, :, n * lanes:(n + 1) * lanes].astype(F32)
    return [
        jnp.concatenate(
            [wide[n, pl.ds(t, slots, stride=RATE), :].astype(BF16) for n in range(wide.shape[0])], axis=1
        )
        for t in range(RATE)
    ]


def conv_kernel(place_ref, old_ref, w_ref, out_ref, wide):
    total = None
    for t, rows in enumerate(tap_rows(old_ref, wide, 0)):
        part = dot(rows, w_ref[t])
        total = part if total is None else total + part
    out_ref[pl.program_id(0)] = total.astype(BF16)


def conv_call(place, old, w_conv):
    groups, rows, width = old.shape
    slots = rows // RATE
    cols = w_conv.shape[2]
    return pl.pallas_call(
        conv_kernel,
        name="conv",
        grid_spec=pltpu.PrefetchScalarGridSpec(
            num_scalar_prefetch=1,
            grid=(groups,),
            in_specs=[
                pl.BlockSpec((1, rows, width), lambda g, s: (g, 0, 0)),
                pl.BlockSpec((RATE, width, cols), lambda g, s: (0, 0, 0)),
            ],
            out_specs=VMEM,
            scratch_shapes=[pltpu.VMEM((width // 128, rows, 128), F32)],
        ),
        out_shape=held(groups, slots, cols),
        compiler_params=params(1, 58),
        cost_estimate=cost(2 * groups * rows * width * cols, 2 * groups * rows * width),
    )(place, old, w_conv)


def taps_kernel(old_ref, wait_ref, out_ref, wide):
    for t, rows in enumerate(tap_rows(old_ref, wide, 0)):
        out_ref[t, 0] = rows


def taps_call(old, wait):
    groups, rows, width = old.shape
    slots = rows // RATE
    return pl.pallas_call(
        taps_kernel,
        name="taps",
        grid=(groups,),
        in_specs=[pl.BlockSpec((1, rows, width), lambda g: (g, 0, 0)), ANY],
        out_specs=pl.BlockSpec((RATE, 1, slots, width), lambda g: (0, g, 0, 0)),
        out_shape=jax.ShapeDtypeStruct((RATE, groups, slots, width), BF16),
        scratch_shapes=[pltpu.VMEM((width // 128, rows, 128), F32)],
        compiler_params=params(1, 12),
        cost_estimate=cost(0, 4 * groups * rows * width),
    )(old, wait)


def qkv_kernel(mem_ref, p_ref, c_ref, gain_ref, wq_ref, wk_ref, wv_ref, wait_ref,
               nm_ref, km_ref, vm_ref, nt_ref, qt_ref, kt_ref, vt_ref):
    g, j = pl.program_id(0), pl.program_id(1)
    gain = gain_ref[...]

    @pl.when(j == 0)
    def _():
        scaled, _ = normalize(mem_ref[0].astype(F32))
        normed = (scaled * gain).astype(BF16)
        nm_ref[0] = normed
        km_ref[g] = dot(normed, wk_ref[...]).astype(BF16)
        vm_ref[g] = dot(normed, wv_ref[...]).astype(BF16)

    @pl.when(j > 0)
    def _():
        values = jnp.concatenate([p_ref[0], c_ref[0]], axis=0).astype(F32)
        scaled, _ = normalize(values)
        normed = (scaled * gain).astype(BF16)
        nt_ref[0] = normed
        rows = at_rows(j - 1, normed.shape[0])
        qt_ref[g, rows, :] = dot(normed, wq_ref[...]).astype(BF16)
        kt_ref[g, rows, :] = dot(normed, wk_ref[...]).astype(BF16)
        vt_ref[g, rows, :] = dot(normed, wv_ref[...]).astype(BF16)


def qkv_call(memory, prompt, cont, gain, w_query, w_key, w_value, wait):
    groups, mem, width = memory.shape
    half_p, half_c = prompt.shape[1] // 2, cont.shape[1] // 2
    half = half_p + half_c
    cols = w_query.shape[1]
    lead = lambda g, j: (g, 0, 0)
    later = lambda g, j: (g, jnp.maximum(j - 1, 0), 0)
    sds = jax.ShapeDtypeStruct
    return pl.pallas_call(
        qkv_kernel,
        name="qkv",
        grid=(groups, 3),
        in_specs=[
            pl.BlockSpec((1, mem, width), lead),
            pl.BlockSpec((1, half_p, width), later),
            pl.BlockSpec((1, half_c, width), later),
            pl.BlockSpec((1, width), lambda g, j: (0, 0)),
            VMEM,
            VMEM,
            VMEM,
            ANY,
        ],
        out_specs=[pl.BlockSpec((1, mem, width), lead), VMEM, VMEM, pl.BlockSpec((1, half, width), later)]
        + [VMEM] * 3,
        out_shape=[
            sds((groups, mem, width), BF16),
            held(groups, mem, cols),
            held(groups, mem, cols),
            sds((groups, 2 * half, width), BF16),
            held(groups, 2 * half, cols),
            held(groups, 2 * half, cols),
            held(groups, 2 * half, cols),
        ],
        compiler_params=params(2, 24),
        cost_estimate=cost(
            2 * groups * width * cols * (2 * mem + 6 * half), 8 * groups * (mem + 2 * half) * width
        ),
    )(memory, prompt, cont, gain, *near(w_query, w_key, w_value), wait)


def tiles(half_p, half_c, branch_ref, group):
    half = half_p + half_c

    def causal(shape):
        return lax.broadcasted_iota(jnp.int32, shape, 0) <= lax.broadcasted_iota(jnp.int32, shape, 1)

    def seen(offset):
        def mask(shape):
            key = lax.broadcasted_iota(jnp.int32, shape, 0) + offset
            query = lax.broadcasted_iota(jnp.int32, shape, 1)
            return key < jnp.where(query < half_c, branch_ref[group, 0], branch_ref[group, 1])

        return mask

    first, second = (0, half_p), (half, half + half_p)
    cont0, cont1 = (half_p, half), (half + half_p, 2 * half)
    lead = [("s", None, None), ("m", None, None)]
    return [
        ([first], lead + [("t", first, causal)], None),
        ([second], lead + [("t", first, None), ("t", second, causal)], None),
        ([cont0, cont1], lead + [("t", first, seen(0)), ("t", second, seen(half_p))], causal),
    ]


def rows_of(ref, ranges):
    parts = [ref[a:b, :] for a, b in ranges]
    return parts[0] if len(parts) == 1 else jnp.concatenate(parts, axis=0)


def attn_kernel(group, half_p, half_c, place_ref, branch_ref, own_ref, far_ref, near_ref, diag_ref, gain_ref,
                wk_ref, wv_ref, q_ref, km_ref, kt_ref, vm_ref, vt_ref, wait_ref,
                sq_ref, n_ref, ks_ref, vs_ref, mixed_ref, lse_ref):
    h = pl.program_id(0)
    cols = own_ref.shape[2]
    column = pl.ds(pl.multiple_of(h * HEAD_DIM, HEAD_DIM), HEAD_DIM)

    @pl.when(h == 0)
    def _():
        me = place_ref[0]
        for flip, block in ((0, own_ref), (2, far_ref), (1, near_ref), (3, diag_ref)):
            at = pl.multiple_of((me ^ flip) * cols, cols)
            sq_ref[:, pl.ds(at, cols)] = block[group]
        scaled, _ = normalize(sq_ref[...].astype(F32))
        normed = (scaled * gain_ref[...]).astype(BF16)
        n_ref[...] = normed
        ks_ref[...] = dot(normed, wk_ref[...]).astype(BF16)
        vs_ref[...] = dot(normed, wv_ref[...]).astype(BF16)

    view = lambda ref: ref.at[group, :, column]
    key_refs = {"m": view(km_ref), "t": view(kt_ref)}
    value_refs = {"m": view(vm_ref), "t": view(vt_ref)}
    query_ref = view(q_ref)
    vals = {("s", None): vs_ref[:, column].T, ("m", None): value_refs["m"][...].T}

    def key(source, span):
        if source == "s":
            return ks_ref[:, column]
        return key_refs[source][...] if span is None else key_refs[source][span[0]:span[1], :]

    def value_t(source, span):
        if (source, span) not in vals:
            vals[(source, span)] = value_refs[source][span[0]:span[1], :].T
        return vals[(source, span)]

    for spans, pieces, own in tiles(half_p, half_c, branch_ref, group):
        q = rows_of(query_ref, spans)
        scores = []
        for source, span, mask in pieces:
            s = dot_nt(key(source, span), q)
            if mask is not None:
                s = jnp.where(mask(s.shape), s, NEGATIVE)
            scores.append(s)
        top = functools.reduce(jnp.maximum, [jnp.max(s, axis=0, keepdims=True) for s in scores])
        owns = []
        if own is not None:
            for span in spans:
                s = dot_nt(key_refs["t"][span[0]:span[1], :], query_ref[span[0]:span[1], :])
                owns.append(jnp.where(own(s.shape), s, NEGATIVE))
            top = jnp.maximum(
                top, jnp.concatenate([jnp.max(s, axis=0, keepdims=True) for s in owns], axis=1)
            )
        total = None
        out = None
        for (source, span, mask), s in zip(pieces, scores):
            p = jnp.exp2((s - top) * SCALE2)
            part = jnp.sum(p, axis=0, keepdims=True)
            term = dot(value_t(source, span), p.astype(BF16))
            total = part if total is None else total + part
            out = term if out is None else out + term
        if own is not None:
            width = half_c
            sums, terms = [], []
            for n, (span, s) in enumerate(zip(spans, owns)):
                p = jnp.exp2((s - top[:, n * width:(n + 1) * width]) * SCALE2)
                sums.append(jnp.sum(p, axis=0, keepdims=True))
                terms.append(dot(value_t("t", span), p.astype(BF16)))
            total = total + jnp.concatenate(sums, axis=1)
            out = out + jnp.concatenate(terms, axis=1)
        lse = top * SCALE2 + jnp.log(total) * LOG2E
        out = (out * (1.0 / total)).T.astype(BF16)
        at = 0
        for a, b in spans:
            mixed_ref[a:b, column] = out[at:at + b - a, :]
            lse_ref[h, :, a:b] = lse[:, at:at + b - a]
            at += b - a


def attn_call(group, place, branch, blocks, gain, w_key, w_value, q, k, v, half_p, half_c, wait):
    rows, cols = q.shape[1:]
    heads = cols // HEAD_DIM
    slots = blocks[0].shape[1]
    width = w_key.shape[0]
    keys = sum(a.shape[1] for a in k)
    return pl.pallas_call(
        functools.partial(attn_kernel, group, half_p, half_c),
        name=f"attn{group}",
        grid_spec=pltpu.PrefetchScalarGridSpec(
            num_scalar_prefetch=2,
            grid=(heads,),
            in_specs=[VMEM] * 4 + [pl.BlockSpec((1, width), lambda h, *s: (0, 0))] + [VMEM] * 7 + [ANY],
            out_specs=[pl.BlockSpec((slots, width), lambda h, *s: (0, 0))] * 2 + [VMEM] * 4,
        ),
        out_shape=[
            jax.ShapeDtypeStruct((slots, width), BF16),
            jax.ShapeDtypeStruct((slots, width), BF16),
            held(slots, cols),
            held(slots, cols),
            held(rows, cols),
            pltpu.VMEM((heads, 1, rows), F32),
        ],
        compiler_params=params(1, 10),
        cost_estimate=cost(8 * heads * rows * keys * HEAD_DIM, 4 * keys * cols, heads * rows * keys),
    )(place, branch, *near(*blocks), gain, *near(w_key, w_value, q, *k, *v), wait)


def attn_back_kernel(group, half_p, half_c, core_ref, branch_ref, q_ref, ks_ref, km_ref, kt_ref, vs_ref,
                     vm_ref, vt_ref, lse_ref, ga_own_ref, ga_oth_ref, wo_ref, wq_ref, wk_ref, wv_ref,
                     p_ref, c_ref, sq_ref, gain_ref, wait_ref,
                     ds_ref, dm_ref, dt_ref, send_ref, keep_ref, sqsend_ref, sqown_ref, sqfar_ref,
                     do_ref, kacc, vacc, wide):
    h = pl.program_id(0)
    half = half_p + half_c
    cols = wq_ref.shape[1]
    slots, mem = ks_ref.shape[0], km_ref.shape[1]
    me = core_ref[0]
    core = me & 1
    wo = wo_ref[pl.ds(pl.multiple_of(h * HEAD_DIM, HEAD_DIM), HEAD_DIM), :]
    do_ref[pl.ds(pl.multiple_of(core * half, half), half), :] = dot_nt(ga_own_ref[...], wo).astype(BF16)
    do_ref[pl.ds(pl.multiple_of((1 - core) * half, half), half), :] = dot_nt(ga_oth_ref[...], wo).astype(BF16)
    head = pl.ds(pl.multiple_of(h * HEAD_DIM, HEAD_DIM), HEAD_DIM)
    view = lambda ref: ref.at[group, :, head]
    key_refs = {"s": ks_ref.at[:, head], "m": view(km_ref), "t": view(kt_ref)}
    value_refs = {"s": vs_ref.at[:, head], "m": view(vm_ref), "t": view(vt_ref)}
    starts = {"s": 0, "m": slots, "t": slots + mem}
    sizes = {"s": slots, "m": mem}
    query_ref = view(q_ref)
    column = lambda n: pl.ds(pl.multiple_of(n * cols + h * HEAD_DIM, HEAD_DIM), HEAD_DIM)
    done = set()

    def bounds(source, span):
        a, b = (0, sizes[source]) if span is None else span
        return starts[source] + a, starts[source] + b

    def gather(acc, source, span, value):
        a, b = bounds(source, span)
        if (id(acc), a) in done:
            acc[a:b, :] += value
        else:
            done.add((id(acc), a))
            acc[a:b, :] = value

    for spans, pieces, own in tiles(half_p, half_c, branch_ref, group):
        q = rows_of(query_ref, spans)
        do = rows_of(do_ref, spans)
        lse = [lse_ref[h, :, a:b] for a, b in spans]
        lse = lse[0] if len(lse) == 1 else jnp.concatenate(lse, axis=1)
        todo = [(source, span, mask, q, do, lse, None) for source, span, mask in pieces]
        if own is not None:
            for n, span in enumerate(spans):
                cut = slice(n * half_c, (n + 1) * half_c)
                todo.append(("t", span, own, q[cut, :], do[cut, :], lse[:, cut], n))
        kept = []
        row_dot = None
        own_dots = []
        for source, span, mask, qq, dd, ll, n in todo:
            k = key_refs[source][...] if span is None else key_refs[source][span[0]:span[1], :]
            v = value_refs[source][...] if span is None else value_refs[source][span[0]:span[1], :]
            s = dot_nt(k, qq)
            if mask is not None:
                s = jnp.where(mask(s.shape), s, NEGATIVE)
            p = jnp.exp2(s * SCALE2 - ll)
            dp = dot_nt(v, dd)
            part = jnp.sum(p * dp, axis=0, keepdims=True)
            if n is None:
                row_dot = part if row_dot is None else row_dot + part
            else:
                own_dots.append(part)
            kept.append((k, p, dp))
        if own_dots:
            row_dot = row_dot + jnp.concatenate(own_dots, axis=1)
        dq = None
        own_dq = []
        for (source, span, mask, qq, dd, ll, n), (k, p, dp) in zip(todo, kept):
            rd = row_dot if n is None else row_dot[:, n * half_c:(n + 1) * half_c]
            ds = (p * (dp - rd)).astype(BF16)
            gather(kacc, source, span, dot(ds, qq))
            gather(vacc, source, span, dot(p.astype(BF16), dd))
            term = dot_tn(k, ds)
            if n is None:
                dq = term if dq is None else dq + term
            else:
                own_dq.append(term)
        if own_dq:
            dq = dq + jnp.concatenate(own_dq, axis=1)
        dq = (dq * SCALE).T.astype(BF16)
        at = 0
        for a, b in spans:
            dt_ref[a:b, column(0)] = dq[at:at + b - a, :]
            at += b - a
    for source, ref, n, at in (("s", ds_ref, slots, 0), ("m", dm_ref, mem, 0), ("t", dt_ref, 2 * half, 1)):
        a = starts[source]
        ref[:, column(at)] = (kacc[a:a + n, :] * SCALE).astype(BF16)
        ref[:, column(at + 1)] = vacc[a:a + n, :].astype(BF16)

    @pl.when(h == pl.num_programs(0) - 1)
    def _():
        gain = gain_ref[...]
        grad = dot_nt(ds_ref[:, :cols], wk_ref[...]) + dot_nt(ds_ref[:, cols:], wv_ref[...])
        scaled, inv_std = normalize(sq_ref[...].astype(F32))
        wide[...] = norm_pull(grad, gain, scaled, inv_std)
        for ref, flip in ((sqown_ref, 0), (sqfar_ref, 2), (sqsend_ref.at[0], 1), (sqsend_ref.at[1], 3)):
            ref[...] = wide[:, at_rows(me ^ flip, cols)].astype(BF16)
        for ref, part in ((send_ref, 1 - core), (keep_ref, core)):
            rows = pl.ds(pl.multiple_of(part * half, half), half)
            grad = (
                dot_nt(dt_ref[rows, :cols], wq_ref[...])
                + dot_nt(dt_ref[rows, cols:2 * cols], wk_ref[...])
                + dot_nt(dt_ref[rows, 2 * cols:], wv_ref[...])
            )
            x = jnp.concatenate(
                [
                    p_ref[group, at_rows(part, half_p), :],
                    c_ref[group, at_rows(part, half_c), :],
                ],
                axis=0,
            ).astype(F32)
            scaled, inv_std = normalize(x)
            ref[...] = norm_pull(grad, gain, scaled, inv_std).astype(BF16)


def attn_back_call(group, place, branch, q, k, v, lse, ga_own, ga_oth, w_out, w_query, w_key, w_value,
                   prompt, cont, squeezed, gain, wait):
    rows, cols = q.shape[1:]
    heads = cols // HEAD_DIM
    half_p, half_c = prompt.shape[1] // 2, cont.shape[1] // 2
    half = half_p + half_c
    width = prompt.shape[2]
    slots, mem = k[0].shape[0], k[1].shape[1]
    n_keys = slots + mem + rows
    return pl.pallas_call(
        functools.partial(attn_back_kernel, group, half_p, half_c),
        name=f"attnback{group}",
        grid_spec=pltpu.PrefetchScalarGridSpec(
            num_scalar_prefetch=2,
            grid=(heads,),
            in_specs=[VMEM] * 17 + [pl.BlockSpec((1, width), lambda h, *s: (0, 0)), ANY],
            out_specs=[VMEM] * 8,
            scratch_shapes=[
                pltpu.VMEM((rows, HEAD_DIM), BF16),
                pltpu.VMEM((n_keys, HEAD_DIM), F32),
                pltpu.VMEM((n_keys, HEAD_DIM), F32),
                pltpu.VMEM((slots, width), F32),
            ],
        ),
        out_shape=[held(slots, 2 * cols), held(mem, 2 * cols), held(rows, 3 * cols)]
        + [held(half, width)] * 2
        + [held(2, slots, cols)]
        + [held(slots, cols)] * 2,
        compiler_params=params(1, 18),
        cost_estimate=cost(
            20 * heads * rows * n_keys * HEAD_DIM + 8 * rows * width * cols,
            8 * n_keys * cols + 12 * rows * width,
            heads * rows * n_keys,
        ),
    )(place, branch, *near(q, *k, *v, lse, ga_own, ga_oth, w_out, w_query, w_key, w_value, prompt, cont,
                           squeezed), gain, wait)


def ffn_kernel(group, core_ref, p_ref, c_ref, cp_ref, cc_ref, m0_ref, m2_ref, m1_ref, m3_ref,
               w0_ref, w2_ref, w1_ref, w3_ref, gain_ref, up_ref, down_ref, wait_ref,
               nf_ref, act_ref, pre_ref, gsend_ref, gkeep_ref, fsend_ref, fkeep_ref):
    j = pl.program_id(0)
    core = core_ref[0] & 1
    first = (core_ref[0] < 2).astype(F32)
    part = jnp.where(j == 0, 1 - core, core)
    half_p, half_c = p_ref.shape[1] // 2, c_ref.shape[1] // 2
    half = half_p + half_c
    both = lambda p, c: jnp.concatenate(
        [p[group, at_rows(part, half_p), :], c[group, at_rows(part, half_c), :]], axis=0
    )
    rows = at_rows(part, half)
    gain = gain_ref[...]
    cot = both(cp_ref, cc_ref)
    attended = (dot(m0_ref[rows, :], w0_ref[...]) + dot(m2_ref[rows, :], w2_ref[...])) + (
        dot(m1_ref[rows, :], w1_ref[...]) + dot(m3_ref[rows, :], w3_ref[...])
    )
    hidden = both(p_ref, c_ref).astype(F32) + attended
    scaled, inv_std = normalize(hidden)
    normed = (scaled * gain).astype(BF16)
    nf_ref[rows, :] = normed
    units = up_ref.shape[1]
    chunk = 256
    for a in range(0, units, chunk):
        cut = slice(a, a + chunk)
        active, slope = gelu_both(dot(normed, up_ref[:, cut]))
        act_ref[rows, cut] = active.astype(BF16)
        pre_ref[rows, cut] = (dot_nt(cot, down_ref[cut, :]) * slope).astype(BF16)
    grad = dot_nt(pre_ref[rows, :], up_ref[...])
    grad = norm_pull(grad, gain, scaled, inv_std)
    term = dot(act_ref[rows, :], down_ref[...])

    @pl.when(j == 0)
    def _():
        gsend_ref[...] = grad.astype(BF16)
        fsend_ref[...] = term.astype(BF16)

    @pl.when(j == 1)
    def _():
        gkeep_ref[...] = (grad + first * cot.astype(F32)).astype(BF16)
        fkeep_ref[...] = (term + first * hidden).astype(BF16)


def ffn_call(group, place, prompt, cont, cot_p, cot_c, mixed, w_out, gain, w_up, w_down, wait):
    half = (prompt.shape[1] + cont.shape[1]) // 2
    width, units = prompt.shape[2], w_up.shape[1]
    cols = mixed[0].shape[1]
    return pl.pallas_call(
        functools.partial(ffn_kernel, group),
        name=f"ffn{group}",
        grid_spec=pltpu.PrefetchScalarGridSpec(
            num_scalar_prefetch=1,
            grid=(2,),
            in_specs=[VMEM] * 12 + [pl.BlockSpec((1, width), lambda j, s: (0, 0)), VMEM, VMEM, ANY],
            out_specs=[VMEM] * 7,
        ),
        out_shape=[held(2 * half, width), held(2 * half, units), held(2 * half, units)]
        + [held(half, width)] * 4,
        compiler_params=params(1, 12),
        cost_estimate=cost(
            4 * half * width * (4 * units + 4 * cols), 2 * half * (12 * width), 4 * half * units
        ),
    )(place, *near(prompt, cont, cot_p, cot_c, *mixed, *w_out), gain, *near(w_up, w_down), wait)


def block_of(p, send, order, place_ref):
    first = place_ref[1 + order[0]] ^ send
    return (first << order[0]) + ((p >> 1) << order[1]) + ((p & 1) << order[2])


def lanes_of(i, order, place_ref, size):
    return [at_rows(block_of(n, 1 - i, order, place_ref), size) for n in range(4)]


def row_specs(order, *arrays):
    spec = lambda a, n: pl.BlockSpec((a.shape[0] // 8, a.shape[1]), lambda i, s: (block_of(n, 1 - i, order, s), 0))
    return [spec(a, n) for a in arrays for n in range(4)]


def side_by_side(ref, lanes, *at):
    return jnp.concatenate([ref[(*at, slice(None), n)] for n in lanes], axis=1)


def stacked(refs):
    return jnp.concatenate([r[...] for r in refs], axis=0)


def put(i, outs, columns):
    size = outs[0].shape[1]
    for step in range(2):

        @pl.when(i == step)
        def _(step=step):
            for n in range(4):
                ref, row = (outs[-1], n) if step else (outs[n * (len(outs) - 1) // 4], n % outs[0].shape[0])
                at = 0
                for value in columns:
                    width = value.shape[1]
                    ref[row, :, at:at + width] = value[n * size:(n + 1) * size].astype(BF16)
                    at += width


def store_gain(ref, lanes, gain):
    for n, rows in enumerate(lanes):
        ref[rows, :] = gain[n * rows.size:(n + 1) * rows.size]


def payload(size, cols, sends):
    return [held(4 // sends, size, cols)] * sends + [held(4, size, cols)]


def up_weights_kernel(groups, order, place_ref, *refs):
    nf, pre = refs[:groups], refs[groups:2 * groups]
    up_refs, gain_refs = refs[2 * groups:2 * groups + 4], refs[2 * groups + 4:2 * groups + 8]
    *outs, partial_ref = refs[2 * groups + 9:]
    i = pl.program_id(0)
    lanes = lanes_of(i, order, place_ref, outs[0].shape[1])
    up = None
    for g in range(groups):
        part = dot_tn(side_by_side(nf[g], lanes), pre[g][...])
        up = part if up is None else up + part
    gain = jnp.sum(up * stacked(up_refs).astype(F32), axis=1, keepdims=True) / stacked(gain_refs)
    put(i, outs, [up])
    store_gain(partial_ref, lanes, gain)


def up_weights_call(order, place, nf, pre, w_up, gain, wait):
    groups = len(nf)
    rows, width = nf[0].shape
    units = w_up.shape[1]
    size = width // 8
    return pl.pallas_call(
        functools.partial(up_weights_kernel, groups, order),
        name="upweights",
        grid_spec=pltpu.PrefetchScalarGridSpec(
            num_scalar_prefetch=1,
            grid=(2,),
            in_specs=[VMEM] * (2 * groups) + row_specs(order, w_up, gain) + [ANY],
            out_specs=[VMEM] * 4,
        ),
        out_shape=payload(size, units, 2) + [pltpu.VMEM((width, 128), F32)],
        compiler_params=params(1, 10),
        cost_estimate=cost(2 * groups * rows * width * units, 6 * groups * rows * width),
    )(place, *near(*nf, *pre), *([w_up] * 4), *([gain] * 4), wait)


def down_weights_kernel(groups, order, place_ref, *refs):
    act = refs[:groups]
    cp_ref, cc_ref, wait_ref, *outs = refs[groups:]
    half_p, half_c = cp_ref.shape[1] // 2, cc_ref.shape[1] // 2
    i = pl.program_id(0)
    lanes = lanes_of(i, order, place_ref, outs[0].shape[1])
    down = None
    for g in range(groups):
        p, c = side_by_side(cp_ref, lanes, g), side_by_side(cc_ref, lanes, g)
        both = jnp.concatenate([p[:half_p], c[:half_c], p[half_p:], c[half_c:]], axis=0)
        part = dot_tn(both, act[g][...])
        down = part if down is None else down + part
    put(i, outs, [down])


def down_weights_call(order, place, act, cot_p, cot_c, wait):
    groups = len(act)
    rows, units = act[0].shape
    width = cot_p.shape[2]
    return pl.pallas_call(
        functools.partial(down_weights_kernel, groups, order),
        name="downweights",
        grid_spec=pltpu.PrefetchScalarGridSpec(
            num_scalar_prefetch=1, grid=(2,), in_specs=[VMEM] * (groups + 2) + [ANY], out_specs=[VMEM] * 3
        ),
        out_shape=payload(width // 8, units, 2),
        compiler_params=params(1, 10),
        cost_estimate=cost(2 * groups * rows * width * units, 6 * groups * rows * width),
    )(place, *near(*act, cot_p, cot_c), wait)


def attn_weights_kernel(groups, order, place_ref, *refs):
    i = pl.program_id(0)
    take = iter(refs)
    some = lambda n: [next(take) for _ in range(n)]
    n_mem, n_tok = some(4), some(4)
    n_sq = some(groups)
    grads = [some(3) for _ in range(groups)]
    weights, gain_refs = [some(4) for _ in range(3)], some(4)
    partial_ref, _, *outs = take
    cols = weights[0][0].shape[1]
    join = lambda p, g: jnp.concatenate([r[g] for r in p], axis=1)
    plus = lambda a, b: b if a is None else a + b
    lead = tok = None
    lanes = lanes_of(i, order, place_ref, outs[0].shape[1])
    for g in range(groups):
        ds, dm, dt = grads[g]
        lead = plus(lead, dot_tn(side_by_side(n_sq[g], lanes), ds[...]))
        lead = plus(lead, dot_tn(join(n_mem, g), dm[...]))
        tok = plus(tok, dot_tn(join(n_tok, g), dt[...]))
    values = [tok[:, :cols], tok[:, cols:2 * cols] + lead[:, :cols], tok[:, 2 * cols:] + lead[:, cols:]]
    gain = sum(v * stacked(w).astype(F32) for v, w in zip(values, weights))
    gain = jnp.sum(gain, axis=1, keepdims=True) / stacked(gain_refs)
    ffn = jnp.concatenate([partial_ref[n, :] for n in lanes], axis=0)
    low = lax.broadcasted_iota(jnp.int32, ffn.shape, 1) < 64
    put(i, outs, values + [jnp.where(low, gain, ffn)])


def attn_weights_call(order, place, n_sq, n_mem, n_tok, grads, weights, gain, partial, wait):
    groups = len(n_sq)
    width, cols = weights[0].shape
    size = width // 8
    lane3 = lambda a, n: pl.BlockSpec(
        (groups, a.shape[1], size), lambda i, s: (0, 0, block_of(n, 1 - i, order, s))
    )
    specs = [lane3(a, n) for a in (n_mem, n_tok) for n in range(4)]
    whole = near(*n_sq, *[x for group in grads for x in group])
    rows = n_sq[0].shape[0] + n_mem.shape[1] + 2 * n_tok.shape[1]
    return pl.pallas_call(
        functools.partial(attn_weights_kernel, groups, order),
        name="qkvweights",
        grid_spec=pltpu.PrefetchScalarGridSpec(
            num_scalar_prefetch=1,
            grid=(2,),
            in_specs=specs + [VMEM] * len(whole) + row_specs(order, *weights, gain) + [VMEM, ANY],
            out_specs=[VMEM] * 2,
        ),
        out_shape=payload(size, 3 * cols + 128, 1),
        compiler_params=params(1, 24),
        cost_estimate=cost(4 * groups * rows * width * cols, 4 * groups * rows * width),
    )(
        place, *([n_mem] * 4), *([n_tok] * 4), *whole, *[w for w in weights for _ in range(4)], *([gain] * 4),
        *near(partial), wait,
    )


def conv_weights_kernel(groups, half, order, place_ref, *refs):
    i = pl.program_id(0)
    take = iter(refs)
    some = lambda n: [next(take) for _ in range(n)]
    taps, grads = some(4), some(groups)
    ga = [some(2) for _ in range(groups)]
    mixed = some(groups)
    _, *outs = take
    core = place_ref[0] & 1
    lanes = lanes_of(i, order, place_ref, outs[0].shape[1])
    plus = lambda a, b: b if a is None else a + b
    conv = [None] * taps[0].shape[0]
    out = None
    for g in range(groups):
        for t in range(len(conv)):
            rows = jnp.concatenate([r[t, g] for r in taps], axis=1)
            conv[t] = plus(conv[t], dot_tn(rows, grads[g][...]))
        for ref, part in ((ga[g][0], core), (ga[g][1], 1 - core)):
            out = plus(out, dot_tn(side_by_side(ref, lanes), mixed[g][at_rows(part, half), :]))
    put(i, outs, conv + [out])


def conv_weights_call(order, place, taps, grads, ga, mixed, wait):
    rate, groups, slots, width = taps.shape
    cols = grads[0].shape[1]
    size = width // 8
    half = ga[0][0].shape[0]
    lane = lambda n: pl.BlockSpec(
        (rate, groups, slots, size), lambda i, s: (0, 0, 0, block_of(n, 1 - i, order, s))
    )
    whole = near(*grads, *[x for pair in ga for x in pair], *mixed)
    return pl.pallas_call(
        functools.partial(conv_weights_kernel, groups, half, order),
        name="convweights",
        grid_spec=pltpu.PrefetchScalarGridSpec(
            num_scalar_prefetch=1,
            grid=(2,),
            in_specs=[lane(n) for n in range(4)] + [VMEM] * len(whole) + [ANY],
            out_specs=[VMEM] * 2,
        ),
        out_shape=payload(size, (rate + 1) * cols, 1),
        compiler_params=params(1, 24),
        cost_estimate=cost(2 * rate * groups * slots * width * cols, 8 * rate * width * cols),
    )(place, *([taps] * 4), *whole, wait)


def split_kernel(bit, place_ref, keep_ref, *refs):
    got, (send_ref, next_ref) = refs[:-3], refs[-2:]
    mine = place_ref[1 + bit]
    rows = send_ref.shape[0]
    for ref, part in ((send_ref, 1 - mine), (next_ref, mine)):
        at = at_rows(part, rows)
        if len(got) == 1:
            ref[...] = (keep_ref[at, :].astype(F32) + got[0][at, :].astype(F32)).astype(BF16)
        else:
            for n in range(2):

                @pl.when(part == n)
                def _(n=n, ref=ref):
                    half = slice(n * rows, (n + 1) * rows)
                    ref[...] = (keep_ref[half, :].astype(F32) + got[n][...].astype(F32)).astype(BF16)


def split_call(bit, place, keep, got, wait):
    rows, cols = keep.shape
    return pl.pallas_call(
        functools.partial(split_kernel, bit),
        name="split",
        grid_spec=pltpu.PrefetchScalarGridSpec(
            num_scalar_prefetch=1, grid=(1,), in_specs=[VMEM] * (1 + len(got)) + [ANY], out_specs=[VMEM] * 2
        ),
        out_shape=[held(rows // 2, cols)] * 2,
        compiler_params=params(1, 8),
        cost_estimate=cost(rows * cols, 6 * rows * cols),
    )(place, *near(keep, *got), wait)


def pause_kernel(*refs):
    refs[-1][...] = jnp.zeros(refs[-1].shape, F32)


def pause_call(arrays):
    return pl.pallas_call(
        pause_kernel,
        name="pause",
        in_specs=[ANY] * len(arrays),
        out_specs=VMEM,
        out_shape=pltpu.VMEM((8, 128), F32),
        compiler_params=params(0, 1),
        cost_estimate=pl.CostEstimate(flops=10**10, bytes_accessed=10**8, transcendentals=0),
    )(*arrays)


def finish_kernel(parts, keep_ref, got_ref, wait_ref, *refs):
    at = 0
    for (width, flipped), ref in zip(parts, refs):
        value = keep_ref[:, at:at + width].astype(F32) + got_ref[:, at:at + width].astype(F32)
        if len(ref.shape) == 3:
            cols = ref.shape[2]
            for n in range(ref.shape[0]):
                ref[n] = value[:, n * cols:(n + 1) * cols]
        elif ref.shape[0] == 2:
            ref[...] = jnp.concatenate([value.T[:1, :], value.T[64:65, :]], axis=0)
        else:
            ref[...] = value.T if flipped else value
        at += width


def finish_call(parts, keep, got, wait):
    return pl.pallas_call(
        functools.partial(finish_kernel, [(width, flipped) for width, _, flipped in parts]),
        name="finish",
        in_specs=[VMEM, VMEM, ANY],
        out_specs=[VMEM] * len(parts),
        out_shape=[jax.ShapeDtypeStruct(shape, F32) for _, shape, _ in parts],
        compiler_params=params(0, 8),
        cost_estimate=cost(keep.size, 8 * keep.size),
    )(*near(keep, got), wait)


def assemble_kernel(count, place_ref, *refs):
    own, oth = refs[:count], refs[count:2 * count]
    p_ref, c_ref = refs[-2:]
    half_p = p_ref.shape[1]
    mine = pl.program_id(1) == (place_ref[0] & 1)
    for n in range(count):
        for ref, hit in ((own[n], mine), (oth[n], jnp.logical_not(mine))):

            @pl.when(jnp.logical_and(pl.program_id(0) == n, hit))
            def _(ref=ref):
                p_ref[0] = ref[:half_p]
                c_ref[0] = ref[half_p:]


def assemble_call(place, own, oth, half_p, wait):
    half, width = own[0].shape
    groups = len(own)
    sds = jax.ShapeDtypeStruct
    block = lambda n: pl.BlockSpec((1, n, width), lambda i, j, s: (i, j, 0))
    return pl.pallas_call(
        functools.partial(assemble_kernel, groups),
        name="assemble",
        grid_spec=pltpu.PrefetchScalarGridSpec(
            num_scalar_prefetch=1,
            grid=(groups, 2),
            in_specs=[VMEM] * (2 * groups) + [ANY],
            out_specs=[block(half_p), block(half - half_p)],
        ),
        out_shape=[
            sds((groups, 2 * half_p, width), BF16),
            sds((groups, 2 * (half - half_p), width), BF16),
        ],
        compiler_params=params(2),
        cost_estimate=cost(0, 8 * groups * half * width),
    )(place, *near(*own, *oth), wait)


def swap(x, flip, name, axis="tensor"):
    with jax.named_scope("x_" + name):
        return lax.ppermute(x, axis, [(i, i ^ flip) for i in range(lax.axis_size(axis))])


def tie(*arrays):
    return lax.optimization_barrier(arrays)


class Pieces:
    def __init__(self, name, keep, got, count=2):
        rows = keep.shape[0] // count
        self.name = name
        self.own = [add_low(keep[n * rows:(n + 1) * rows], got[n * rows:(n + 1) * rows]) for n in range(count)]
        self.far = []

    def start(self, count=1):
        for _ in range(count):
            n = len(self.far)
            self.far.append(swap(self.own[n], 2, f"{self.name}{'abcd'[n]}"))
        return self

    def hold(self, n, *others):
        *others, self.far[n] = tie(*others, self.far[n])
        return others

    def total(self, base=None):
        far = jnp.concatenate(self.far, axis=0).astype(F32)
        value = jnp.concatenate(self.own, axis=0).astype(F32) + far
        return (value if base is None else value + base.astype(F32)).astype(BF16)


def add_low(a, b):
    return (a.astype(F32) + b.astype(F32)).astype(BF16)


class Spread:
    def __init__(self, name, payload, order, low_bits, place):
        self.name = name
        self.bits = [b + low_bits for b in order] + list(range(low_bits - 1, -1, -1))
        self.low_bits = low_bits
        self.place = place
        size, cols = payload[-1].shape[1:]
        *self.send, self.keep = (x.reshape(-1, cols) for x in payload)
        self.got = []
        self.step = 0

    def start(self, parts=(0, 1)):
        bit = self.bits[self.step]
        for n in parts[:len(self.send)]:
            name = f"{self.name}{self.step}" + ("ab"[n] if len(self.send) > 1 else "")
            self.got.append(swap(self.send[n], 1 << bit, name, "dp"))
        if len(self.got) == len(self.send):
            self.step += 1
        return self

    def hold(self, *others):
        *rest, = tie(*others, *self.got)
        self.got = rest[len(others):]
        return rest[:len(others)]

    def split(self, wait=None):
        bit = self.bits[self.step]
        index = bit - self.low_bits if bit >= self.low_bits else 3 + bit
        send, self.keep = split_call(index, self.place, self.keep, self.got, self.keep if wait is None else wait)
        self.send, self.got = [send], []
        return self

    def next(self):
        return self if self.step == len(self.bits) else self.split().start()

    def end(self, parts, wait=None):
        if not self.got:
            self.start()
        while self.step < len(self.bits):
            self.next()
        return finish_call(parts, self.keep, self.got[0], self.keep if wait is None else wait)


def meet(spreads, *others):
    arrays = tie(*others, *[x for s in spreads for x in s.got])
    at = len(others)
    for s in spreads:
        s.got = list(arrays[at:at + len(s.got)])
        at += len(s.got)
    return list(arrays[:len(others)])


def per_device(prompt, cont, memory, old_memory, branch_at, gain_attn, w_query, w_key, w_value, w_out,
               gain_ffn, w_up, w_down, w_conv, cot_prompt, cot_cont):
    groups, prompt_len, width = prompt.shape
    half_p, half_c = prompt_len // 2, cont.shape[1] // 2
    units, cols = w_up.shape[1], w_query.shape[1]
    me = lax.axis_index("tensor")
    dp = lax.axis_index("dp")
    low_bits = lax.axis_size("dp").bit_length() - 4
    place = [me] + [(dp >> (low_bits + n)) & 1 for n in range(3)] + [(dp >> n) & 1 for n in range(low_bits)]
    place = jnp.stack(place).astype(jnp.int32)
    gain_a = gain_attn.reshape(1, width)
    gain_f = gain_ffn.reshape(1, width)
    column_a = jnp.broadcast_to(gain_attn[:, None], (width, 128))
    column_f = jnp.broadcast_to(gain_ffn[:, None], (width, 128))
    x_first, z_first = (0, 1, 2), (1, 0, 2)

    sq_own = conv_call(place, old_memory, w_conv)
    sq_far = swap(sq_own, 2, "sqfar")
    sq_near = swap(sq_own, 1, "sqnear")
    n_mem, k_mem, v_mem, n_tok, q_tok, k_tok, v_tok = qkv_call(
        memory, prompt, cont, gain_a, w_query, w_key, w_value, sq_own
    )
    k_mem, sq_far, w_out = tie(k_mem, sq_far, w_out)
    sq_diag = swap(sq_far, 1, "sqdiag")
    w_far = swap(w_out, 2, "wfar")
    w_near = swap(w_out, 1, "wnear")

    lead, mixed, lse, far = [], [], [], []
    wait = k_mem
    for g in range(groups):
        squeezed, n_sq, k_sq, v_sq, m, l = attn_call(
            g, place, branch_at, (sq_own, sq_far, sq_near, sq_diag), gain_a, w_key, w_value, q_tok,
            (k_mem, k_tok), (v_mem, v_tok), half_p, half_c, wait,
        )
        if g == 0:
            m, w_far = tie(m, w_far)
            w_diag = swap(w_far, 1, "wdiag")
        else:
            m, far[-1] = tie(m, far[-1])
        far.append(swap(m, 2, f"mfar{g}"))
        lead.append((squeezed, n_sq, k_sq, v_sq))
        mixed.append(m)
        lse.append(l)
        wait = m
    w_all = (w_out, w_far, w_near, w_diag)

    def run_ffn(g, wait):
        blocks = (mixed[g], far[g], swap(mixed[g], 1, f"mnear{g}"), swap(far[g], 1, f"mdiag{g}"))
        return list(ffn_call(
            g, place, prompt, cont, cot_prompt, cot_cont, blocks, w_all, gain_f, w_up, w_down, wait
        ))

    def combine(g, chip, other):
        low = add_low(chip, other)
        return low, swap(low, 1, f"ga{g}")

    def run_back(g, grad, wait):
        squeezed, _, k_sq, v_sq = lead[g]
        return list(attn_back_call(
            g, place, branch_at, q_tok, (k_sq, k_mem, k_tok), (v_sq, v_mem, v_tok), lse[g], grad[0], grad[1],
            w_out, w_query, w_key, w_value, prompt, cont, squeezed, gain_a, wait,
        ))

    last = groups - 1
    ffn, chips, others, grads, back = [], [], [], [], []
    for g in range(groups):
        ffn.append(run_ffn(g, wait))
        if g == 0:
            for n in range(1, groups):
                ffn[0][3], far[n] = tie(ffn[0][3], far[n])
        else:
            ffn[g][3], others[g - 1] = tie(ffn[g][3], others[g - 1])
        got = swap(ffn[g][3], 1, f"gsend{g}")
        if g == 0:
            taps = taps_call(old_memory, ffn[0][3])
            taps, got = tie(taps, got)
        else:
            grads.append(combine(g - 1, chips[g - 1], others[g - 1]))
        wait = add_low(ffn[g][4], got)
        chips.append(wait)
        others.append(swap(wait, 2, f"gfar{g}"))
    up = up_weights_call(x_first, place, [f[0] for f in ffn], [f[2] for f in ffn], w_up, column_f, wait)
    out = [
        Pieces(f"out{g}", ffn[g][6], swap(ffn[g][5], 1, f"outsend{g}"), 2 if g == 0 else 1) for g in range(groups)
    ]
    down = down_weights_call(z_first, place, [f[1] for f in ffn], cot_prompt, cot_cont, up[2])
    *up, gain_up = up
    up = Spread("up", up, x_first, low_bits, place).start((0,))
    wait = down[2]
    down = Spread("down", down, z_first, low_bits, place).start((0,))
    out[0].own[0], wait = tie(out[0].own[0], wait)
    out[0].start()
    tok, sq_own_grad, sq_back = [], [], []
    for g in range(groups):
        if g == last:
            grads.append(combine(last, chips[last], others[last]))
        back.append(run_back(g, grads[g], wait))
        if g == 0:
            back[g] = down.hold(*up.hold(*out[0].hold(0, *back[g])))
            up.start((1,))
            down.start((1,))
        if g == last - 1:
            *back[g], others[last] = tie(*back[g], others[last])
        if g > 0:
            *back[g], sq_back[-1] = tie(*tok[-1].hold(0, *back[g]), sq_back[-1])
            tok[-1].start()
        if g == last:
            back[g] = down.hold(*up.hold(*back[g]))
            up.next()
            down.next()
        got = swap(back[g][5], 1, f"sqsend{g}")
        sq_own_grad.append(add_low(back[g][6], got[0]))
        sq_back.append(swap(add_low(back[g][7], got[1]), 2, f"sqback{g}"))
        tok.append(Pieces(f"tok{g}", back[g][4], swap(back[g][3], 1, f"toksend{g}")))
        wait = tok[g].own[0]
        if g < last:
            tok[g].start()

    n_sq = [x[1] for x in lead]
    dqkv = [x[:3] for x in back]
    up.send[0], down.send[0], wait = tie(up.send[0], down.send[0], wait)
    for g in range(1, groups):
        *out[g].own, wait = tie(*out[g].own, wait)
    qkv = attn_weights_call(
        z_first, place, n_sq, n_mem, n_tok, dqkv, (w_query, w_key, w_value), column_a, gain_up, wait
    )
    *qkv, sq_back[last] = tie(*qkv, sq_back[last])
    if last > 0:
        qkv = tok[last - 1].hold(1, *qkv)
    wait = qkv[-1]
    qkv = Spread("qkv", qkv, z_first, low_bits, place).start()
    tok[last].own[0], wait = tie(tok[last].own[0], wait)
    tok[last].start()
    conv = conv_weights_call(
        x_first, place, taps, [add_low(a, b) for a, b in zip(sq_own_grad, sq_back)], grads, mixed, wait
    )
    conv = down.hold(*up.hold(*conv))
    conv = Spread("conv", conv, x_first, low_bits, place).start()
    for spread in (up, down):
        if spread.step < len(spread.bits):
            spread.split()
    pairs = {}
    for g in range(groups):
        tok[g].base, out[g].base = grads[g][0], None

    def round(starting, waiting, pieces, ready=(), fillers=(), far=()):
        sends = [s for s in starting if s.step < len(s.bits) and not s.got]
        rest = [p.own[len(p.far)] for p in pieces]
        owns = [p.total(p.base) for p in ready]
        message = [jnp.concatenate(rest, axis=0)] if rest else []
        arrays = tie(*[x for s in sends for x in s.send], *message, *owns)
        wait = pause_call(arrays)
        hold = [wait]
        at = 0
        for s in sends:
            s.send = [arrays[at]]
            at += 1
            s.start()
        if message:
            hold.append(swap(arrays[at], 2, "rows"))
            at += 1
        for p, x in zip(ready, arrays[at:]):
            pairs[p.name] = (x, swap(x, 1, p.name + "own"))
        results = []
        for make in fillers:
            results.append(list(make(wait)))
            wait = results[-1][0]
        flat = [x for r in results for x in r]
        others = meet(list(waiting) + list(starting), *hold, *flat, *[p.far[-1] for p in far])
        at = 0
        for p, x in zip(far, others[len(hold) + len(flat):]):
            p.far[-1] = x
        for p, x in zip(pieces, rest):
            p.far.append(others[1][at:at + x.shape[0]])
            at += x.shape[0]
        flat = iter(others[len(hold):])
        return others[0], [[next(flat) for _ in r] for r in results]

    def place_rows(name):
        def make(wait):
            own, oth = zip(*[pairs[f"{name}{g}"] for g in range(groups)])
            return assemble_call(place, own, oth, half_p, wait)

        return make

    rows = width // lax.axis_size("dp")
    pause, _ = round((up,), (conv, qkv), (tok[last], out[0]), far=(tok[last],))
    for spread in (conv, qkv):
        spread.split(pause)
    fillers = [lambda wait: up.end([(units, (rows, units), False)], wait), place_rows("tok")]
    pause, ((grad_up,), grad_tok) = round((down, conv, qkv), (), out[1:], tok, fillers)
    for spread in (conv, qkv):
        spread.split(pause)
    fillers = [lambda wait: down.end([(units, (units, rows), True)], wait), place_rows("out")]
    pause, ((grad_down,), out) = round((conv, qkv), (), (), out, fillers)
    whole = (cols, (rows, cols), False)
    grad_q, grad_k, grad_v, gains = qkv.end([whole, whole, whole, (128, (2, rows), True)])
    grad_conv, grad_o = conv.end([(RATE * cols, (RATE, rows, cols), False), (cols, (cols, rows), True)])
    gains = gains + swap(gains, 1, "gain1")
    gains = gains + swap(gains, 2, "gain2")
    return (
        out[0],
        out[1],
        grad_tok[0],
        grad_tok[1],
        grad_q,
        grad_k,
        grad_v,
        grad_o,
        grad_up,
        grad_down,
        grad_conv,
        gains[0],
        gains[1],
    )


def solution(mesh):
    tokens = P("dp", None, None)
    split = P(None, "tensor")
    in_specs = (
        tokens, tokens, tokens, tokens, P("dp", None), P(), split, split, split, P("tensor", None), P(),
        split, P("tensor", None), P(None, None, "tensor"), tokens, tokens,
    )
    both = P("dp", "tensor")
    out_specs = (
        tokens, tokens, tokens, tokens, both, both, both, P("tensor", "dp"), both, P("tensor", "dp"),
        P(None, "dp", "tensor"), P("dp"), P("dp"),
    )
    return jax.shard_map(per_device, mesh=mesh, in_specs=in_specs, out_specs=out_specs, check_vma=False)
```

```python
import functools
import math

import jax
import jax.numpy as jnp
from jax import lax
from jax.experimental import pallas as pl
from jax.experimental.pallas import tpu as pltpu
from jax.sharding import PartitionSpec as P

F32 = jnp.float32
BF16 = jnp.bfloat16
HEAD_DIM = 128
RATE = 3
EPSILON = 1e-05
NEGATIVE = -1e30
SCALE = HEAD_DIM**-0.5
LOG2E = math.log2(math.e)
SCALE2 = SCALE * LOG2E
COST = 0.05
ANY = pl.BlockSpec(memory_space=pl.ANY)
VMEM = pl.BlockSpec(memory_space=pltpu.VMEM)

TAIL_P = 0.3
TAIL = (
    0.11962927179738114,
    0.12075437242074172,
    0.09991089342247686,
    0.12857016178217745,
    -0.0536996295580258,
    0.20637064487815027,
    -0.15721286180378366,
    0.035677073905512405,
)


def dot(a, b):
    return lax.dot_general(a, b, (((1,), (0,)), ((), ())), preferred_element_type=F32)


def dot_nt(a, b):
    return lax.dot_general(a, b, (((1,), (1,)), ((), ())), preferred_element_type=F32)


def dot_tn(a, b):
    return lax.dot_general(a, b, (((0,), (0,)), ((), ())), preferred_element_type=F32)


def params(n, mib=16):
    return pltpu.CompilerParams(dimension_semantics=("arbitrary",) * n, vmem_limit_bytes=mib << 20)


def near(*arrays):
    return [pltpu.with_memory_space_constraint(x, pltpu.VMEM) for x in arrays]


def held(*shape):
    return pltpu.VMEM(shape, BF16)


def at_rows(part, n):
    return pl.ds(pl.multiple_of(part * n, n), n)


def cost(flops, nbytes, trans=0):
    return pl.CostEstimate(
        flops=int(flops * COST), bytes_accessed=int(nbytes * COST), transcendentals=int(trans * COST)
    )


def normalize(values):
    center = values - jnp.mean(values, axis=-1, keepdims=True)
    inv_std = lax.rsqrt(jnp.mean(center * center, axis=-1, keepdims=True) + EPSILON)
    return center * inv_std, inv_std


def norm_pull(grad_outer, gain, scaled, inv_std):
    grad_scaled = grad_outer * gain
    mean_a = jnp.mean(grad_scaled, axis=-1, keepdims=True)
    mean_b = jnp.mean(grad_scaled * scaled, axis=-1, keepdims=True)
    return inv_std * (grad_scaled - mean_a - scaled * mean_b)


def gelu_both(x):
    a = jnp.abs(x)
    t = 1.0 / (1.0 + TAIL_P * a)
    poly = TAIL[7]
    for k in range(6, -1, -1):
        poly = poly * t + TAIL[k]
    bell = jnp.exp2((x * x) * (-0.5 * LOG2E))
    tail = bell * (t * poly)
    cdf = jnp.where(x >= 0.0, 1.0 - tail, tail)
    return x * cdf, cdf + x * (bell * (1.0 / math.sqrt(2.0 * math.pi)))


def tap_rows(old_ref, wide, group):
    lanes = wide.shape[2]
    slots = wide.shape[1] // RATE
    for n in range(wide.shape[0]):
        wide[n] = old_ref[group, :, n * lanes:(n + 1) * lanes].astype(F32)
    return [
        jnp.concatenate(
            [wide[n, pl.ds(t, slots, stride=RATE), :].astype(BF16) for n in range(wide.shape[0])], axis=1
        )
        for t in range(RATE)
    ]


def conv_kernel(place_ref, old_ref, w_ref, out_ref, wide):
    total = None
    for t, rows in enumerate(tap_rows(old_ref, wide, 0)):
        part = dot(rows, w_ref[t])
        total = part if total is None else total + part
    out_ref[pl.program_id(0)] = total.astype(BF16)


def conv_call(place, old, w_conv):
    groups, rows, width = old.shape
    slots = rows // RATE
    cols = w_conv.shape[2]
    return pl.pallas_call(
        conv_kernel,
        name="conv",
        grid_spec=pltpu.PrefetchScalarGridSpec(
            num_scalar_prefetch=1,
            grid=(groups,),
            in_specs=[
                pl.BlockSpec((1, rows, width), lambda g, s: (g, 0, 0)),
                pl.BlockSpec((RATE, width, cols), lambda g, s: (0, 0, 0)),
            ],
            out_specs=VMEM,
            scratch_shapes=[pltpu.VMEM((width // 128, rows, 128), F32)],
        ),
        out_shape=held(groups, slots, cols),
        compiler_params=params(1, 58),
        cost_estimate=cost(2 * groups * rows * width * cols, 2 * groups * rows * width),
    )(place, old, w_conv)


def taps_kernel(old_ref, wait_ref, out_ref, wide):
    for t, rows in enumerate(tap_rows(old_ref, wide, 0)):
        out_ref[t, 0] = rows


def taps_call(old, wait):
    groups, rows, width = old.shape
    slots = rows // RATE
    return pl.pallas_call(
        taps_kernel,
        name="taps",
        grid=(groups,),
        in_specs=[pl.BlockSpec((1, rows, width), lambda g: (g, 0, 0)), ANY],
        out_specs=pl.BlockSpec((RATE, 1, slots, width), lambda g: (0, g, 0, 0)),
        out_shape=jax.ShapeDtypeStruct((RATE, groups, slots, width), BF16),
        scratch_shapes=[pltpu.VMEM((width // 128, rows, 128), F32)],
        compiler_params=params(1, 12),
        cost_estimate=cost(0, 4 * groups * rows * width),
    )(old, wait)


def qkv_kernel(mem_ref, p_ref, c_ref, gain_ref, wq_ref, wk_ref, wv_ref, wait_ref,
               nm_ref, km_ref, vm_ref, nt_ref, qt_ref, kt_ref, vt_ref):
    g, j = pl.program_id(0), pl.program_id(1)
    gain = gain_ref[...]

    @pl.when(j == 0)
    def _():
        scaled, _ = normalize(mem_ref[0].astype(F32))
        normed = (scaled * gain).astype(BF16)
        nm_ref[0] = normed
        km_ref[g] = dot(normed, wk_ref[...]).astype(BF16)
        vm_ref[g] = dot(normed, wv_ref[...]).astype(BF16)

    @pl.when(j > 0)
    def _():
        values = jnp.concatenate([p_ref[0], c_ref[0]], axis=0).astype(F32)
        scaled, _ = normalize(values)
        normed = (scaled * gain).astype(BF16)
        nt_ref[0] = normed
        rows = at_rows(j - 1, normed.shape[0])
        qt_ref[g, rows, :] = dot(normed, wq_ref[...]).astype(BF16)
        kt_ref[g, rows, :] = dot(normed, wk_ref[...]).astype(BF16)
        vt_ref[g, rows, :] = dot(normed, wv_ref[...]).astype(BF16)


def qkv_call(memory, prompt, cont, gain, w_query, w_key, w_value, wait):
    groups, mem, width = memory.shape
    half_p, half_c = prompt.shape[1] // 2, cont.shape[1] // 2
    half = half_p + half_c
    cols = w_query.shape[1]
    lead = lambda g, j: (g, 0, 0)
    later = lambda g, j: (g, jnp.maximum(j - 1, 0), 0)
    sds = jax.ShapeDtypeStruct
    return pl.pallas_call(
        qkv_kernel,
        name="qkv",
        grid=(groups, 3),
        in_specs=[
            pl.BlockSpec((1, mem, width), lead),
            pl.BlockSpec((1, half_p, width), later),
            pl.BlockSpec((1, half_c, width), later),
            pl.BlockSpec((1, width), lambda g, j: (0, 0)),
            VMEM,
            VMEM,
            VMEM,
            ANY,
        ],
        out_specs=[pl.BlockSpec((1, mem, width), lead), VMEM, VMEM, pl.BlockSpec((1, half, width), later)]
        + [VMEM] * 3,
        out_shape=[
            sds((groups, mem, width), BF16),
            held(groups, mem, cols),
            held(groups, mem, cols),
            sds((groups, 2 * half, width), BF16),
            held(groups, 2 * half, cols),
            held(groups, 2 * half, cols),
            held(groups, 2 * half, cols),
        ],
        compiler_params=params(2, 24),
        cost_estimate=cost(
            2 * groups * width * cols * (2 * mem + 6 * half), 8 * groups * (mem + 2 * half) * width
        ),
    )(memory, prompt, cont, gain, *near(w_query, w_key, w_value), wait)


def tiles(half_p, half_c, branch_ref, group):
    half = half_p + half_c

    def causal(shape):
        return lax.broadcasted_iota(jnp.int32, shape, 0) <= lax.broadcasted_iota(jnp.int32, shape, 1)

    def seen(offset):
        def mask(shape):
            key = lax.broadcasted_iota(jnp.int32, shape, 0) + offset
            query = lax.broadcasted_iota(jnp.int32, shape, 1)
            return key < jnp.where(query < half_c, branch_ref[group, 0], branch_ref[group, 1])

        return mask

    first, second = (0, half_p), (half, half + half_p)
    cont0, cont1 = (half_p, half), (half + half_p, 2 * half)
    lead = [("s", None, None), ("m", None, None)]
    return [
        ([first], lead + [("t", first, causal)], None),
        ([second], lead + [("t", first, None), ("t", second, causal)], None),
        ([cont0, cont1], lead + [("t", first, seen(0)), ("t", second, seen(half_p))], causal),
    ]


def rows_of(ref, ranges):
    parts = [ref[a:b, :] for a, b in ranges]
    return parts[0] if len(parts) == 1 else jnp.concatenate(parts, axis=0)


def attn_kernel(group, half_p, half_c, place_ref, branch_ref, own_ref, far_ref, near_ref, diag_ref, gain_ref,
                wk_ref, wv_ref, q_ref, km_ref, kt_ref, vm_ref, vt_ref, wait_ref,
                sq_ref, n_ref, ks_ref, vs_ref, mixed_ref, lse_ref):
    h = pl.program_id(0)
    cols = own_ref.shape[2]
    column = pl.ds(pl.multiple_of(h * HEAD_DIM, HEAD_DIM), HEAD_DIM)

    @pl.when(h == 0)
    def _():
        me = place_ref[0]
        for flip, block in ((0, own_ref), (2, far_ref), (1, near_ref), (3, diag_ref)):
            at = pl.multiple_of((me ^ flip) * cols, cols)
            sq_ref[:, pl.ds(at, cols)] = block[group]
        scaled, _ = normalize(sq_ref[...].astype(F32))
        normed = (scaled * gain_ref[...]).astype(BF16)
        n_ref[...] = normed
        ks_ref[...] = dot(normed, wk_ref[...]).astype(BF16)
        vs_ref[...] = dot(normed, wv_ref[...]).astype(BF16)

    view = lambda ref: ref.at[group, :, column]
    key_refs = {"m": view(km_ref), "t": view(kt_ref)}
    value_refs = {"m": view(vm_ref), "t": view(vt_ref)}
    query_ref = view(q_ref)
    vals = {("s", None): vs_ref[:, column].T, ("m", None): value_refs["m"][...].T}

    def key(source, span):
        if source == "s":
            return ks_ref[:, column]
        return key_refs[source][...] if span is None else key_refs[source][span[0]:span[1], :]

    def value_t(source, span):
        if (source, span) not in vals:
            vals[(source, span)] = value_refs[source][span[0]:span[1], :].T
        return vals[(source, span)]

    for spans, pieces, own in tiles(half_p, half_c, branch_ref, group):
        q = rows_of(query_ref, spans)
        scores = []
        for source, span, mask in pieces:
            s = dot_nt(key(source, span), q)
            if mask is not None:
                s = jnp.where(mask(s.shape), s, NEGATIVE)
            scores.append(s)
        top = functools.reduce(jnp.maximum, [jnp.max(s, axis=0, keepdims=True) for s in scores])
        owns = []
        if own is not None:
            for span in spans:
                s = dot_nt(key_refs["t"][span[0]:span[1], :], query_ref[span[0]:span[1], :])
                owns.append(jnp.where(own(s.shape), s, NEGATIVE))
            top = jnp.maximum(
                top, jnp.concatenate([jnp.max(s, axis=0, keepdims=True) for s in owns], axis=1)
            )
        total = None
        out = None
        for (source, span, mask), s in zip(pieces, scores):
            p = jnp.exp2((s - top) * SCALE2)
            part = jnp.sum(p, axis=0, keepdims=True)
            term = dot(value_t(source, span), p.astype(BF16))
            total = part if total is None else total + part
            out = term if out is None else out + term
        if own is not None:
            width = half_c
            sums, terms = [], []
            for n, (span, s) in enumerate(zip(spans, owns)):
                p = jnp.exp2((s - top[:, n * width:(n + 1) * width]) * SCALE2)
                sums.append(jnp.sum(p, axis=0, keepdims=True))
                terms.append(dot(value_t("t", span), p.astype(BF16)))
            total = total + jnp.concatenate(sums, axis=1)
            out = out + jnp.concatenate(terms, axis=1)
        lse = top * SCALE2 + jnp.log(total) * LOG2E
        out = (out * (1.0 / total)).T.astype(BF16)
        at = 0
        for a, b in spans:
            mixed_ref[a:b, column] = out[at:at + b - a, :]
            lse_ref[h, :, a:b] = lse[:, at:at + b - a]
            at += b - a


def attn_call(group, place, branch, blocks, gain, w_key, w_value, q, k, v, half_p, half_c, wait):
    rows, cols = q.shape[1:]
    heads = cols // HEAD_DIM
    slots = blocks[0].shape[1]
    width = w_key.shape[0]
    keys = sum(a.shape[1] for a in k)
    return pl.pallas_call(
        functools.partial(attn_kernel, group, half_p, half_c),
        name=f"attn{group}",
        grid_spec=pltpu.PrefetchScalarGridSpec(
            num_scalar_prefetch=2,
            grid=(heads,),
            in_specs=[VMEM] * 4 + [pl.BlockSpec((1, width), lambda h, *s: (0, 0))] + [VMEM] * 7 + [ANY],
            out_specs=[pl.BlockSpec((slots, width), lambda h, *s: (0, 0))] * 2 + [VMEM] * 4,
        ),
        out_shape=[
            jax.ShapeDtypeStruct((slots, width), BF16),
            jax.ShapeDtypeStruct((slots, width), BF16),
            held(slots, cols),
            held(slots, cols),
            held(rows, cols),
            pltpu.VMEM((heads, 1, rows), F32),
        ],
        compiler_params=params(1, 10),
        cost_estimate=cost(8 * heads * rows * keys * HEAD_DIM, 4 * keys * cols, heads * rows * keys),
    )(place, branch, *near(*blocks), gain, *near(w_key, w_value, q, *k, *v), wait)


def attn_back_kernel(group, half_p, half_c, core_ref, branch_ref, q_ref, ks_ref, km_ref, kt_ref, vs_ref,
                     vm_ref, vt_ref, lse_ref, ga_own_ref, ga_oth_ref, wo_ref, wq_ref, wk_ref, wv_ref,
                     p_ref, c_ref, sq_ref, gain_ref, wait_ref,
                     ds_ref, dm_ref, dt_ref, send_ref, keep_ref, sqsend_ref, sqown_ref, sqfar_ref,
                     do_ref, kacc, vacc, wide):
    h = pl.program_id(0)
    half = half_p + half_c
    cols = wq_ref.shape[1]
    slots, mem = ks_ref.shape[0], km_ref.shape[1]
    me = core_ref[0]
    core = me & 1
    wo = wo_ref[pl.ds(pl.multiple_of(h * HEAD_DIM, HEAD_DIM), HEAD_DIM), :]
    do_ref[pl.ds(pl.multiple_of(core * half, half), half), :] = dot_nt(ga_own_ref[...], wo).astype(BF16)
    do_ref[pl.ds(pl.multiple_of((1 - core) * half, half), half), :] = dot_nt(ga_oth_ref[...], wo).astype(BF16)
    head = pl.ds(pl.multiple_of(h * HEAD_DIM, HEAD_DIM), HEAD_DIM)
    view = lambda ref: ref.at[group, :, head]
    key_refs = {"s": ks_ref.at[:, head], "m": view(km_ref), "t": view(kt_ref)}
    value_refs = {"s": vs_ref.at[:, head], "m": view(vm_ref), "t": view(vt_ref)}
    starts = {"s": 0, "m": slots, "t": slots + mem}
    sizes = {"s": slots, "m": mem}
    query_ref = view(q_ref)
    column = lambda n: pl.ds(pl.multiple_of(n * cols + h * HEAD_DIM, HEAD_DIM), HEAD_DIM)
    done = set()

    def bounds(source, span):
        a, b = (0, sizes[source]) if span is None else span
        return starts[source] + a, starts[source] + b

    def gather(acc, source, span, value):
        a, b = bounds(source, span)
        if (id(acc), a) in done:
            acc[a:b, :] += value
        else:
            done.add((id(acc), a))
            acc[a:b, :] = value

    for spans, pieces, own in tiles(half_p, half_c, branch_ref, group):
        q = rows_of(query_ref, spans)
        do = rows_of(do_ref, spans)
        lse = [lse_ref[h, :, a:b] for a, b in spans]
        lse = lse[0] if len(lse) == 1 else jnp.concatenate(lse, axis=1)
        todo = [(source, span, mask, q, do, lse, None) for source, span, mask in pieces]
        if own is not None:
            for n, span in enumerate(spans):
                cut = slice(n * half_c, (n + 1) * half_c)
                todo.append(("t", span, own, q[cut, :], do[cut, :], lse[:, cut], n))
        kept = []
        row_dot = None
        own_dots = []
        for source, span, mask, qq, dd, ll, n in todo:
            k = key_refs[source][...] if span is None else key_refs[source][span[0]:span[1], :]
            v = value_refs[source][...] if span is None else value_refs[source][span[0]:span[1], :]
            s = dot_nt(k, qq)
            if mask is not None:
                s = jnp.where(mask(s.shape), s, NEGATIVE)
            p = jnp.exp2(s * SCALE2 - ll)
            dp = dot_nt(v, dd)
            part = jnp.sum(p * dp, axis=0, keepdims=True)
            if n is None:
                row_dot = part if row_dot is None else row_dot + part
            else:
                own_dots.append(part)
            kept.append((k, p, dp))
        if own_dots:
            row_dot = row_dot + jnp.concatenate(own_dots, axis=1)
        dq = None
        own_dq = []
        for (source, span, mask, qq, dd, ll, n), (k, p, dp) in zip(todo, kept):
            rd = row_dot if n is None else row_dot[:, n * half_c:(n + 1) * half_c]
            ds = (p * (dp - rd)).astype(BF16)
            gather(kacc, source, span, dot(ds, qq))
            gather(vacc, source, span, dot(p.astype(BF16), dd))
            term = dot_tn(k, ds)
            if n is None:
                dq = term if dq is None else dq + term
            else:
                own_dq.append(term)
        if own_dq:
            dq = dq + jnp.concatenate(own_dq, axis=1)
        dq = (dq * SCALE).T.astype(BF16)
        at = 0
        for a, b in spans:
            dt_ref[a:b, column(0)] = dq[at:at + b - a, :]
            at += b - a
    for source, ref, n, at in (("s", ds_ref, slots, 0), ("m", dm_ref, mem, 0), ("t", dt_ref, 2 * half, 1)):
        a = starts[source]
        ref[:, column(at)] = (kacc[a:a + n, :] * SCALE).astype(BF16)
        ref[:, column(at + 1)] = vacc[a:a + n, :].astype(BF16)

    @pl.when(h == pl.num_programs(0) - 1)
    def _():
        gain = gain_ref[...]
        grad = dot_nt(ds_ref[:, :cols], wk_ref[...]) + dot_nt(ds_ref[:, cols:], wv_ref[...])
        scaled, inv_std = normalize(sq_ref[...].astype(F32))
        wide[...] = norm_pull(grad, gain, scaled, inv_std)
        for ref, flip in ((sqown_ref, 0), (sqfar_ref, 2), (sqsend_ref.at[0], 1), (sqsend_ref.at[1], 3)):
            ref[...] = wide[:, at_rows(me ^ flip, cols)].astype(BF16)
        for ref, part in ((send_ref, 1 - core), (keep_ref, core)):
            rows = pl.ds(pl.multiple_of(part * half, half), half)
            grad = (
                dot_nt(dt_ref[rows, :cols], wq_ref[...])
                + dot_nt(dt_ref[rows, cols:2 * cols], wk_ref[...])
                + dot_nt(dt_ref[rows, 2 * cols:], wv_ref[...])
            )
            x = jnp.concatenate(
                [
                    p_ref[group, at_rows(part, half_p), :],
                    c_ref[group, at_rows(part, half_c), :],
                ],
                axis=0,
            ).astype(F32)
            scaled, inv_std = normalize(x)
            ref[...] = norm_pull(grad, gain, scaled, inv_std).astype(BF16)


def attn_back_call(group, place, branch, q, k, v, lse, ga_own, ga_oth, w_out, w_query, w_key, w_value,
                   prompt, cont, squeezed, gain, wait):
    rows, cols = q.shape[1:]
    heads = cols // HEAD_DIM
    half_p, half_c = prompt.shape[1] // 2, cont.shape[1] // 2
    half = half_p + half_c
    width = prompt.shape[2]
    slots, mem = k[0].shape[0], k[1].shape[1]
    n_keys = slots + mem + rows
    return pl.pallas_call(
        functools.partial(attn_back_kernel, group, half_p, half_c),
        name=f"attnback{group}",
        grid_spec=pltpu.PrefetchScalarGridSpec(
            num_scalar_prefetch=2,
            grid=(heads,),
            in_specs=[VMEM] * 17 + [pl.BlockSpec((1, width), lambda h, *s: (0, 0)), ANY],
            out_specs=[VMEM] * 8,
            scratch_shapes=[
                pltpu.VMEM((rows, HEAD_DIM), BF16),
                pltpu.VMEM((n_keys, HEAD_DIM), F32),
                pltpu.VMEM((n_keys, HEAD_DIM), F32),
                pltpu.VMEM((slots, width), F32),
            ],
        ),
        out_shape=[held(slots, 2 * cols), held(mem, 2 * cols), held(rows, 3 * cols)]
        + [held(half, width)] * 2
        + [held(2, slots, cols)]
        + [held(slots, cols)] * 2,
        compiler_params=params(1, 18),
        cost_estimate=cost(
            20 * heads * rows * n_keys * HEAD_DIM + 8 * rows * width * cols,
            8 * n_keys * cols + 12 * rows * width,
            heads * rows * n_keys,
        ),
    )(place, branch, *near(q, *k, *v, lse, ga_own, ga_oth, w_out, w_query, w_key, w_value, prompt, cont,
                           squeezed), gain, wait)


def ffn_kernel(group, core_ref, p_ref, c_ref, cp_ref, cc_ref, m0_ref, m2_ref, m1_ref, m3_ref,
               w0_ref, w2_ref, w1_ref, w3_ref, gain_ref, up_ref, down_ref, wait_ref,
               nf_ref, act_ref, pre_ref, gsend_ref, gkeep_ref, fsend_ref, fkeep_ref):
    j = pl.program_id(0)
    core = core_ref[0] & 1
    first = (core_ref[0] < 2).astype(F32)
    part = jnp.where(j == 0, 1 - core, core)
    half_p, half_c = p_ref.shape[1] // 2, c_ref.shape[1] // 2
    half = half_p + half_c
    both = lambda p, c: jnp.concatenate(
        [p[group, at_rows(part, half_p), :], c[group, at_rows(part, half_c), :]], axis=0
    )
    rows = at_rows(part, half)
    gain = gain_ref[...]
    cot = both(cp_ref, cc_ref)
    attended = (dot(m0_ref[rows, :], w0_ref[...]) + dot(m2_ref[rows, :], w2_ref[...])) + (
        dot(m1_ref[rows, :], w1_ref[...]) + dot(m3_ref[rows, :], w3_ref[...])
    )
    hidden = both(p_ref, c_ref).astype(F32) + attended
    scaled, inv_std = normalize(hidden)
    normed = (scaled * gain).astype(BF16)
    nf_ref[rows, :] = normed
    units = up_ref.shape[1]
    chunk = 256
    for a in range(0, units, chunk):
        cut = slice(a, a + chunk)
        active, slope = gelu_both(dot(normed, up_ref[:, cut]))
        act_ref[rows, cut] = active.astype(BF16)
        pre_ref[rows, cut] = (dot_nt(cot, down_ref[cut, :]) * slope).astype(BF16)
    grad = dot_nt(pre_ref[rows, :], up_ref[...])
    grad = norm_pull(grad, gain, scaled, inv_std)
    term = dot(act_ref[rows, :], down_ref[...])

    @pl.when(j == 0)
    def _():
        gsend_ref[...] = grad.astype(BF16)
        fsend_ref[...] = term.astype(BF16)

    @pl.when(j == 1)
    def _():
        gkeep_ref[...] = (grad + first * cot.astype(F32)).astype(BF16)
        fkeep_ref[...] = (term + first * hidden).astype(BF16)


def ffn_call(group, place, prompt, cont, cot_p, cot_c, mixed, w_out, gain, w_up, w_down, wait):
    half = (prompt.shape[1] + cont.shape[1]) // 2
    width, units = prompt.shape[2], w_up.shape[1]
    cols = mixed[0].shape[1]
    return pl.pallas_call(
        functools.partial(ffn_kernel, group),
        name=f"ffn{group}",
        grid_spec=pltpu.PrefetchScalarGridSpec(
            num_scalar_prefetch=1,
            grid=(2,),
            in_specs=[VMEM] * 12 + [pl.BlockSpec((1, width), lambda j, s: (0, 0)), VMEM, VMEM, ANY],
            out_specs=[VMEM] * 7,
        ),
        out_shape=[held(2 * half, width), held(2 * half, units), held(2 * half, units)]
        + [held(half, width)] * 4,
        compiler_params=params(1, 12),
        cost_estimate=cost(
            4 * half * width * (4 * units + 4 * cols), 2 * half * (12 * width), 4 * half * units
        ),
    )(place, *near(prompt, cont, cot_p, cot_c, *mixed, *w_out), gain, *near(w_up, w_down), wait)


def block_of(p, send, order, place_ref):
    first = place_ref[1 + order[0]] ^ send
    return (first << order[0]) + ((p >> 1) << order[1]) + ((p & 1) << order[2])


def lanes_of(i, order, place_ref, size):
    return [at_rows(block_of(n, 1 - i, order, place_ref), size) for n in range(4)]


def row_specs(order, *arrays):
    spec = lambda a, n: pl.BlockSpec((a.shape[0] // 8, a.shape[1]), lambda i, s: (block_of(n, 1 - i, order, s), 0))
    return [spec(a, n) for a in arrays for n in range(4)]


def side_by_side(ref, lanes, *at):
    return jnp.concatenate([ref[(*at, slice(None), n)] for n in lanes], axis=1)


def stacked(refs):
    return jnp.concatenate([r[...] for r in refs], axis=0)


def put(i, outs, columns):
    size = outs[0].shape[1]
    for step in range(2):

        @pl.when(i == step)
        def _(step=step):
            for n in range(4):
                ref, row = (outs[-1], n) if step else (outs[n * (len(outs) - 1) // 4], n % outs[0].shape[0])
                at = 0
                for value in columns:
                    width = value.shape[1]
                    ref[row, :, at:at + width] = value[n * size:(n + 1) * size].astype(BF16)
                    at += width


def store_gain(ref, lanes, gain):
    for n, rows in enumerate(lanes):
        ref[rows, :] = gain[n * rows.size:(n + 1) * rows.size]


def payload(size, cols, sends):
    return [held(4 // sends, size, cols)] * sends + [held(4, size, cols)]


def up_weights_kernel(groups, order, place_ref, *refs):
    nf, pre = refs[:groups], refs[groups:2 * groups]
    up_refs, gain_refs = refs[2 * groups:2 * groups + 4], refs[2 * groups + 4:2 * groups + 8]
    *outs, partial_ref = refs[2 * groups + 9:]
    i = pl.program_id(0)
    lanes = lanes_of(i, order, place_ref, outs[0].shape[1])
    up = None
    for g in range(groups):
        part = dot_tn(side_by_side(nf[g], lanes), pre[g][...])
        up = part if up is None else up + part
    gain = jnp.sum(up * stacked(up_refs).astype(F32), axis=1, keepdims=True) / stacked(gain_refs)
    put(i, outs, [up])
    store_gain(partial_ref, lanes, gain)


def up_weights_call(order, place, nf, pre, w_up, gain, wait):
    groups = len(nf)
    rows, width = nf[0].shape
    units = w_up.shape[1]
    size = width // 8
    return pl.pallas_call(
        functools.partial(up_weights_kernel, groups, order),
        name="upweights",
        grid_spec=pltpu.PrefetchScalarGridSpec(
            num_scalar_prefetch=1,
            grid=(2,),
            in_specs=[VMEM] * (2 * groups) + row_specs(order, w_up, gain) + [ANY],
            out_specs=[VMEM] * 4,
        ),
        out_shape=payload(size, units, 2) + [pltpu.VMEM((width, 128), F32)],
        compiler_params=params(1, 10),
        cost_estimate=cost(2 * groups * rows * width * units, 6 * groups * rows * width),
    )(place, *near(*nf, *pre), *([w_up] * 4), *([gain] * 4), wait)


def down_weights_kernel(groups, order, place_ref, *refs):
    act = refs[:groups]
    cp_ref, cc_ref, wait_ref, *outs = refs[groups:]
    half_p, half_c = cp_ref.shape[1] // 2, cc_ref.shape[1] // 2
    i = pl.program_id(0)
    lanes = lanes_of(i, order, place_ref, outs[0].shape[1])
    down = None
    for g in range(groups):
        p, c = side_by_side(cp_ref, lanes, g), side_by_side(cc_ref, lanes, g)
        both = jnp.concatenate([p[:half_p], c[:half_c], p[half_p:], c[half_c:]], axis=0)
        part = dot_tn(both, act[g][...])
        down = part if down is None else down + part
    put(i, outs, [down])


def down_weights_call(order, place, act, cot_p, cot_c, wait):
    groups = len(act)
    rows, units = act[0].shape
    width = cot_p.shape[2]
    return pl.pallas_call(
        functools.partial(down_weights_kernel, groups, order),
        name="downweights",
        grid_spec=pltpu.PrefetchScalarGridSpec(
            num_scalar_prefetch=1, grid=(2,), in_specs=[VMEM] * (groups + 2) + [ANY], out_specs=[VMEM] * 3
        ),
        out_shape=payload(width // 8, units, 2),
        compiler_params=params(1, 10),
        cost_estimate=cost(2 * groups * rows * width * units, 6 * groups * rows * width),
    )(place, *near(*act, cot_p, cot_c), wait)


def attn_weights_kernel(groups, order, place_ref, *refs):
    i = pl.program_id(0)
    take = iter(refs)
    some = lambda n: [next(take) for _ in range(n)]
    n_mem, n_tok = some(4), some(4)
    n_sq = some(groups)
    grads = [some(3) for _ in range(groups)]
    weights, gain_refs = [some(4) for _ in range(3)], some(4)
    partial_ref, _, *outs = take
    cols = weights[0][0].shape[1]
    join = lambda p, g: jnp.concatenate([r[g] for r in p], axis=1)
    plus = lambda a, b: b if a is None else a + b
    lead = tok = None
    lanes = lanes_of(i, order, place_ref, outs[0].shape[1])
    for g in range(groups):
        ds, dm, dt = grads[g]
        lead = plus(lead, dot_tn(side_by_side(n_sq[g], lanes), ds[...]))
        lead = plus(lead, dot_tn(join(n_mem, g), dm[...]))
        tok = plus(tok, dot_tn(join(n_tok, g), dt[...]))
    values = [tok[:, :cols], tok[:, cols:2 * cols] + lead[:, :cols], tok[:, 2 * cols:] + lead[:, cols:]]
    gain = sum(v * stacked(w).astype(F32) for v, w in zip(values, weights))
    gain = jnp.sum(gain, axis=1, keepdims=True) / stacked(gain_refs)
    ffn = jnp.concatenate([partial_ref[n, :] for n in lanes], axis=0)
    low = lax.broadcasted_iota(jnp.int32, ffn.shape, 1) < 64
    put(i, outs, values + [jnp.where(low, gain, ffn)])


def attn_weights_call(order, place, n_sq, n_mem, n_tok, grads, weights, gain, partial, wait):
    groups = len(n_sq)
    width, cols = weights[0].shape
    size = width // 8
    lane3 = lambda a, n: pl.BlockSpec(
        (groups, a.shape[1], size), lambda i, s: (0, 0, block_of(n, 1 - i, order, s))
    )
    specs = [lane3(a, n) for a in (n_mem, n_tok) for n in range(4)]
    whole = near(*n_sq, *[x for group in grads for x in group])
    rows = n_sq[0].shape[0] + n_mem.shape[1] + 2 * n_tok.shape[1]
    return pl.pallas_call(
        functools.partial(attn_weights_kernel, groups, order),
        name="qkvweights",
        grid_spec=pltpu.PrefetchScalarGridSpec(
            num_scalar_prefetch=1,
            grid=(2,),
            in_specs=specs + [VMEM] * len(whole) + row_specs(order, *weights, gain) + [VMEM, ANY],
            out_specs=[VMEM] * 2,
        ),
        out_shape=payload(size, 3 * cols + 128, 1),
        compiler_params=params(1, 24),
        cost_estimate=cost(4 * groups * rows * width * cols, 4 * groups * rows * width),
    )(
        place, *([n_mem] * 4), *([n_tok] * 4), *whole, *[w for w in weights for _ in range(4)], *([gain] * 4),
        *near(partial), wait,
    )


def conv_weights_kernel(groups, half, order, place_ref, *refs):
    i = pl.program_id(0)
    take = iter(refs)
    some = lambda n: [next(take) for _ in range(n)]
    taps, grads = some(4), some(groups)
    ga = [some(2) for _ in range(groups)]
    mixed = some(groups)
    _, *outs = take
    core = place_ref[0] & 1
    lanes = lanes_of(i, order, place_ref, outs[0].shape[1])
    plus = lambda a, b: b if a is None else a + b
    conv = [None] * taps[0].shape[0]
    out = None
    for g in range(groups):
        for t in range(len(conv)):
            rows = jnp.concatenate([r[t, g] for r in taps], axis=1)
            conv[t] = plus(conv[t], dot_tn(rows, grads[g][...]))
        for ref, part in ((ga[g][0], core), (ga[g][1], 1 - core)):
            out = plus(out, dot_tn(side_by_side(ref, lanes), mixed[g][at_rows(part, half), :]))
    put(i, outs, conv + [out])


def conv_weights_call(order, place, taps, grads, ga, mixed, wait):
    rate, groups, slots, width = taps.shape
    cols = grads[0].shape[1]
    size = width // 8
    half = ga[0][0].shape[0]
    lane = lambda n: pl.BlockSpec(
        (rate, groups, slots, size), lambda i, s: (0, 0, 0, block_of(n, 1 - i, order, s))
    )
    whole = near(*grads, *[x for pair in ga for x in pair], *mixed)
    return pl.pallas_call(
        functools.partial(conv_weights_kernel, groups, half, order),
        name="convweights",
        grid_spec=pltpu.PrefetchScalarGridSpec(
            num_scalar_prefetch=1,
            grid=(2,),
            in_specs=[lane(n) for n in range(4)] + [VMEM] * len(whole) + [ANY],
            out_specs=[VMEM] * 2,
        ),
        out_shape=payload(size, (rate + 1) * cols, 1),
        compiler_params=params(1, 24),
        cost_estimate=cost(2 * rate * groups * slots * width * cols, 8 * rate * width * cols),
    )(place, *([taps] * 4), *whole, wait)


def split_kernel(bit, place_ref, keep_ref, *refs):
    got, (send_ref, next_ref) = refs[:-3], refs[-2:]
    mine = place_ref[1 + bit]
    rows = send_ref.shape[0]
    for ref, part in ((send_ref, 1 - mine), (next_ref, mine)):
        at = at_rows(part, rows)
        if len(got) == 1:
            ref[...] = (keep_ref[at, :].astype(F32) + got[0][at, :].astype(F32)).astype(BF16)
        else:
            for n in range(2):

                @pl.when(part == n)
                def _(n=n, ref=ref):
                    half = slice(n * rows, (n + 1) * rows)
                    ref[...] = (keep_ref[half, :].astype(F32) + got[n][...].astype(F32)).astype(BF16)


def split_call(bit, place, keep, got, wait):
    rows, cols = keep.shape
    return pl.pallas_call(
        functools.partial(split_kernel, bit),
        name="split",
        grid_spec=pltpu.PrefetchScalarGridSpec(
            num_scalar_prefetch=1, grid=(1,), in_specs=[VMEM] * (1 + len(got)) + [ANY], out_specs=[VMEM] * 2
        ),
        out_shape=[held(rows // 2, cols)] * 2,
        compiler_params=params(1, 8),
        cost_estimate=cost(rows * cols, 6 * rows * cols),
    )(place, *near(keep, *got), wait)


def pause_kernel(*refs):
    refs[-1][...] = jnp.zeros(refs[-1].shape, F32)


def pause_call(arrays):
    return pl.pallas_call(
        pause_kernel,
        name="pause",
        in_specs=[ANY] * len(arrays),
        out_specs=VMEM,
        out_shape=pltpu.VMEM((8, 128), F32),
        compiler_params=params(0, 1),
        cost_estimate=pl.CostEstimate(flops=10**10, bytes_accessed=10**8, transcendentals=0),
    )(*arrays)


def finish_kernel(parts, keep_ref, got_ref, wait_ref, *refs):
    at = 0
    for (width, flipped), ref in zip(parts, refs):
        value = keep_ref[:, at:at + width].astype(F32) + got_ref[:, at:at + width].astype(F32)
        if len(ref.shape) == 3:
            cols = ref.shape[2]
            for n in range(ref.shape[0]):
                ref[n] = value[:, n * cols:(n + 1) * cols]
        elif ref.shape[0] == 2:
            ref[...] = jnp.concatenate([value.T[:1, :], value.T[64:65, :]], axis=0)
        else:
            ref[...] = value.T if flipped else value
        at += width


def finish_call(parts, keep, got, wait):
    return pl.pallas_call(
        functools.partial(finish_kernel, [(width, flipped) for width, _, flipped in parts]),
        name="finish",
        in_specs=[VMEM, VMEM, ANY],
        out_specs=[VMEM] * len(parts),
        out_shape=[jax.ShapeDtypeStruct(shape, F32) for _, shape, _ in parts],
        compiler_params=params(0, 8),
        cost_estimate=cost(keep.size, 8 * keep.size),
    )(*near(keep, got), wait)


def assemble_kernel(count, place_ref, *refs):
    own, oth = refs[:count], refs[count:2 * count]
    p_ref, c_ref = refs[-2:]
    half_p = p_ref.shape[1]
    mine = pl.program_id(1) == (place_ref[0] & 1)
    for n in range(count):
        for ref, hit in ((own[n], mine), (oth[n], jnp.logical_not(mine))):

            @pl.when(jnp.logical_and(pl.program_id(0) == n, hit))
            def _(ref=ref):
                p_ref[0] = ref[:half_p]
                c_ref[0] = ref[half_p:]


def assemble_call(place, own, oth, half_p, wait):
    half, width = own[0].shape
    groups = len(own)
    sds = jax.ShapeDtypeStruct
    block = lambda n: pl.BlockSpec((1, n, width), lambda i, j, s: (i, j, 0))
    return pl.pallas_call(
        functools.partial(assemble_kernel, groups),
        name="assemble",
        grid_spec=pltpu.PrefetchScalarGridSpec(
            num_scalar_prefetch=1,
            grid=(groups, 2),
            in_specs=[VMEM] * (2 * groups) + [ANY],
            out_specs=[block(half_p), block(half - half_p)],
        ),
        out_shape=[
            sds((groups, 2 * half_p, width), BF16),
            sds((groups, 2 * (half - half_p), width), BF16),
        ],
        compiler_params=params(2),
        cost_estimate=cost(0, 8 * groups * half * width),
    )(place, *near(*own, *oth), wait)


def swap(x, flip, name, axis="tensor"):
    with jax.named_scope("x_" + name):
        return lax.ppermute(x, axis, [(i, i ^ flip) for i in range(lax.axis_size(axis))])


def tie(*arrays):
    return lax.optimization_barrier(arrays)


class Pieces:
    def __init__(self, name, keep, got, quarters=(2, 2)):
        at = [keep.shape[0] // 4 * sum(quarters[:n]) for n in range(len(quarters) + 1)]
        self.name = name
        self.own = [add_low(keep[a:b], got[a:b]) for a, b in zip(at, at[1:])]
        self.far = []

    def start(self, count=1):
        for _ in range(count):
            n = len(self.far)
            self.far.append(swap(self.own[n], 2, f"{self.name}{'abcd'[n]}"))
        return self

    def hold(self, n, *others):
        *others, self.far[n] = tie(*others, self.far[n])
        return others

    def total(self, base=None):
        far = jnp.concatenate(self.far, axis=0).astype(F32)
        value = jnp.concatenate(self.own, axis=0).astype(F32) + far
        return (value if base is None else value + base.astype(F32)).astype(BF16)


def add_low(a, b):
    return (a.astype(F32) + b.astype(F32)).astype(BF16)


class Spread:
    def __init__(self, name, payload, order, low_bits, place):
        self.name = name
        self.bits = [b + low_bits for b in order] + list(range(low_bits - 1, -1, -1))
        self.low_bits = low_bits
        self.place = place
        size, cols = payload[-1].shape[1:]
        *self.send, self.keep = (x.reshape(-1, cols) for x in payload)
        self.got = []
        self.step = 0

    def start(self, parts=(0, 1)):
        bit = self.bits[self.step]
        for n in parts[:len(self.send)]:
            name = f"{self.name}{self.step}" + ("ab"[n] if len(self.send) > 1 else "")
            self.got.append(swap(self.send[n], 1 << bit, name, "dp"))
        if len(self.got) == len(self.send):
            self.step += 1
        return self

    def hold(self, *others):
        *rest, = tie(*others, *self.got)
        self.got = rest[len(others):]
        return rest[:len(others)]

    def split(self, wait=None):
        bit = self.bits[self.step]
        index = bit - self.low_bits if bit >= self.low_bits else 3 + bit
        send, self.keep = split_call(index, self.place, self.keep, self.got, self.keep if wait is None else wait)
        self.send, self.got = [send], []
        return self

    def next(self):
        return self if self.step == len(self.bits) else self.split().start()

    def end(self, parts, wait=None):
        if not self.got:
            self.start()
        while self.step < len(self.bits):
            self.next()
        return finish_call(parts, self.keep, self.got[0], self.keep if wait is None else wait)


def meet(spreads, *others):
    arrays = tie(*others, *[x for s in spreads for x in s.got])
    at = len(others)
    for s in spreads:
        s.got = list(arrays[at:at + len(s.got)])
        at += len(s.got)
    return list(arrays[:len(others)])


def per_device(prompt, cont, memory, old_memory, branch_at, gain_attn, w_query, w_key, w_value, w_out,
               gain_ffn, w_up, w_down, w_conv, cot_prompt, cot_cont):
    groups, prompt_len, width = prompt.shape
    half_p, half_c = prompt_len // 2, cont.shape[1] // 2
    units, cols = w_up.shape[1], w_query.shape[1]
    me = lax.axis_index("tensor")
    dp = lax.axis_index("dp")
    low_bits = lax.axis_size("dp").bit_length() - 4
    place = [me] + [(dp >> (low_bits + n)) & 1 for n in range(3)] + [(dp >> n) & 1 for n in range(low_bits)]
    place = jnp.stack(place).astype(jnp.int32)
    gain_a = gain_attn.reshape(1, width)
    gain_f = gain_ffn.reshape(1, width)
    column_a = jnp.broadcast_to(gain_attn[:, None], (width, 128))
    column_f = jnp.broadcast_to(gain_ffn[:, None], (width, 128))
    x_first, z_first = (0, 1, 2), (1, 0, 2)

    sq_own = conv_call(place, old_memory, w_conv)
    sq_far = swap(sq_own, 2, "sqfar")
    sq_near = swap(sq_own, 1, "sqnear")
    n_mem, k_mem, v_mem, n_tok, q_tok, k_tok, v_tok = qkv_call(
        memory, prompt, cont, gain_a, w_query, w_key, w_value, sq_own
    )
    k_mem, sq_far, w_out = tie(k_mem, sq_far, w_out)
    sq_diag = swap(sq_far, 1, "sqdiag")
    w_far = swap(w_out, 2, "wfar")
    w_near = swap(w_out, 1, "wnear")

    lead, mixed, lse, far = [], [], [], []
    wait = k_mem
    for g in range(groups):
        squeezed, n_sq, k_sq, v_sq, m, l = attn_call(
            g, place, branch_at, (sq_own, sq_far, sq_near, sq_diag), gain_a, w_key, w_value, q_tok,
            (k_mem, k_tok), (v_mem, v_tok), half_p, half_c, wait,
        )
        if g == 0:
            m, w_far = tie(m, w_far)
            w_diag = swap(w_far, 1, "wdiag")
        else:
            m, far[-1] = tie(m, far[-1])
        far.append(swap(m, 2, f"mfar{g}"))
        lead.append((squeezed, n_sq, k_sq, v_sq))
        mixed.append(m)
        lse.append(l)
        wait = m
    w_all = (w_out, w_far, w_near, w_diag)

    def run_ffn(g, wait):
        blocks = (mixed[g], far[g], swap(mixed[g], 1, f"mnear{g}"), swap(far[g], 1, f"mdiag{g}"))
        return list(ffn_call(
            g, place, prompt, cont, cot_prompt, cot_cont, blocks, w_all, gain_f, w_up, w_down, wait
        ))

    def combine(g, chip, other):
        low = add_low(chip, other)
        return low, swap(low, 1, f"ga{g}")

    def run_back(g, grad, wait):
        squeezed, _, k_sq, v_sq = lead[g]
        return list(attn_back_call(
            g, place, branch_at, q_tok, (k_sq, k_mem, k_tok), (v_sq, v_mem, v_tok), lse[g], grad[0], grad[1],
            w_out, w_query, w_key, w_value, prompt, cont, squeezed, gain_a, wait,
        ))

    last = groups - 1
    ffn, chips, others, grads, back = [], [], [], [], []
    for g in range(groups):
        ffn.append(run_ffn(g, wait))
        if g == 0:
            for n in range(1, groups):
                ffn[0][3], far[n] = tie(ffn[0][3], far[n])
        else:
            ffn[g][3], others[g - 1] = tie(ffn[g][3], others[g - 1])
        got = swap(ffn[g][3], 1, f"gsend{g}")
        if g == 0:
            taps = taps_call(old_memory, ffn[0][3])
            taps, got = tie(taps, got)
        else:
            grads.append(combine(g - 1, chips[g - 1], others[g - 1]))
        wait = add_low(ffn[g][4], got)
        chips.append(wait)
        others.append(swap(wait, 2, f"gfar{g}"))
    up = up_weights_call(x_first, place, [f[0] for f in ffn], [f[2] for f in ffn], w_up, column_f, wait)
    out = [
        Pieces(f"out{g}", ffn[g][6], swap(ffn[g][5], 1, f"outsend{g}"), (2, 2) if g == 0 else (4,))
        for g in range(groups)
    ]
    down = down_weights_call(z_first, place, [f[1] for f in ffn], cot_prompt, cot_cont, up[2])
    *up, gain_up = up
    up = Spread("up", up, x_first, low_bits, place).start((0,))
    wait = down[2]
    down = Spread("down", down, z_first, low_bits, place).start((0,))
    out[0].own[0], wait = tie(out[0].own[0], wait)
    out[0].start()
    tok = []
    for g in range(groups):
        if g == last:
            grads.append(combine(last, chips[last], others[last]))
        back.append(run_back(g, grads[g], wait))
        if g == 0:
            back[g] = down.hold(*up.hold(*out[0].hold(0, *back[g])))
            up.start((1,))
            down.start((1,))
        if g == last - 1:
            *back[g], others[last] = tie(*back[g], others[last])
        if g > 0:
            back[g] = tok[-1].hold(0, *back[g])
        if g == last:
            back[g] = down.hold(*up.hold(*back[g]))
            up.next()
            down.next()
        got = swap(back[g][3], 1, f"toksend{g}")
        tok.append(Pieces(f"tok{g}", back[g][4], got, (3, 1) if g < last else (4,)))
        wait = tok[g].own[0]
        if g < last:
            tok[g].start()

    got = [swap(back[g][5], 1, f"sqsend{g}") for g in range(groups)]
    sq_own_grad = [add_low(back[g][6], got[g][0]) for g in range(groups)]
    sq_back = swap(jnp.concatenate([add_low(back[g][7], got[g][1]) for g in range(groups)], axis=0), 2, "sqback")
    n_sq = [x[1] for x in lead]
    dqkv = [x[:3] for x in back]
    up.send[0], down.send[0], wait = tie(up.send[0], down.send[0], wait)
    for g in range(1, groups):
        *out[g].own, wait = tie(*out[g].own, wait)
    qkv = attn_weights_call(
        z_first, place, n_sq, n_mem, n_tok, dqkv, (w_query, w_key, w_value), column_a, gain_up, wait
    )
    *qkv, sq_back = tie(*qkv, sq_back)
    slots = sq_back.shape[0] // groups
    sq_back = [sq_back[g * slots:(g + 1) * slots] for g in range(groups)]
    wait = qkv[-1]
    qkv = Spread("qkv", qkv, z_first, low_bits, place).start()
    conv = conv_weights_call(
        x_first, place, taps, [add_low(a, b) for a, b in zip(sq_own_grad, sq_back)], grads, mixed, wait
    )
    conv = down.hold(*up.hold(*conv))
    conv = Spread("conv", conv, x_first, low_bits, place).start()
    for spread in (up, down):
        if spread.step < len(spread.bits):
            spread.split()
    pairs = {}
    for g in range(groups):
        tok[g].base, out[g].base = grads[g][0], None

    def round(starting, waiting, pieces, ready=(), fillers=(), far=()):
        sends = [s for s in starting if s.step < len(s.bits) and not s.got]
        rest = [p.own[len(p.far)] for p in pieces]
        owns = [p.total(p.base) for p in ready]
        message = [jnp.concatenate(rest, axis=0)] if rest else []
        arrays = tie(*[x for s in sends for x in s.send], *message, *owns)
        wait = pause_call(arrays)
        hold = [wait]
        at = 0
        for s in sends:
            s.send = [arrays[at]]
            at += 1
            s.start()
        if message:
            hold.append(swap(arrays[at], 2, "rows"))
            at += 1
        for p, x in zip(ready, arrays[at:]):
            pairs[p.name] = (x, swap(x, 1, p.name + "own"))
        results = []
        for make in fillers:
            results.append(list(make(wait)))
            wait = results[-1][0]
        flat = [x for r in results for x in r]
        others = meet(list(waiting) + list(starting), *hold, *flat, *[p.far[-1] for p in far])
        at = 0
        for p, x in zip(far, others[len(hold) + len(flat):]):
            p.far[-1] = x
        for p, x in zip(pieces, rest):
            p.far.append(others[1][at:at + x.shape[0]])
            at += x.shape[0]
        flat = iter(others[len(hold):])
        return others[0], [[next(flat) for _ in r] for r in results]

    def place_rows(name):
        def make(wait):
            own, oth = zip(*[pairs[f"{name}{g}"] for g in range(groups)])
            return assemble_call(place, own, oth, half_p, wait)

        return make

    rows = width // lax.axis_size("dp")
    pause, _ = round((up,), (conv, qkv), (*tok, out[0]))
    for spread in (conv, qkv):
        spread.split(pause)
    fillers = [lambda wait: up.end([(units, (rows, units), False)], wait), place_rows("tok")]
    pause, ((grad_up,), grad_tok) = round((down, conv, qkv), (), out[1:], tok, fillers)
    for spread in (conv, qkv):
        spread.split(pause)
    fillers = [lambda wait: down.end([(units, (units, rows), True)], wait), place_rows("out")]
    pause, ((grad_down,), out) = round((conv, qkv), (), (), out, fillers)
    whole = (cols, (rows, cols), False)
    grad_q, grad_k, grad_v, gains = qkv.end([whole, whole, whole, (128, (2, rows), True)])
    grad_conv, grad_o = conv.end([(RATE * cols, (RATE, rows, cols), False), (cols, (cols, rows), True)])
    gains = gains + swap(gains, 1, "gain1")
    gains = gains + swap(gains, 2, "gain2")
    return (
        out[0],
        out[1],
        grad_tok[0],
        grad_tok[1],
        grad_q,
        grad_k,
        grad_v,
        grad_o,
        grad_up,
        grad_down,
        grad_conv,
        gains[0],
        gains[1],
    )


def solution(mesh):
    tokens = P("dp", None, None)
    split = P(None, "tensor")
    in_specs = (
        tokens, tokens, tokens, tokens, P("dp", None), P(), split, split, split, P("tensor", None), P(),
        split, P("tensor", None), P(None, None, "tensor"), tokens, tokens,
    )
    both = P("dp", "tensor")
    out_specs = (
        tokens, tokens, tokens, tokens, both, both, both, P("tensor", "dp"), both, P("tensor", "dp"),
        P(None, "dp", "tensor"), P("dp"), P("dp"),
    )
    return jax.shard_map(per_device, mesh=mesh, in_specs=in_specs, out_specs=out_specs, check_vma=False)
```
